32 devices in a mesh: wide: 8 (over z, x), narrow: 4 (over y, core).
Axes of the slice: x: 2, y: 2, z: 4, core: 2. Of those that a mesh axis runs over, the one named last changes fastest.
Arguments:
- tokens: bfloat16 [224, 72, 768], P(('wide', 'narrow')), may hold values from -6 to 6
- visible: int32 [224], P(('wide', 'narrow')), may hold values from 48 to 72
- first_gain: bfloat16 [768], replicated, may hold values from 0.5 to 1.5
- first_shift: bfloat16 [768], replicated, may hold values from -4 to 4
- joint_weight: bfloat16 [768, 2304], replicated, may hold values from -0.21875 to 0.21875
- query_bias: bfloat16 [768], replicated, may hold values from -4 to 4
- value_bias: bfloat16 [768], replicated, may hold values from -4 to 4
- mixer_weight: bfloat16 [768, 768], replicated, may hold values from -2 to 2
- mixer_bias: bfloat16 [768], replicated, may hold values from -4 to 4
- second_gain: bfloat16 [768], replicated, may hold values from 0.5 to 1.5
- second_shift: bfloat16 [768], replicated, may hold values from -4 to 4
- expand_weight: bfloat16 [768, 3072], replicated, may hold values from -0.21875 to 0.21875
- expand_bias: bfloat16 [3072], replicated, may hold values from -4 to 4
- shrink_weight: bfloat16 [3072, 768], replicated, may hold values from -0.15625 to 0.15625
- shrink_bias: bfloat16 [768], replicated, may hold values from -4 to 4
- cotangent: bfloat16 [224, 72, 768], P(('wide', 'narrow')), may hold values from -6 to 6
Outputs:
- layer_out: bfloat16 [224, 72, 768], P(('wide', 'narrow'))
- input_grad: bfloat16 [224, 72, 768], P(('wide', 'narrow'))
- delta_firstgain: float32 [768], P('narrow')
- delta_firstshift: float32 [768], P('narrow')
- delta_joint: float32 [768, 2304], P('narrow')
- delta_query: float32 [768], P('narrow')
- delta_value: float32 [768], P('narrow')
- delta_mixer: float32 [768, 768], P('narrow')
- delta_mixerbias: float32 [768], P('narrow')
- delta_secondgain: float32 [768], P('narrow')
- delta_secondshift: float32 [768], P('narrow')
- delta_expand: float32 [768, 3072], P('narrow')
- delta_expandbias: float32 [3072], P('narrow')
- delta_shrink: float32 [3072, 768], P('narrow')
- delta_shrinkbias: float32 [768], P('narrow')
The draws below stay inside these ranges and needn't reach their ends.
Inputs may be any that keep to these rules, and one draw needn't show every extreme that they name: Each item's visible patches fill its first slots; later slots are padding.
All inputs are finite; a program needn't handle non-finite values.
Results may differ from the reference program's by a relative error of at most 0.013.
Values sent between devices are 32-bit elements; how exact they have to be, the bound alone decides.
A program may use at most 192 MiB of HBM per device.

```python
import jax
import jax.numpy as jnp
from jax import lax

D = 768
HEAD_DIM = 64
FF = 3072
SLOTS = 72
ITEMS_DEV = 7
ITEMS = 224


def place_ends(values, rng, least, top_value):
    spot = [jax.random.randint(jax.random.fold_in(rng, axis), (), 0, length) for axis, length in enumerate(values.shape)]
    widest = values.shape.index(max(values.shape))
    next_to = spot[:widest] + [(spot[widest] + 1) % values.shape[widest]] + spot[widest + 1:]
    return values.at[tuple(spot)].set(least).at[tuple(next_to)].set(top_value)


def strengthened(entries, key, source, target, blocks, factor):
    owner, partner = [(jnp.arange(entries.shape[position]) // (entries.shape[position] // blocks)).reshape([-1 if axis == position else 1 for axis in range(entries.ndim)]) for position in (source, target)]
    chosen = jax.random.permutation(key, blocks)[partner]
    strong = (owner == chosen) | (owner == (partner + blocks // 2) % blocks)
    return jnp.where(strong, factor * entries, entries)


def level_of(rng, dims, split, low, largest):
    def one(axis_at, shards_of):
        steps = jax.random.uniform(jax.random.fold_in(jax.random.fold_in(rng, 6), axis_at), (shards_of,), jnp.float32, low / len(split), largest / len(split))
        return jnp.repeat(jnp.exp(steps), dims[axis_at] // shards_of).reshape((-1,) + (1,) * (len(dims) - axis_at - 1))

    loudness = one(*split[0])
    for cut in split[1:]:
        loudness = loudness * one(*cut)
    return loudness


def noise(stream_key, shape, scale, reach, pieces=(), kind=jnp.bfloat16):
    entries = jax.random.normal(stream_key, shape, jnp.float32) * scale
    if len(pieces) > 0:
        entries = level_of(stream_key, shape, pieces, -0.22, 0.18) * entries
    return jnp.clip(entries, min=-reach, max=reach).astype(kind)


def gaussian_with(key, extent, width, reach, split, heavy, kind=jnp.bfloat16):
    values = width * jax.random.normal(key, extent, jnp.float32)
    if split:
        values = values * level_of(key, extent, split, -0.22, 0.18)
    return jnp.clip(strengthened(values, jax.random.fold_in(key, 3), *heavy), -reach, reach).astype(kind)


def setup_inputs(seed: int = 0) -> dict:
    key_of = jax.random.split(jax.random.key(seed), 17)
    return {
        "tokens": noise(key_of[0], (ITEMS, SLOTS, D), 1.0, 6.0, ((0, 32),)),
        "visible": place_ends(jax.random.randint(key_of[1], (ITEMS,), SLOTS * 2 // 3, SLOTS + 1), jax.random.fold_in(key_of[1], 1), SLOTS * 2 // 3, SLOTS).astype(jnp.int32),
        "first_gain": jnp.clip(1.0 + 0.1 * jax.random.normal(key_of[2], (D,), jnp.float32), 0.5, 1.5).astype(jnp.bfloat16),
        "first_shift": noise(key_of[3], (D,), 0.3, 4.0),
        "joint_weight": noise(key_of[4], (D, 3 * D), D ** -0.5, 0.21875),
        "query_bias": noise(key_of[5], (D,), 0.3, 4.0),
        "value_bias": noise(key_of[6], (D,), 0.3, 4.0),
        "mixer_weight": noise(key_of[7], (D, D), (D * 8 // (SLOTS * 9)) ** -0.5, 2.0),
        "mixer_bias": noise(key_of[8], (D,), 0.3, 4.0),
        "second_gain": jnp.clip(1.0 + 0.1 * jax.random.normal(key_of[9], (D,), jnp.float32), 0.5, 1.5).astype(jnp.bfloat16),
        "second_shift": noise(key_of[10], (D,), 0.3, 4.0),
        "expand_weight": noise(key_of[11], (D, FF), D ** -0.5, 0.21875),
        "expand_bias": noise(key_of[12], (FF,), 0.3, 4.0),
        "shrink_weight": noise(key_of[13], (FF, D), (FF // 2) ** -0.5, 0.15625),
        "shrink_bias": noise(key_of[14], (D,), 0.3, 4.0),
        "cotangent": gaussian_with(key_of[15], (ITEMS, SLOTS, D), 1.0, 6.0, ((0, 32),), (0, 2, 32, 2.75)),
    }


EPSILON = 1e-06
HIGH = lax.Precision.HIGHEST

@jax.custom_vjp
def low(v):
    return lax.optimization_barrier(v.astype(jnp.bfloat16)).astype(jnp.float32)

@jax.custom_vjp
def low_back(v):
    return v

def low_keep(v):
    return (low(v), None)

def low_pass(kept, grad):
    return (grad,)

def back_keep(v):
    return (v, None)

def back_low(kept, grad):
    return (low(grad),)
low.defvjp(low_keep, low_pass)
low_back.defvjp(back_keep, back_low)

def layer_norm(values, gain_vec, shift_vec):
    center = values - lax.optimization_barrier(jnp.mean(values, axis=-1, keepdims=True))
    spread = lax.optimization_barrier(jnp.mean(center * center, axis=-1, keepdims=True))
    return center * lax.rsqrt(spread + EPSILON) * gain_vec + shift_vec

def encode_group(tokens, live_slots, params):
    first_gain, first_shift, joint_weight, query_bias, value_bias, mixer_weight, mixer_bias, second_gain, second_shift, expand_weight, expand_bias, shrink_weight, shrink_bias = params
    item_count, slot_count, model_width = tokens.shape
    head_count = model_width // HEAD_DIM
    head_shape = (item_count, slot_count, head_count, HEAD_DIM)
    first_low = low(layer_norm(tokens, first_gain, first_shift))
    joint_out = jnp.einsum('isd,de->ise', first_low, joint_weight, precision=HIGH)
    query_low = low(low_back(joint_out[..., :model_width] + query_bias)).reshape(head_shape)
    key_part = low(low_back(joint_out[..., model_width:2 * model_width])).reshape(head_shape)
    value_part = low(low_back(joint_out[..., 2 * model_width:] + value_bias)).reshape(head_shape)
    logits = low_back(jnp.einsum('iqhe,ikhe->ihqk', query_low, key_part, precision=HIGH) * HEAD_DIM ** (-0.5))
    logits = jnp.where(live_slots[:, None, None, :] > 0.5, logits, -1000000000.0)
    row_max = lax.optimization_barrier(jnp.max(logits, axis=-1, keepdims=True))
    expo = jnp.exp(logits - row_max)
    attend = low(expo / lax.optimization_barrier(jnp.sum(expo, axis=-1, keepdims=True)))
    mixed_low = jnp.einsum('ihqk,ikhe->iqhe', attend, value_part, precision=HIGH)
    mixed_low = low(low_back(mixed_low.reshape(item_count, slot_count, model_width)))
    branch = low_back(jnp.einsum('isd,de->ise', mixed_low, mixer_weight, precision=HIGH) + mixer_bias)
    middle = tokens + branch
    second_low = low(layer_norm(middle, second_gain, second_shift))
    hidden = low_back(jnp.einsum('isd,df->isf', second_low, expand_weight, precision=HIGH) + expand_bias)
    active_low = low(jax.nn.gelu(hidden, approximate=False))
    output = low_back(jnp.einsum('isf,fd->isd', active_low, shrink_weight, precision=HIGH) + shrink_bias)
    return (middle + output) * live_slots[..., None]

def reference(tokens, visible, first_gain, first_shift, joint_weight, query_bias, value_bias, mixer_weight, mixer_bias, second_gain, second_shift, expand_weight, expand_bias, shrink_weight, shrink_bias, cotangent):
    params = (first_gain.astype(jnp.float32), first_shift.astype(jnp.float32), joint_weight.astype(jnp.float32), query_bias.astype(jnp.float32), value_bias.astype(jnp.float32), mixer_weight.astype(jnp.float32), mixer_bias.astype(jnp.float32), second_gain.astype(jnp.float32), second_shift.astype(jnp.float32), expand_weight.astype(jnp.float32), expand_bias.astype(jnp.float32), shrink_weight.astype(jnp.float32), shrink_bias.astype(jnp.float32))
    total_items = tokens.shape[0]
    live_slots = (jnp.arange(SLOTS, dtype=jnp.int32)[None, :] < visible[:, None]).astype(jnp.float32)
    group_size = 4 * ITEMS_DEV
    blocks = total_items // group_size
    inputs = tokens.astype(jnp.float32).reshape(blocks, group_size, SLOTS, D)
    live_blocks = live_slots.reshape(blocks, group_size, SLOTS)

    def whole(inputs, params):

        def group_step(bundle):
            return encode_group(bundle[0], bundle[1], params)
        return lax.map(jax.checkpoint(group_step), (inputs, live_blocks))
    result, pullback = jax.vjp(whole, inputs, params)
    input_cot, param_cots = pullback(cotangent.astype(jnp.float32).reshape(blocks, group_size, SLOTS, D))
    layer_out = result.reshape(total_items, SLOTS, D).astype(jnp.bfloat16)
    input_grad = input_cot.reshape(total_items, SLOTS, D).astype(jnp.bfloat16)
    return (layer_out, input_grad, param_cots[0], param_cots[1], param_cots[2], param_cots[3], param_cots[4], param_cots[5], param_cots[6], param_cots[7], param_cots[8], param_cots[9], param_cots[10], param_cots[11], param_cots[12])
```

```python
import functools

import jax
import jax.numpy as jnp
from jax import lax
from jax.experimental import pallas as pl
from jax.experimental.pallas import tpu as pltpu
from jax.sharding import PartitionSpec as P

HEAD_DIM = 64
SUB = 8
DEPTH = 6
MESH = pl.DeviceIdType.MESH


EPSILON = 1e-06


def normalize(features, gain_vec, shift_vec):
    center = features - jnp.mean(features, axis=-1, keepdims=True)
    spread = jnp.mean(center * center, axis=-1, keepdims=True)
    return center * lax.rsqrt(spread + EPSILON) * gain_vec + shift_vec


def gelu_exact(pre_act):
    return jax.nn.gelu(pre_act, approximate=False)


def contract_cols(left_mat, right_mat):
    return lax.dot_general(
        left_mat, right_mat, (((1,), (1,)), ((), ())), preferred_element_type=jnp.float32
    )


def attention_logits(query_low, key_part, key_live, score_scale):
    logits = (
        jnp.einsum("iqhe,ikhe->ihqk", query_low, key_part, preferred_element_type=jnp.float32)
        * score_scale
    )
    return jnp.where(key_live, logits, -1000000000.0)


def flip(index, place):
    return index + (1 - 2 * lax.rem(lax.div(index, 2**place), 2)) * 2**place


def bit_of(index, place):
    return lax.rem(lax.div(index, 2**place), 2)


def reversed_bits(value, count):
    out = 0
    for place in range(count):
        out = out * 2 + (value >> place) % 2
    return out


class Plan:
    def __init__(self, narrow, wide, width, ff):
        self.narrow, self.wide, self.width, self.ff = narrow, wide, width, ff
        self.narrow_bits = narrow.bit_length() - 1
        self.wide_bits = wide.bit_length() - 1
        rows = width // narrow
        chunk = SUB
        while rows % (2 * chunk) == 0 and chunk < SUB * wide:
            chunk *= 2
        self.chunk = chunk
        split_bits = (chunk // SUB).bit_length() - 1
        self.sums = []
        length = narrow * chunk
        for place in range(self.narrow_bits):
            length //= 2
            self.sums.append(("narrow", place, length, True))
        for place in range(self.wide_bits):
            halve = place < split_bits
            length = length // 2 if halve else length
            self.sums.append(("wide", place, length, halve))
        self.gathers = []
        for place in reversed(range(split_bits)):
            self.gathers.append(("wide", place, length))
            length *= 2
        self.split_bits = split_bits
        self.depth = len(self.sums) + len(self.gathers)
        self.phases = []
        start = 0
        for rows_block, windows in (
            (ff // narrow, 1),
            (rows, ff // width),
            (rows, 1),
            (rows, 3),
        ):
            count = rows_block // chunk * windows
            self.phases.append((start, count, rows_block, windows))
            start += count
        self.small_at = start
        self.chunks = start + 1


def gradient_kernel(plan, *refs):
    lefts = (refs[0], refs[2], refs[4], refs[6])
    rights = (refs[1], refs[3], refs[5], refs[7])
    small = refs[8]
    outs = refs[9:13]
    small_out = refs[13]
    scratch = refs[14:]
    part = scratch[0]
    landed = scratch[1 : 1 + len(plan.sums)]
    whole = scratch[1 + len(plan.sums)]
    send_sems, recv_sems = scratch[2 + len(plan.sums) :]
    width, chunk, narrow = plan.width, plan.chunk, plan.narrow
    spots = {"narrow": lax.axis_index("narrow"), "wide": lax.axis_index("wide")}

    def partner(axis, place):
        return {
            "wide": flip(spots["wide"], place) if axis == "wide" else spots["wide"],
            "narrow": flip(spots["narrow"], place) if axis == "narrow" else spots["narrow"],
        }

    barrier = pltpu.get_barrier_semaphore()
    for axis, place, _, _ in plan.sums:
        pl.semaphore_signal(barrier, inc=1, device_id=partner(axis, place), device_id_type=MESH)
    pl.semaphore_wait(barrier, len(plan.sums))

    def source(stage, item):
        if stage == 0:
            return part.at[lax.rem(item, 2)]
        return landed[stage - 1].at[lax.rem(item, DEPTH)]

    def piece_start(bits):
        start = 0
        for place in range(bits):
            start = start + bit_of(spots["wide"], place) * (chunk // 2 ** (place + 1))
        return start

    def exchange(stage, item):
        slot = lax.rem(item, DEPTH)
        if stage < len(plan.sums):
            axis, place, length, halve = plan.sums[stage]
            there = (1 - bit_of(spots[axis], place)) * length if halve else 0
            src = source(stage, item).at[pl.ds(pl.multiple_of(there, SUB), length)]
            dst = landed[stage].at[slot]
        else:
            axis, place, length = plan.gathers[stage - len(plan.sums)]
            window = pl.ds(pl.multiple_of(piece_start(place + 1), SUB), length)
            src = whole.at[item, window]
            dst = src
        return pltpu.make_async_remote_copy(
            src_ref=src,
            dst_ref=dst,
            send_sem=send_sems.at[stage, slot],
            recv_sem=recv_sems.at[stage, slot],
            device_id=partner(axis, place),
            device_id_type=MESH,
        )

    def produce(item):
        slot = lax.rem(item, 2)
        for (start, count, rows_block, windows), left, right in zip(plan.phases, lefts, rights):

            @pl.when((item >= start) & (item < start + count))
            def _():
                local = item - start
                row = lax.div(local, windows) * chunk
                col = lax.rem(local, windows) * width
                rows = [
                    left[
                        pl.ds(
                            pl.multiple_of(
                                reversed_bits(spot, plan.narrow_bits) * rows_block + row, chunk
                            ),
                            chunk,
                        ),
                        :,
                    ]
                    for spot in range(narrow)
                ]
                part[slot] = jnp.dot(
                    jnp.concatenate(rows, axis=0),
                    right[:, pl.ds(pl.multiple_of(col, width), width)],
                    preferred_element_type=jnp.float32,
                )

        @pl.when(item == plan.small_at)
        def _():
            part[slot] = small[...]

    def absorb(stage, item):
        axis, place, length, halve = plan.sums[stage]
        here = bit_of(spots[axis], place) * length if halve else 0
        slot = lax.rem(item, DEPTH)
        landed[stage][slot] += source(stage, item)[pl.ds(pl.multiple_of(here, SUB), length)]

    def finish(item):
        for (start, count, _, windows), out in zip(plan.phases, outs):

            @pl.when((item >= start) & (item < start + count))
            def _():
                local = item - start
                row = lax.div(local, windows) * chunk
                col = lax.rem(local, windows) * width
                out[
                    pl.ds(pl.multiple_of(row, chunk), chunk),
                    pl.ds(pl.multiple_of(col, width), width),
                ] = whole[item]

        @pl.when(item == plan.small_at)
        def _():
            small_out[...] = whole[item]

    def step(tick, carry):
        @pl.when(tick < plan.chunks)
        def _():
            produce(tick)
            exchange(0, tick).start()

        for stage in range(plan.depth):
            item = tick - 1 - stage

            @pl.when((item >= 0) & (item < plan.chunks))
            def _():
                exchange(stage, item).wait()
                if stage < len(plan.sums):
                    absorb(stage, item)
                if stage == len(plan.sums) - 1:
                    whole[
                        item, pl.ds(pl.multiple_of(piece_start(plan.split_bits), SUB), SUB)
                    ] = landed[stage][lax.rem(item, DEPTH)]
                if stage + 1 < plan.depth:
                    exchange(stage + 1, item).start()
                else:
                    finish(item)

        return carry

    lax.fori_loop(0, plan.chunks + plan.depth, step, 0)


def reduce_gradients(pairs, vectors, ff, width):
    narrow, wide = lax.axis_size("narrow"), lax.axis_size("wide")
    plan = Plan(narrow, wide, width, ff)
    chunk = plan.chunk
    joined = jnp.concatenate([vector.reshape(narrow, -1) for vector in vectors], axis=1)
    joined = jnp.pad(joined, ((0, 0), (0, chunk * width - joined.shape[1])))
    order = [reversed_bits(spot, plan.narrow_bits) for spot in range(narrow)]
    small = jnp.stack([joined[spot] for spot in order]).reshape(narrow * chunk, width)
    operands = []
    for left, right in pairs:
        extra = -left.shape[0] % 256
        operands.append(jnp.pad(left, ((0, extra), (0, 0))).T)
        operands.append(jnp.pad(right, ((0, extra), (0, 0))))
    shapes = [
        jax.ShapeDtypeStruct((left.shape[1] // narrow, right.shape[1]), jnp.float32)
        for left, right in pairs
    ] + [jax.ShapeDtypeStruct((chunk, width), jnp.float32)]
    scratch = [pltpu.VMEM((2, narrow * chunk, width), jnp.float32)]
    scratch += [pltpu.VMEM((DEPTH, length, width), jnp.float32) for _, _, length, _ in plan.sums]
    scratch += [
        pltpu.VMEM((plan.chunks, chunk, width), jnp.float32),
        pltpu.SemaphoreType.DMA((plan.depth, DEPTH)),
        pltpu.SemaphoreType.DMA((plan.depth, DEPTH)),
    ]
    results = pl.pallas_call(
        functools.partial(gradient_kernel, plan),
        out_shape=shapes,
        in_specs=[pl.BlockSpec(memory_space=pltpu.VMEM)] * (len(operands) + 1),
        out_specs=[pl.BlockSpec(memory_space=pltpu.VMEM)] * len(shapes),
        scratch_shapes=scratch,
        compiler_params=pltpu.CompilerParams(
            collective_id=0, has_side_effects=True, vmem_limit_bytes=60 * 2**20
        ),
        name="gradients",
    )(*operands, small)
    flat = results[-1].reshape(-1)
    sums, offset = [], 0
    for vector in vectors:
        length = vector.size // narrow
        sums.append(flat[offset : offset + length])
        offset += length
    return results[:-1], sums


def shards(
    tokens,
    visible,
    first_gain,
    first_shift,
    joint_weight,
    query_bias,
    value_bias,
    mixer_weight,
    mixer_bias,
    second_gain,
    second_shift,
    expand_weight,
    expand_bias,
    shrink_weight,
    shrink_bias,
    cotangent,
):
    item_count, slot_count, model_width = tokens.shape
    head_count = model_width // HEAD_DIM
    row_count = item_count * slot_count
    head_shape = (item_count, slot_count, head_count, HEAD_DIM)
    score_scale = HEAD_DIM ** (-0.5)
    live_slots = (jnp.arange(slot_count, dtype=jnp.int32)[None, :] < visible[:, None]).astype(
        jnp.float32
    )
    live_rows = live_slots.reshape(row_count, 1)
    key_live = live_slots[:, None, None, :] > 0.5
    flat_in = tokens.reshape(row_count, model_width).astype(jnp.float32)
    first_vals, first_back = jax.vjp(
        normalize, flat_in, first_gain.astype(jnp.float32), first_shift.astype(jnp.float32)
    )
    first_low = first_vals.astype(jnp.bfloat16)
    joint_out = jnp.dot(first_low, joint_weight, preferred_element_type=jnp.float32)
    query_low = (
        (joint_out[:, :model_width] + query_bias.astype(jnp.float32))
        .astype(jnp.bfloat16)
        .reshape(head_shape)
    )
    key_part = joint_out[:, model_width : 2 * model_width].astype(jnp.bfloat16).reshape(head_shape)
    value_part = (
        (joint_out[:, 2 * model_width :] + value_bias.astype(jnp.float32))
        .astype(jnp.bfloat16)
        .reshape(head_shape)
    )
    logits = attention_logits(query_low, key_part, key_live, score_scale)
    row_max = jnp.max(logits, axis=-1, keepdims=True)
    log_total = row_max + jnp.log(jnp.sum(jnp.exp(logits - row_max), axis=-1, keepdims=True))
    attend_low = jnp.exp(logits - log_total).astype(jnp.bfloat16)
    mixed_low = jnp.einsum(
        "ihqk,ikhe->iqhe", attend_low, value_part, preferred_element_type=jnp.float32
    )
    mixed_low = mixed_low.reshape(row_count, model_width).astype(jnp.bfloat16)
    branch = jnp.dot(
        mixed_low, mixer_weight, preferred_element_type=jnp.float32
    ) + mixer_bias.astype(jnp.float32)
    middle = flat_in + branch
    second_vals, second_back = jax.vjp(
        normalize, middle, second_gain.astype(jnp.float32), second_shift.astype(jnp.float32)
    )
    second_low = second_vals.astype(jnp.bfloat16)
    hidden = jnp.dot(
        second_low, expand_weight, preferred_element_type=jnp.float32
    ) + expand_bias.astype(jnp.float32)
    active_vals, gelu_back = jax.vjp(gelu_exact, hidden)
    active_low = active_vals.astype(jnp.bfloat16)
    output = jnp.dot(
        active_low, shrink_weight, preferred_element_type=jnp.float32
    ) + shrink_bias.astype(jnp.float32)
    layer_out = (
        ((middle + output) * live_rows)
        .astype(jnp.bfloat16)
        .reshape(item_count, slot_count, model_width)
    )
    grad_out = cotangent.reshape(row_count, model_width).astype(jnp.float32) * live_rows
    grad_out_low = grad_out.astype(jnp.bfloat16)
    shrink_bias_grad = jnp.sum(grad_out, axis=0)
    grad_active = contract_cols(grad_out_low, shrink_weight)
    grad_hidden = gelu_back(grad_active)[0].astype(jnp.bfloat16)
    expand_bias_grad = jnp.sum(grad_hidden.astype(jnp.float32), axis=0)
    grad_second = contract_cols(grad_hidden, expand_weight)
    grad_norm_two, second_gain_grad, second_shift_grad = second_back(grad_second)
    grad_middle = grad_out + grad_norm_two
    grad_branch = grad_middle.astype(jnp.bfloat16)
    mixer_bias_grad = jnp.sum(grad_branch.astype(jnp.float32), axis=0)
    grad_mixed = contract_cols(grad_branch, mixer_weight).astype(jnp.bfloat16).reshape(head_shape)
    attend_again = jnp.exp(attention_logits(query_low, key_part, key_live, score_scale) - log_total)
    grad_attend = jnp.einsum(
        "iqhe,ikhe->ihqk", grad_mixed, value_part, preferred_element_type=jnp.float32
    )
    grad_value = jnp.einsum(
        "ihqk,iqhe->ikhe",
        attend_again.astype(jnp.bfloat16),
        grad_mixed,
        preferred_element_type=jnp.float32,
    )
    grad_logits = attend_again * (
        grad_attend - jnp.sum(attend_again * grad_attend, axis=-1, keepdims=True)
    )
    grad_logits = grad_logits.astype(jnp.bfloat16)
    grad_query = (
        jnp.einsum("ihqk,ikhe->iqhe", grad_logits, key_part, preferred_element_type=jnp.float32)
        * score_scale
    )
    grad_key = (
        jnp.einsum("ihqk,iqhe->ikhe", grad_logits, query_low, preferred_element_type=jnp.float32)
        * score_scale
    )
    grad_joint = jnp.concatenate(
        [
            grad_query.reshape(row_count, model_width),
            grad_key.reshape(row_count, model_width),
            grad_value.reshape(row_count, model_width),
        ],
        axis=1,
    ).astype(jnp.bfloat16)
    grad_joint_float = grad_joint.astype(jnp.float32)
    query_grad = jnp.sum(grad_joint_float[:, :model_width], axis=0)
    value_grad = jnp.sum(grad_joint_float[:, 2 * model_width :], axis=0)
    grad_first = contract_cols(grad_joint, joint_weight)
    grad_norm_one, first_gain_grad, first_shift_grad = first_back(grad_first)
    input_grad = (
        (grad_middle + grad_norm_one)
        .astype(jnp.bfloat16)
        .reshape(item_count, slot_count, model_width)
    )
    (total_shrink, total_expand, total_mixer, total_joint), vectors = reduce_gradients(
        (
            (active_low, grad_out_low),
            (second_low, grad_hidden),
            (mixed_low, grad_branch),
            (first_low, grad_joint),
        ),
        (
            first_gain_grad,
            first_shift_grad,
            query_grad,
            value_grad,
            mixer_bias_grad,
            second_gain_grad,
            second_shift_grad,
            expand_bias_grad,
            shrink_bias_grad,
        ),
        active_low.shape[1],
        model_width,
    )
    (
        total_first_gain,
        total_first_shift,
        total_query,
        total_value,
        total_mixer_bias,
        total_second_gain,
        total_second_shift,
        total_expand_bias,
        total_shrink_bias,
    ) = vectors
    return (
        layer_out,
        input_grad,
        total_first_gain,
        total_first_shift,
        total_joint,
        total_query,
        total_value,
        total_mixer,
        total_mixer_bias,
        total_second_gain,
        total_second_shift,
        total_expand,
        total_expand_bias,
        total_shrink,
        total_shrink_bias,
    )


def solution(mesh):
    return jax.shard_map(
        shards,
        mesh=mesh,
        in_specs=(
            P(("wide", "narrow"), None, None),
            P(("wide", "narrow")),
            P(),
            P(),
            P(),
            P(),
            P(),
            P(),
            P(),
            P(),
            P(),
            P(),
            P(),
            P(),
            P(),
            P(("wide", "narrow"), None, None),
        ),
        out_specs=(
            P(("wide", "narrow"), None, None),
            P(("wide", "narrow"), None, None),
            P("narrow"),
            P("narrow"),
            P("narrow", None),
            P("narrow"),
            P("narrow"),
            P("narrow", None),
            P("narrow"),
            P("narrow"),
            P("narrow"),
            P("narrow", None),
            P("narrow"),
            P("narrow", None),
            P("narrow"),
        ),
        check_vma=False,
    )
```

```python
import functools
import types

import jax
import jax.numpy as jnp
from jax import lax
from jax.experimental import pallas as pl
from jax.experimental.pallas import tpu as pltpu
from jax.sharding import PartitionSpec as P

HEAD_DIM = 64
EPSILON = 1e-06
SUB = 8
DEPTH = 6
TILE = 256
MESH = pl.DeviceIdType.MESH
ROOT_HALF = 0.5**0.5
PEAK = 0.3989422804014327
BF16 = jnp.bfloat16
F32 = jnp.float32


def flip(index, place):
    return index + (1 - 2 * lax.rem(lax.div(index, 2**place), 2)) * 2**place


def bit_of(index, place):
    return lax.rem(lax.div(index, 2**place), 2)


def reversed_bits(value, count):
    out = 0
    for place in range(count):
        out = out * 2 + (value >> place) % 2
    return out


def aligned(start, size, unit):
    return pl.ds(pl.multiple_of(start, unit), size)


def matmul(left, right, contract=((1,), (0,))):
    return lax.dot_general(left, right, (contract, ((), ())), preferred_element_type=F32)


class Plan:
    def __init__(self, narrow, wide, items, slots, width, ff, least=SUB):
        self.narrow, self.wide, self.width, self.ff = narrow, wide, width, ff
        self.items, self.slots = items, slots
        self.rows = items * slots
        self.padded = self.rows + -self.rows % 256
        self.pairs = width // (2 * HEAD_DIM)
        self.narrow_bits = narrow.bit_length() - 1
        self.wide_bits = wide.bit_length() - 1
        rows = width // narrow
        chunk = least
        while rows % (2 * chunk) == 0 and chunk < SUB * wide:
            chunk *= 2
        self.chunk = chunk
        split_bits = (chunk // SUB).bit_length() - 1 if wide > 1 else 0
        self.sums = []
        length = narrow * chunk
        for place in range(self.narrow_bits):
            length //= 2
            self.sums.append(("narrow", place, length, True))
        for place in range(self.wide_bits):
            halve = place < split_bits
            length = length // 2 if halve else length
            self.sums.append(("wide", place, length, halve))
        self.last = length
        self.gathers = []
        for place in reversed(range(split_bits)):
            self.gathers.append(("wide", place, length))
            length *= 2
        self.split_bits = split_bits
        self.depth = len(self.sums) + len(self.gathers)
        self.phases = []
        start = 0
        for rows_block, windows in (
            (ff // narrow, 1),
            (rows, ff // width),
            (rows, 1),
            (rows, 3),
        ):
            count = rows_block // chunk * windows
            self.phases.append((start, count, rows_block, windows))
            start += count
        self.chunks = start
        self.ff_jobs = ff // TILE
        self.norm_job = self.ff_jobs
        self.mix_job = self.norm_job + 1
        self.item_job = self.mix_job + 1
        self.pack_job = self.item_job + items
        self.first_job = self.pack_job + 1
        self.input_job = self.first_job + 1
        self.vector_tick = self.input_job + 1
        assert self.phases[1][0] >= self.norm_job
        assert self.phases[2][0] >= self.mix_job
        assert self.phases[3][0] >= self.first_job
        self.vector_rows = 8 + ff // width
        self.vector_rows += -self.vector_rows % SUB
        self.ticks = self.chunks + self.depth + 1
        assert self.vector_tick + len(self.sums) < self.ticks


def gelu_parts(hidden):
    normal = 0.5 + 0.5 * lax.erf(hidden * ROOT_HALF)
    return normal


def layer_kernel(plan, names, *refs):
    r = types.SimpleNamespace(**dict(zip(names, refs)))
    width, chunk, narrow, slots = plan.width, plan.chunk, plan.narrow, plan.slots
    rows, padded, pairs = plan.rows, plan.padded, plan.pairs
    landed = [getattr(r, f"land{stage}") for stage in range(len(plan.sums))]
    score_scale = HEAD_DIM ** (-0.5)
    spots = {"narrow": lax.axis_index("narrow"), "wide": lax.axis_index("wide")}

    def partner(axis, place):
        return {
            "wide": flip(spots["wide"], place) if axis == "wide" else spots["wide"],
            "narrow": flip(spots["narrow"], place) if axis == "narrow" else spots["narrow"],
        }

    loads = {}
    for number, name in enumerate(("tok", "jw", "mw", "ew", "sw", "cot")):
        loads[name] = pltpu.make_async_copy(
            getattr(r, name + "_in"), getattr(r, name), r.load_sems.at[number]
        )
        loads[name].start()

    barrier = pltpu.get_barrier_semaphore() if plan.sums else None
    for axis, place, _, _ in plan.sums:
        pl.semaphore_signal(barrier, inc=1, device_id=partner(axis, place), device_id_type=MESH)

    def vector(row):
        return r.vec[row : row + 1, :]

    def item_rows(item):
        return aligned(item * slots, slots, SUB)

    def row_live(item):
        return lax.broadcasted_iota(jnp.int32, (slots, 1), 0) < r.visible[item]

    lanes = lax.broadcasted_iota(jnp.int32, (slots, 2 * HEAD_DIM), 1)
    first_head = lanes < HEAD_DIM

    def both_heads(value):
        zero = jnp.zeros_like(value)
        return jnp.concatenate(
            [jnp.where(first_head, value, zero), jnp.where(first_head, zero, value)], axis=0
        ).astype(BF16)

    def one_head_each(value):
        return jnp.where(first_head, value[:slots], value[slots:])

    def normalized(values):
        center = values - jnp.mean(values, axis=-1, keepdims=True)
        spread = lax.rsqrt(jnp.mean(center * center, axis=-1, keepdims=True) + EPSILON)
        return center * spread, spread

    def norm_backward(grad, unit, spread):
        return spread * (
            grad
            - jnp.mean(grad, axis=-1, keepdims=True)
            - unit * jnp.mean(grad * unit, axis=-1, keepdims=True)
        )

    def each_item(body):
        lax.fori_loop(0, plan.items, lambda item, carry: (body(item), carry)[1], 0)

    def each_tile(count, body):
        lax.fori_loop(0, count, lambda tile, carry: (body(tile), carry)[1], 0)

    def pair_lanes(part, pair):
        start = part * width + pair * 2 * HEAD_DIM
        return slice(start, start + 2 * HEAD_DIM)

    r.stage[rows:, :] = jnp.zeros((padded - rows, width), F32)
    r.sums[...] = jnp.zeros_like(r.sums)
    loads["tok"].wait()

    def first_norm(item):
        unit, _ = normalized(r.tok[item].astype(F32))
        r.stage[item_rows(item), :] = unit * vector(0) + vector(1)

    each_item(first_norm)
    r.rowb[...] = r.stage[...].astype(BF16)
    loads["jw"].wait()
    for part, bias in enumerate((2, None, 3)):

        def joint_tile(tile):
            cols = aligned(part * width + tile * TILE, TILE, TILE)
            value = matmul(r.rowb[...], r.jw[:, cols])
            if bias is not None:
                value = value + r.vec[bias : bias + 1, aligned(tile * TILE, TILE, TILE)]
            r.qkv[:, cols] = value.astype(BF16).astype(F32)

        each_tile(width // TILE, joint_tile)
    r.first_t[...] = r.stage[...].T.astype(BF16)
    r.qkv[rows:, :] = jnp.zeros((padded - rows, 3 * width), F32)

    def attend_item(item):
        here = item_rows(item)
        key_live = (
            lax.broadcasted_iota(jnp.int32, (2 * slots, slots), 1) < r.visible[item]
        )
        for pair in range(pairs):
            query = both_heads(r.qkv[here, pair_lanes(0, pair)])
            keys = r.qkv[here, pair_lanes(1, pair)].astype(BF16)
            values = r.qkv[here, pair_lanes(2, pair)].astype(BF16)
            logits = matmul(query, keys, ((1,), (1,))) * score_scale
            logits = jnp.where(key_live, logits, -1000000000.0)
            expo = jnp.exp(logits - jnp.max(logits, axis=-1, keepdims=True))
            attend = expo * (1.0 / jnp.sum(expo, axis=-1, keepdims=True))
            r.attend[item * pairs + pair] = attend
            mixed = one_head_each(matmul(attend.astype(BF16), values))
            r.stage[here, pair_lanes(0, pair)] = mixed

    each_item(attend_item)
    r.rowb[...] = r.stage[...].astype(BF16)
    loads["mw"].wait()

    def mixer_tile(tile):
        cols = aligned(tile * TILE, TILE, TILE)
        r.middle[:, cols] = matmul(r.rowb[...], r.mw[:, cols]) + r.vec[4:5, cols]

    each_tile(width // TILE, mixer_tile)
    r.mixed_t[...] = r.stage[...].T.astype(BF16)

    def second_norm(item):
        here = item_rows(item)
        middle = r.middle[here, :] + r.tok[item].astype(F32)
        r.middle[here, :] = middle
        unit, _ = normalized(middle)
        r.stage[here, :] = unit * vector(5) + vector(6)

    each_item(second_norm)
    r.second[...] = r.stage[...].astype(BF16)
    loads["ew"].wait()

    def expand_bias(tile):
        per_row = width // TILE
        return r.vec[
            pl.ds(8 + lax.div(tile, per_row), 1),
            aligned(lax.rem(tile, per_row) * TILE, TILE, TILE),
        ]

    def expand_tile(tile):
        cols = aligned(tile * TILE, TILE, TILE)
        hidden = matmul(r.second[...], r.ew[:, cols]) + expand_bias(tile)
        active = hidden * gelu_parts(hidden)
        r.wide_rows[:, cols] = active.astype(BF16)
        r.active_t[cols, :] = active.T.astype(BF16)

    each_tile(plan.ff_jobs, expand_tile)
    r.second_t[...] = r.stage[...].T.astype(BF16)
    loads["cot"].wait()

    def mask_cotangent(item):
        grad = r.cot[item].astype(F32)
        r.stage[item_rows(item), :] = jnp.where(row_live(item), grad, 0.0)

    each_item(mask_cotangent)
    r.grad_out[...] = r.stage[...].astype(BF16)
    loads["sw"].wait()

    def ff_job(tile):
        cols = aligned(tile * TILE, TILE, TILE)
        output = matmul(r.wide_rows[:, cols], r.sw[cols, :])
        hidden = matmul(r.second[...], r.ew[:, cols]) + expand_bias(tile)
        grad = matmul(r.grad_out[...], r.sw[cols, :], ((1,), (1,)))
        slope = gelu_parts(hidden) + hidden * (PEAK * jnp.exp(-0.5 * hidden * hidden))
        grad_hidden = (grad * slope).astype(BF16)
        r.wide_rows[:, cols] = grad_hidden
        r.expand_sums[tile] = jnp.sum(grad_hidden.astype(F32), axis=0, keepdims=True)
        grad_second = matmul(grad_hidden, r.ew[:, cols], ((1,), (1,)))

        @pl.when(tile == 0)
        def _():
            r.acc_out[...] = output
            r.acc_grad[...] = grad_second

        @pl.when(tile > 0)
        def _():
            r.acc_out[...] += output
            r.acc_grad[...] += grad_second

    def norm_job():
        def one(item):
            here = item_rows(item)
            live = row_live(item)
            middle = r.middle[here, :]
            grad_out = jnp.where(live, r.cot[item].astype(F32), 0.0)
            layer_out = jnp.where(live, middle + (r.acc_out[here, :] + vector(7)), 0.0)
            r.cot[item] = layer_out.astype(BF16)
            unit, spread = normalized(middle)
            grad = r.acc_grad[here, :]
            r.sums[5:6, :] += jnp.sum(grad * unit, axis=0, keepdims=True)
            r.sums[6:7, :] += jnp.sum(grad, axis=0, keepdims=True)
            r.sums[7:8, :] += jnp.sum(grad_out, axis=0, keepdims=True)
            grad_middle = grad_out + norm_backward(grad * vector(5), unit, spread)
            r.acc_out[here, :] = grad_middle
            r.sums[4:5, :] += jnp.sum(
                grad_middle.astype(BF16).astype(F32), axis=0, keepdims=True
            )

        each_item(one)
        r.grad_branch[:rows_full, :] = r.acc_out[:rows_full, :].astype(BF16)
        tail = jnp.concatenate(
            [r.acc_out[rows_full:rows, :], jnp.zeros((padded - rows, width), F32)], axis=0
        )
        r.grad_branch[rows_full:, :] = tail.astype(BF16)
        layer_copy().start()

    rows_full = rows // 16 * 16

    def layer_copy():
        return pltpu.make_async_copy(r.cot, r.layer_out, r.load_sems.at[0])

    def input_copy():
        return pltpu.make_async_copy(r.tok, r.input_grad, r.load_sems.at[1])

    def mix_job():
        def one(tile):
            cols = aligned(tile * TILE, TILE, TILE)
            value = matmul(r.grad_branch[...], r.mw[cols, :], ((1,), (1,)))
            r.stage[:, cols] = value.astype(BF16).astype(F32)

        each_tile(width // TILE, one)

    def item_job(item):
        here = item_rows(item)
        for pair in range(pairs):
            query = both_heads(r.qkv[here, pair_lanes(0, pair)])
            keys = r.qkv[here, pair_lanes(1, pair)].astype(BF16)
            values = r.qkv[here, pair_lanes(2, pair)].astype(BF16)
            grad_mixed = both_heads(r.stage[here, pair_lanes(0, pair)])
            attend = r.attend[item * pairs + pair]
            grad_attend = matmul(grad_mixed, values, ((1,), (1,)))
            grad_value = matmul(attend.astype(BF16), grad_mixed, ((0,), (0,)))
            inner = jnp.sum(attend * grad_attend, axis=-1, keepdims=True)
            grad_logits = (attend * (grad_attend - inner)).astype(BF16)
            grad_query = one_head_each(matmul(grad_logits, keys)) * score_scale
            grad_key = matmul(grad_logits, query, ((0,), (0,))) * score_scale
            r.qkv[here, pair_lanes(0, pair)] = grad_query
            r.qkv[here, pair_lanes(1, pair)] = grad_key
            r.qkv[here, pair_lanes(2, pair)] = grad_value

    def joint_rows(part):
        return slice(part * padded, (part + 1) * padded)

    def pack_job():
        for part in range(3):
            value = r.qkv[:, part * width : (part + 1) * width].astype(BF16)
            r.sw[joint_rows(part), :] = value
            if part != 1:
                row = 2 if part == 0 else 3
                r.sums[row : row + 1, :] = jnp.sum(value.astype(F32), axis=0, keepdims=True)

    def first_job():
        def one(tile):
            cols = aligned(tile * TILE, TILE, TILE)
            total = None
            for part in range(3):
                value = matmul(
                    r.sw[joint_rows(part), :],
                    r.jw[cols, part * width : (part + 1) * width],
                    ((1,), (1,)),
                )
                total = value if total is None else total + value
            r.acc_grad[:, cols] = total

        each_tile(width // TILE, one)

    def input_job():
        def one(item):
            here = item_rows(item)
            unit, spread = normalized(r.tok[item].astype(F32))
            grad = r.acc_grad[here, :]
            r.sums[0:1, :] += jnp.sum(grad * unit, axis=0, keepdims=True)
            r.sums[1:2, :] += jnp.sum(grad, axis=0, keepdims=True)
            total = r.acc_out[here, :] + norm_backward(grad * vector(0), unit, spread)
            r.tok[item] = total.astype(BF16)

        each_item(one)
        per_row = width // TILE
        for tile in range(plan.ff_jobs):
            row, start = 8 + tile // per_row, tile % per_row * TILE
            r.sums[row : row + 1, start : start + TILE] = r.expand_sums[tile]
        input_copy().start()

    def source(stage, item):
        if stage == 0:
            return r.part.at[lax.rem(item, 2)]
        return landed[stage - 1].at[lax.rem(item, DEPTH)]

    def piece_start(bits):
        start = 0
        for place in range(bits):
            start = start + bit_of(spots["wide"], place) * (chunk // 2 ** (place + 1))
        return start

    def exchange(stage, item):
        slot = lax.rem(item, DEPTH)
        if stage < len(plan.sums):
            axis, place, length, halve = plan.sums[stage]
            there = (1 - bit_of(spots[axis], place)) * length if halve else 0
            src = source(stage, item).at[aligned(there, length, SUB)]
            dst = landed[stage].at[slot]
        else:
            axis, place, length = plan.gathers[stage - len(plan.sums)]
            src = r.whole.at[item, aligned(piece_start(place + 1), length, SUB)]
            dst = src
        return pltpu.make_async_remote_copy(
            src_ref=src,
            dst_ref=dst,
            send_sem=r.send_sems.at[stage, slot],
            recv_sem=r.recv_sems.at[stage, slot],
            device_id=partner(axis, place),
            device_id_type=MESH,
        )

    def produce(item):
        slot = lax.rem(item, 2)
        lefts = (r.active_t, r.second_t, r.mixed_t, r.first_t)
        rights = (r.grad_out, r.wide_rows, r.grad_branch, r.sw)
        for number, (start, count, rows_block, windows) in enumerate(plan.phases):
            left, right = lefts[number], rights[number]

            @pl.when((item >= start) & (item < start + count))
            def _():
                local = item - start
                row = lax.div(local, windows) * chunk
                window = lax.rem(local, windows)
                picked = [
                    left[
                        aligned(
                            reversed_bits(spot, plan.narrow_bits) * rows_block + row, chunk, chunk
                        ),
                        :,
                    ]
                    for spot in range(narrow)
                ]
                if number == 3:
                    other = right[aligned(window * padded, padded, 256), :]
                else:
                    other = right[:, aligned(window * width, width, 128)]
                r.part[slot] = matmul(jnp.concatenate(picked, axis=0), other)

    def absorb(stage, item):
        axis, place, length, halve = plan.sums[stage]
        here = bit_of(spots[axis], place) * length if halve else 0
        slot = lax.rem(item, DEPTH)
        landed[stage][slot] += source(stage, item)[aligned(here, length, SUB)]

    def result_copy(item, act):
        outs = (r.out_shrink, r.out_expand, r.out_mixer, r.out_joint)
        for (start, count, _, windows), out in zip(plan.phases, outs):

            @pl.when((item >= start) & (item < start + count))
            def _():
                local = item - start
                row = lax.div(local, windows) * chunk
                col = lax.rem(local, windows) * width
                copy = pltpu.make_async_copy(
                    r.whole.at[item],
                    out.at[aligned(row, chunk, chunk), aligned(col, width, 128)],
                    r.out_sems.at[lax.rem(item, 2)],
                )
                if act == "start":
                    copy.start()
                else:
                    copy.wait()

    def vector_exchange(stage):
        axis, place, _, _ = plan.sums[stage]
        return pltpu.make_async_remote_copy(
            src_ref=r.sums if stage == 0 else r.vector_land.at[stage - 1],
            dst_ref=r.vector_land.at[stage],
            send_sem=r.vector_sems.at[0, stage],
            recv_sem=r.vector_sems.at[1, stage],
            device_id=partner(axis, place),
            device_id_type=MESH,
        )

    def vector_step(tick):
        count = len(plan.sums)
        for stage in range(count + 1):

            @pl.when(tick == plan.vector_tick + stage)
            def _():
                if stage > 0:
                    vector_exchange(stage - 1).wait()
                    before = r.sums if stage == 1 else r.vector_land.at[stage - 2]
                    r.vector_land[stage - 1] += before[...]
                if stage < count:
                    vector_exchange(stage).start()

    if plan.sums:
        pl.semaphore_wait(barrier, len(plan.sums))

    def step(tick, carry):
        @pl.when(tick < plan.chunks)
        def _():
            produce(tick)
            if plan.depth:
                exchange(0, tick).start()
            else:
                r.whole[tick] = r.part[lax.rem(tick, 2)]
                result_copy(tick, "start")

        for stage in range(plan.depth):
            item = tick - 1 - stage

            @pl.when((item >= 0) & (item < plan.chunks))
            def _():
                exchange(stage, item).wait()
                if stage < len(plan.sums):
                    absorb(stage, item)
                if stage == len(plan.sums) - 1:
                    r.whole[item, aligned(piece_start(plan.split_bits), plan.last, SUB)] = landed[
                        stage
                    ][lax.rem(item, DEPTH)]
                if stage + 1 < plan.depth:
                    exchange(stage + 1, item).start()
                else:
                    result_copy(item, "start")

        done = tick - 1 - plan.depth

        @pl.when(done >= 0)
        def _():
            result_copy(done, "wait")

        vector_step(tick)
        pl.when(tick < plan.ff_jobs)(lambda: ff_job(tick))
        pl.when(tick == plan.norm_job)(norm_job)
        pl.when(tick == plan.mix_job)(mix_job)
        pl.when((tick >= plan.item_job) & (tick < plan.pack_job))(
            lambda: item_job(tick - plan.item_job)
        )
        pl.when(tick == plan.pack_job)(pack_job)
        pl.when(tick == plan.first_job)(first_job)
        pl.when(tick == plan.input_job)(input_job)
        return carry

    lax.fori_loop(0, plan.ticks, step, 0)
    r.vector_out[...] = r.vector_land[len(plan.sums) - 1] if plan.sums else r.sums[...]
    layer_copy().wait()
    input_copy().wait()


def shards(
    tokens,
    visible,
    first_gain,
    first_shift,
    joint_weight,
    query_bias,
    value_bias,
    mixer_weight,
    mixer_bias,
    second_gain,
    second_shift,
    expand_weight,
    expand_bias,
    shrink_weight,
    shrink_bias,
    cotangent,
):
    items, slots, width = tokens.shape
    ff = expand_weight.shape[1]
    narrow, wide = lax.axis_size("narrow"), lax.axis_size("wide")
    plan = Plan(narrow, wide, items, slots, width, ff, SUB if wide > 1 else TILE)
    padded, chunk = plan.padded, plan.chunk
    vectors = jnp.stack(
        [
            first_gain,
            first_shift,
            query_bias,
            value_bias,
            mixer_bias,
            second_gain,
            second_shift,
            shrink_bias,
            *expand_bias.reshape(ff // width, width),
        ]
    ).astype(F32)
    hbm = pl.BlockSpec(memory_space=pl.ANY)
    vmem = pl.BlockSpec(memory_space=pltpu.VMEM)
    smem = pl.BlockSpec(memory_space=pltpu.SMEM)
    inputs = {
        "visible": (visible, smem),
        "vec": (vectors, vmem),
        "tok_in": (tokens, hbm),
        "cot_in": (cotangent, hbm),
        "jw_in": (joint_weight, hbm),
        "mw_in": (mixer_weight, hbm),
        "ew_in": (expand_weight, hbm),
        "sw_in": (shrink_weight, hbm),
    }
    block = width // narrow
    outputs = {
        "layer_out": (tokens.shape, BF16, hbm),
        "input_grad": (tokens.shape, BF16, hbm),
        "out_shrink": ((ff // narrow, width), F32, hbm),
        "out_expand": ((block, ff), F32, hbm),
        "out_mixer": ((block, width), F32, hbm),
        "out_joint": ((block, 3 * width), F32, hbm),
        "vector_out": ((plan.vector_rows, width), F32, vmem),
    }
    scratch = {
        "tok": pltpu.VMEM(tokens.shape, BF16),
        "cot": pltpu.VMEM(tokens.shape, BF16),
        "jw": pltpu.VMEM(joint_weight.shape, BF16),
        "mw": pltpu.VMEM(mixer_weight.shape, BF16),
        "ew": pltpu.VMEM(expand_weight.shape, BF16),
        "sw": pltpu.VMEM(shrink_weight.shape, BF16),
        "stage": pltpu.VMEM((padded, width), F32),
        "rowb": pltpu.VMEM((padded, width), BF16),
        "qkv": pltpu.VMEM((padded, 3 * width), F32),
        "attend": pltpu.VMEM((items * plan.pairs, 2 * slots, slots), F32),
        "first_t": pltpu.VMEM((width, padded), BF16),
        "mixed_t": pltpu.VMEM((width, padded), BF16),
        "second": pltpu.VMEM((padded, width), BF16),
        "second_t": pltpu.VMEM((width, padded), BF16),
        "middle": pltpu.VMEM((padded, width), F32),
        "wide_rows": pltpu.VMEM((padded, ff), BF16),
        "active_t": pltpu.VMEM((ff, padded), BF16),
        "grad_out": pltpu.VMEM((padded, width), BF16),
        "acc_out": pltpu.VMEM((padded, width), F32),
        "acc_grad": pltpu.VMEM((padded, width), F32),
        "grad_branch": pltpu.VMEM((padded, width), BF16),
        "sums": pltpu.VMEM((plan.vector_rows, width), F32),
        "expand_sums": pltpu.VMEM((plan.ff_jobs, 1, TILE), F32),
        "part": pltpu.VMEM((2, narrow * chunk, width), F32),
        "whole": pltpu.VMEM((plan.chunks, chunk, width), F32),
        "load_sems": pltpu.SemaphoreType.DMA((6,)),
        "out_sems": pltpu.SemaphoreType.DMA((2,)),
    }
    if plan.sums:
        for stage, (_, _, length, _) in enumerate(plan.sums):
            scratch[f"land{stage}"] = pltpu.VMEM((DEPTH, length, width), F32)
        scratch["vector_land"] = pltpu.VMEM((len(plan.sums), plan.vector_rows, width), F32)
        scratch["vector_sems"] = pltpu.SemaphoreType.DMA((2, len(plan.sums)))
        scratch["send_sems"] = pltpu.SemaphoreType.DMA((plan.depth, DEPTH))
        scratch["recv_sems"] = pltpu.SemaphoreType.DMA((plan.depth, DEPTH))
    remote = {"collective_id": 0} if plan.sums else {}
    results = pl.pallas_call(
        functools.partial(layer_kernel, plan, (*inputs, *outputs, *scratch)),
        out_shape=[jax.ShapeDtypeStruct(shape, kind) for shape, kind, _ in outputs.values()],
        in_specs=[spec for _, spec in inputs.values()],
        out_specs=[spec for _, _, spec in outputs.values()],
        scratch_shapes=list(scratch.values()),
        compiler_params=pltpu.CompilerParams(
            has_side_effects=True, vmem_limit_bytes=61 * 2**20, **remote
        ),
        name="layer",
    )(*(value for value, _ in inputs.values()))
    layer_out, input_grad, shrink, expand, mixer, joint, sums = results
    own = lax.axis_index("narrow")
    mine = lax.dynamic_slice_in_dim(sums[:8], own * block, block, axis=1)
    wide_sums = sums[8 : 8 + ff // width].reshape(ff)
    expand_sum = lax.dynamic_slice_in_dim(wide_sums, own * (ff // narrow), ff // narrow)
    return (
        layer_out,
        input_grad,
        mine[0],
        mine[1],
        joint,
        mine[2],
        mine[3],
        mixer,
        mine[4],
        mine[5],
        mine[6],
        expand,
        expand_sum,
        shrink,
        mine[7],
    )


def solution(mesh):
    return jax.shard_map(
        shards,
        mesh=mesh,
        in_specs=(
            P(("wide", "narrow"), None, None),
            P(("wide", "narrow")),
            P(),
            P(),
            P(),
            P(),
            P(),
            P(),
            P(),
            P(),
            P(),
            P(),
            P(),
            P(),
            P(),
            P(("wide", "narrow"), None, None),
        ),
        out_specs=(
            P(("wide", "narrow"), None, None),
            P(("wide", "narrow"), None, None),
            P("narrow"),
            P("narrow"),
            P("narrow", None),
            P("narrow"),
            P("narrow"),
            P("narrow", None),
            P("narrow"),
            P("narrow"),
            P("narrow"),
            P("narrow", None),
            P("narrow"),
            P("narrow", None),
            P("narrow"),
        ),
        check_vma=False,
    )
```

```python
import functools
import types

import jax
import jax.numpy as jnp
from jax import lax
from jax.experimental import pallas as pl
from jax.experimental.pallas import tpu as pltpu
from jax.sharding import PartitionSpec as P

HEAD_DIM = 64
EPSILON = 1e-06
SUB = 8
LAGS = ([1, 2, 2, 2, 2, 2, 2, 2], [1, 2, 2, 2, 2, 2, 2, 2])
MOST = 32
TILE = 256
MESH = pl.DeviceIdType.MESH
ROOT_HALF = 0.5**0.5
PEAK = 0.3989422804014327
BF16 = jnp.bfloat16
F32 = jnp.float32


def bit_of(index, place):
    return lax.rem(lax.div(index, 2**place), 2)


def reversed_bits(value, count):
    out = 0
    for place in range(count):
        out = out * 2 + (value >> place) % 2
    return out


def aligned(start, size, unit):
    return pl.ds(pl.multiple_of(start, unit), size)


def matmul(left, right, contract=((1,), (0,))):
    return lax.dot_general(left, right, (contract, ((), ())), preferred_element_type=F32)


class Move:
    def __init__(self, kind, flips, length, select=None, inner=False):
        self.kind, self.flips, self.length = kind, flips, length
        self.select, self.inner = select, inner


class Part:
    def __init__(self, column, columns, picks, sums, gathers, selects):
        self.column, self.columns, self.picks = column, columns, picks
        self.sums, self.moves = sums, sums + gathers
        self.selects = selects
        self.lags = LAGS[column > 0] if len(self.moves) == 8 else [1] + [2] * (len(self.moves) - 1)
        self.due = [sum(self.lags[: stage + 1]) for stage in range(len(self.moves))]

    def slots(self, stage):
        after = self.lags[stage + 1] if stage + 1 < len(self.sums) else 0
        count = 2 * self.lags[stage] + after + 2
        if self.moves[stage].kind in ("fold", "unfold"):
            kinds = [move.kind for move in self.moves]
            ahead = self.due[kinds.index("unfold")] - self.due[kinds.index("fold") - 1]
            count = max(count, ahead + 2)
        return count


class Plan:
    def __init__(self, narrow, wide, items, slots, width, ff):
        self.narrow, self.wide, self.width, self.ff = narrow, wide, width, ff
        self.items, self.slots = items, slots
        self.rows = items * slots
        self.padded = self.rows + -self.rows % 256
        self.pairs = width // (2 * HEAD_DIM)
        narrow_bits = self.narrow_bits = narrow.bit_length() - 1
        wide_bits = self.wide_bits = wide.bit_length() - 1
        rows = width // narrow
        chunk = SUB
        while rows % (2 * chunk) == 0 and chunk < MOST:
            chunk *= 2
        self.chunk = chunk
        near, mirror = (("wide", 1),), (("wide", 1), ("wide", 2))
        x, y, core = (("wide", 0),), (("narrow", 1),), (("narrow", 0),)
        if (narrow, wide) == (4, 8):
            self.links = (core, y, x, near, mirror)
            half, quarter = chunk // 2, chunk // 4
            z_bit, x_bit, y_bit, core_bit = ("wide", 2), x[0], y[0], core[0]
            one = Part(
                0,
                width // 3 * 2,
                [(spot % 2 * 2 + spot // 2, 0, chunk) for spot in range(4)],
                [
                    Move("halve", core, 2 * chunk, core_bit),
                    Move("halve", y, chunk, y_bit),
                    Move("fold", near, chunk),
                    Move("halve", mirror, half, z_bit, True),
                    Move("halve", x, quarter, x_bit, True),
                ],
                [
                    Move("double", x, quarter, inner=True),
                    Move("double", mirror, half, inner=True),
                    Move("unfold", near, chunk),
                ],
                [(z_bit, half), (x_bit, quarter)],
            )
            two = Part(
                width // 3 * 2,
                width // 3,
                [
                    (2 * (spot % 2) + spot // 4, spot // 2 % 2 * half, half)
                    for spot in range(8)
                ],
                [
                    Move("halve", core, 2 * chunk, core_bit),
                    Move("halve", x, chunk, x_bit),
                    Move("halve", y, half, y_bit),
                    Move("fold", near, half),
                    Move("halve", mirror, quarter, z_bit, True),
                ],
                [
                    Move("double", mirror, quarter, inner=True),
                    Move("unfold", near, half),
                    Move("double", x, half),
                ],
                [(x_bit, half), (z_bit, quarter)],
            )
            self.parts = (one, two)
        else:
            self.links = tuple((("narrow", place),) for place in range(narrow_bits))
            self.links += tuple((("wide", place),) for place in range(wide_bits))
            sums, gathers, selects = [], [], []
            length = narrow * chunk
            for (axis, place), in self.links:
                if length > SUB:
                    length //= 2
                    sums.append(Move("halve", ((axis, place),), length, (axis, place)))
                    if axis == "wide":
                        selects.append(((axis, place), length))
                        gathers.insert(0, Move("double", ((axis, place),), length))
                else:
                    sums.append(Move("add", ((axis, place),), length))
            picks = [(reversed_bits(spot, narrow_bits), 0, chunk) for spot in range(narrow)]
            self.parts = (Part(0, width, picks, sums, gathers, selects),)
        self.stages = max(len(part.moves) for part in self.parts)
        self.depth = max(part.due[-1] for part in self.parts)
        self.slots_most = max(
            part.slots(stage) for part in self.parts for stage in range(len(part.moves))
        )
        self.phases = []
        start = 0
        for rows_block, windows in (
            (ff // narrow, 1),
            (rows, ff // width),
            (rows, 1),
            (rows, 3),
        ):
            count = rows_block // chunk * windows
            self.phases.append((start, count, rows_block, windows))
            start += count
        self.chunks = start
        self.ff_jobs = ff // TILE
        self.norm_job = self.ff_jobs
        self.mix_job = self.norm_job + 1
        self.item_job = self.mix_job + 1
        self.pack_job = self.item_job + items
        self.first_job = self.pack_job + 1
        self.input_job = self.first_job + 1
        self.stride = self.phases[1][0] // self.ff_jobs
        self.vector_tick = (self.input_job + 1) * self.stride
        assert self.stride >= 1
        assert self.phases[2][0] > self.mix_job * self.stride
        assert self.phases[3][0] > self.first_job * self.stride
        self.vector_rows = 8 + ff // width
        self.vector_rows += -self.vector_rows % SUB
        self.ticks = self.chunks + self.depth + 1
        self.vector_every = (self.ticks - 1 - self.vector_tick) // len(self.links)
        assert self.vector_every > 0


def gelu_parts(hidden):
    normal = 0.5 + 0.5 * lax.erf(hidden * ROOT_HALF)
    return normal


def layer_kernel(plan, names, *refs):
    r = types.SimpleNamespace(**dict(zip(names, refs)))
    width, chunk, narrow, slots = plan.width, plan.chunk, plan.narrow, plan.slots
    rows, padded, pairs = plan.rows, plan.padded, plan.pairs
    score_scale = HEAD_DIM ** (-0.5)
    spots = {"narrow": lax.axis_index("narrow"), "wide": lax.axis_index("wide")}
    inner = bit_of(spots["wide"], 1) != bit_of(spots["wide"], 2)
    outer = bit_of(spots["wide"], 1) == bit_of(spots["wide"], 2)

    bits = {
        (axis, place): bit_of(spots[axis], place)
        for axis, count in (("narrow", plan.narrow_bits), ("wide", plan.wide_bits))
        for place in range(count)
    }
    partners = {}
    for flips in plan.links:
        there = dict(spots)
        for axis, place in flips:
            there[axis] = there[axis] + (1 - 2 * bits[axis, place]) * 2**place
        partners[flips] = there

    loads = {}
    for number, name in enumerate(("tok", "jw", "mw", "ew", "sw", "cot")):
        loads[name] = pltpu.make_async_copy(
            getattr(r, name + "_in"), getattr(r, name), r.load_sems.at[number]
        )
        loads[name].start()

    barrier = pltpu.get_barrier_semaphore()
    for flips in plan.links:
        pl.semaphore_signal(barrier, inc=1, device_id=partners[flips], device_id_type=MESH)

    def vector(row):
        return r.vec[row : row + 1, :]

    def item_rows(item):
        return aligned(item * slots, slots, SUB)

    def row_live(item):
        return lax.broadcasted_iota(jnp.int32, (slots, 1), 0) < r.visible[item]

    lanes = lax.broadcasted_iota(jnp.int32, (slots, 2 * HEAD_DIM), 1)
    first_head = lanes < HEAD_DIM

    def both_heads(value):
        zero = jnp.zeros_like(value)
        return jnp.concatenate(
            [jnp.where(first_head, value, zero), jnp.where(first_head, zero, value)], axis=0
        ).astype(BF16)

    def one_head_each(value):
        return jnp.where(first_head, value[:slots], value[slots:])

    def normalized(values):
        center = values - jnp.mean(values, axis=-1, keepdims=True)
        spread = lax.rsqrt(jnp.mean(center * center, axis=-1, keepdims=True) + EPSILON)
        return center * spread, spread

    def norm_backward(grad, unit, spread):
        return spread * (
            grad
            - jnp.mean(grad, axis=-1, keepdims=True)
            - unit * jnp.mean(grad * unit, axis=-1, keepdims=True)
        )

    def each_item(body):
        lax.fori_loop(0, plan.items, lambda item, carry: (body(item), carry)[1], 0)

    def each_tile(count, body):
        lax.fori_loop(0, count, lambda tile, carry: (body(tile), carry)[1], 0)

    def pair_lanes(part, pair):
        start = part * width + pair * 2 * HEAD_DIM
        return slice(start, start + 2 * HEAD_DIM)

    r.stage[rows:, :] = jnp.zeros((padded - rows, width), F32)
    r.sums[...] = jnp.zeros_like(r.sums)
    loads["tok"].wait()

    def first_norm(item):
        unit, _ = normalized(r.tok[item].astype(F32))
        r.stage[item_rows(item), :] = unit * vector(0) + vector(1)

    each_item(first_norm)
    r.rowb[...] = r.stage[...].astype(BF16)
    loads["jw"].wait()
    for part, bias in enumerate((2, None, 3)):

        def joint_tile(tile):
            cols = aligned(part * width + tile * TILE, TILE, TILE)
            value = matmul(r.rowb[...], r.jw[:, cols])
            if bias is not None:
                value = value + r.vec[bias : bias + 1, aligned(tile * TILE, TILE, TILE)]
            r.qkv[:, cols] = value.astype(BF16).astype(F32)

        each_tile(width // TILE, joint_tile)
    r.first_t[...] = r.stage[...].T.astype(BF16)
    r.qkv[rows:, :] = jnp.zeros((padded - rows, 3 * width), F32)

    def attend_item(item):
        here = item_rows(item)
        key_live = (
            lax.broadcasted_iota(jnp.int32, (2 * slots, slots), 1) < r.visible[item]
        )
        for pair in range(pairs):
            query = both_heads(r.qkv[here, pair_lanes(0, pair)])
            keys = r.qkv[here, pair_lanes(1, pair)].astype(BF16)
            values = r.qkv[here, pair_lanes(2, pair)].astype(BF16)
            logits = matmul(query, keys, ((1,), (1,))) * score_scale
            logits = jnp.where(key_live, logits, -1000000000.0)
            expo = jnp.exp(logits - jnp.max(logits, axis=-1, keepdims=True))
            attend = expo * (1.0 / jnp.sum(expo, axis=-1, keepdims=True))
            r.attend[item * pairs + pair] = attend
            mixed = one_head_each(matmul(attend.astype(BF16), values))
            r.stage[here, pair_lanes(0, pair)] = mixed

    each_item(attend_item)
    r.rowb[...] = r.stage[...].astype(BF16)
    loads["mw"].wait()

    def mixer_tile(tile):
        cols = aligned(tile * TILE, TILE, TILE)
        r.middle[:, cols] = matmul(r.rowb[...], r.mw[:, cols]) + r.vec[4:5, cols]

    each_tile(width // TILE, mixer_tile)
    r.mixed_t[...] = r.stage[...].T.astype(BF16)

    def second_norm(item):
        here = item_rows(item)
        middle = r.middle[here, :] + r.tok[item].astype(F32)
        r.middle[here, :] = middle
        unit, _ = normalized(middle)
        r.stage[here, :] = unit * vector(5) + vector(6)

    each_item(second_norm)
    r.second[...] = r.stage[...].astype(BF16)
    loads["ew"].wait()

    def expand_bias(tile):
        per_row = width // TILE
        return r.vec[
            pl.ds(8 + lax.div(tile, per_row), 1),
            aligned(lax.rem(tile, per_row) * TILE, TILE, TILE),
        ]

    def expand_tile(tile):
        cols = aligned(tile * TILE, TILE, TILE)
        hidden = matmul(r.second[...], r.ew[:, cols]) + expand_bias(tile)
        active = hidden * gelu_parts(hidden)
        r.wide_rows[:, cols] = active.astype(BF16)
        r.active_t[cols, :] = active.T.astype(BF16)

    each_tile(plan.ff_jobs, expand_tile)
    r.second_t[...] = r.stage[...].T.astype(BF16)
    loads["cot"].wait()

    def mask_cotangent(item):
        grad = r.cot[item].astype(F32)
        r.stage[item_rows(item), :] = jnp.where(row_live(item), grad, 0.0)

    each_item(mask_cotangent)
    r.grad_out[...] = r.stage[...].astype(BF16)
    loads["sw"].wait()

    def ff_job(tile):
        cols = aligned(tile * TILE, TILE, TILE)
        output = matmul(r.wide_rows[:, cols], r.sw[cols, :])
        hidden = matmul(r.second[...], r.ew[:, cols]) + expand_bias(tile)
        grad = matmul(r.grad_out[...], r.sw[cols, :], ((1,), (1,)))
        slope = gelu_parts(hidden) + hidden * (PEAK * jnp.exp(-0.5 * hidden * hidden))
        grad_hidden = (grad * slope).astype(BF16)
        r.wide_rows[:, cols] = grad_hidden
        r.expand_sums[tile] = jnp.sum(grad_hidden.astype(F32), axis=0, keepdims=True)
        grad_second = matmul(grad_hidden, r.ew[:, cols], ((1,), (1,)))

        @pl.when(tile == 0)
        def _():
            r.acc_out[...] = output
            r.acc_grad[...] = grad_second

        @pl.when(tile > 0)
        def _():
            r.acc_out[...] += output
            r.acc_grad[...] += grad_second

    def norm_job():
        def one(item):
            here = item_rows(item)
            live = row_live(item)
            middle = r.middle[here, :]
            grad_out = jnp.where(live, r.cot[item].astype(F32), 0.0)
            layer_out = jnp.where(live, middle + (r.acc_out[here, :] + vector(7)), 0.0)
            r.cot[item] = layer_out.astype(BF16)
            unit, spread = normalized(middle)
            grad = r.acc_grad[here, :]
            r.sums[5:6, :] += jnp.sum(grad * unit, axis=0, keepdims=True)
            r.sums[6:7, :] += jnp.sum(grad, axis=0, keepdims=True)
            r.sums[7:8, :] += jnp.sum(grad_out, axis=0, keepdims=True)
            grad_middle = grad_out + norm_backward(grad * vector(5), unit, spread)
            r.acc_out[here, :] = grad_middle
            r.sums[4:5, :] += jnp.sum(
                grad_middle.astype(BF16).astype(F32), axis=0, keepdims=True
            )

        each_item(one)
        r.grad_branch[:rows_full, :] = r.acc_out[:rows_full, :].astype(BF16)
        tail = jnp.concatenate(
            [r.acc_out[rows_full:rows, :], jnp.zeros((padded - rows, width), F32)], axis=0
        )
        r.grad_branch[rows_full:, :] = tail.astype(BF16)
        layer_copy().start()

    rows_full = rows // 16 * 16

    def layer_copy():
        return pltpu.make_async_copy(r.cot, r.layer_out, r.load_sems.at[0])

    def input_copy():
        return pltpu.make_async_copy(r.tok, r.input_grad, r.load_sems.at[1])

    def mix_job():
        def one(tile):
            cols = aligned(tile * TILE, TILE, TILE)
            value = matmul(r.grad_branch[...], r.mw[cols, :], ((1,), (1,)))
            r.stage[:, cols] = value.astype(BF16).astype(F32)

        each_tile(width // TILE, one)

    def item_job(item):
        here = item_rows(item)
        for pair in range(pairs):
            query = both_heads(r.qkv[here, pair_lanes(0, pair)])
            keys = r.qkv[here, pair_lanes(1, pair)].astype(BF16)
            values = r.qkv[here, pair_lanes(2, pair)].astype(BF16)
            grad_mixed = both_heads(r.stage[here, pair_lanes(0, pair)])
            attend = r.attend[item * pairs + pair]
            grad_attend = matmul(grad_mixed, values, ((1,), (1,)))
            grad_value = matmul(attend.astype(BF16), grad_mixed, ((0,), (0,)))
            inner = jnp.sum(attend * grad_attend, axis=-1, keepdims=True)
            grad_logits = (attend * (grad_attend - inner)).astype(BF16)
            grad_query = one_head_each(matmul(grad_logits, keys)) * score_scale
            grad_key = matmul(grad_logits, query, ((0,), (0,))) * score_scale
            r.qkv[here, pair_lanes(0, pair)] = grad_query
            r.qkv[here, pair_lanes(1, pair)] = grad_key
            r.qkv[here, pair_lanes(2, pair)] = grad_value

    def joint_rows(part):
        return slice(part * padded, (part + 1) * padded)

    def pack_job():
        for part in range(3):
            value = r.qkv[:, part * width : (part + 1) * width].astype(BF16)
            r.sw[joint_rows(part), :] = value
            if part != 1:
                row = 2 if part == 0 else 3
                r.sums[row : row + 1, :] = jnp.sum(value.astype(F32), axis=0, keepdims=True)

    def first_job():
        def one(tile):
            cols = aligned(tile * TILE, TILE, TILE)
            total = None
            for part in range(3):
                value = matmul(
                    r.sw[joint_rows(part), :],
                    r.jw[cols, part * width : (part + 1) * width],
                    ((1,), (1,)),
                )
                total = value if total is None else total + value
            r.acc_grad[:, cols] = total

        each_tile(width // TILE, one)

    def input_job():
        def one(item):
            here = item_rows(item)
            unit, spread = normalized(r.tok[item].astype(F32))
            grad = r.acc_grad[here, :]
            r.sums[0:1, :] += jnp.sum(grad * unit, axis=0, keepdims=True)
            r.sums[1:2, :] += jnp.sum(grad, axis=0, keepdims=True)
            total = r.acc_out[here, :] + norm_backward(grad * vector(0), unit, spread)
            r.tok[item] = total.astype(BF16)

        each_item(one)
        per_row = width // TILE
        for tile in range(plan.ff_jobs):
            row, start = 8 + tile // per_row, tile % per_row * TILE
            r.sums[row : row + 1, start : start + TILE] = r.expand_sums[tile]
        input_copy().start()

    def when(condition, action):
        if condition is True:
            action()
        else:
            pl.when(condition)(action)

    def roles(move):
        if move.kind == "fold":
            return outer, inner
        if move.kind == "unfold":
            return inner, outer
        return (inner, inner) if move.inner else (True, True)

    def land(number, stage, item):
        ref = getattr(r, f"land{number}_{stage}")
        return ref.at[lax.rem(item, plan.parts[number].slots(stage))]

    def source(number, stage, item):
        if stage == 0:
            return getattr(r, f"part{number}").at[lax.rem(item, 2)]
        return land(number, stage - 1, item)

    kept, given, regions = {}, {}, {}
    for number, part in enumerate(plan.parts):
        for stage, move in enumerate(part.moves):
            bit = bits[move.select] if move.select else 0
            kept[number, stage] = bit * move.length
            given[number, stage] = (1 - bit) * move.length if move.select else 0
            regions[number, stage] = sum(
                bits[select] * size for select, size in part.selects if size >= move.length
            )

    def in_whole(number, stage, item):
        part = plan.parts[number]
        return (
            item,
            aligned(regions[number, stage], part.moves[stage].length, SUB),
            pl.ds(part.column, part.columns),
        )

    def transfer(number, stage, item):
        part = plan.parts[number]
        move = part.moves[stage]
        slot = lax.rem(item, part.slots(stage))
        if stage < len(part.sums):
            src = source(number, stage, item).at[
                aligned(given[number, stage], move.length, SUB)
            ]
            dst = land(number, stage, item)
        else:
            src = r.whole.at[in_whole(number, stage, item)]
            dst = src
        return pltpu.make_async_remote_copy(
            src_ref=src,
            dst_ref=dst,
            send_sem=r.send_sems.at[number, stage, slot],
            recv_sem=r.recv_sems.at[number, stage, slot],
            device_id=partners[move.flips],
            device_id_type=MESH,
        )

    def begin(number, stage, item):
        sender, _ = roles(plan.parts[number].moves[stage])
        when(sender, lambda: transfer(number, stage, item).start())

    def settle(number, stage, item):
        part = plan.parts[number]
        move = part.moves[stage]
        sender, receiver = roles(move)

        def receive():
            if stage < len(part.sums):
                land(number, stage, item)[...] += source(number, stage, item)[
                    aligned(kept[number, stage], move.length, SUB)
                ]
            if stage == len(part.sums) - 1:
                r.whole[in_whole(number, stage, item)] = land(number, stage, item)[...]

        if move.kind in ("fold", "unfold"):
            when(sender, lambda: transfer(number, stage, item).wait_send())

            def arrive():
                transfer(number, stage, item).wait_recv()
                receive()

        else:

            def arrive():
                transfer(number, stage, item).wait()
                receive()

        when(receiver, arrive)
        if stage + 1 < len(part.moves):
            begin(number, stage + 1, item)

    def produce(item):
        slot = lax.rem(item, 2)
        lefts = (r.active_t, r.second_t, r.mixed_t, r.first_t)
        rights = (r.grad_out, r.wide_rows, r.grad_branch, r.sw)
        for phase, (start, count, rows_block, windows) in enumerate(plan.phases):
            left, right = lefts[phase], rights[phase]

            @pl.when((item >= start) & (item < start + count))
            def _():
                local = item - start
                row = lax.div(local, windows) * chunk
                window = lax.rem(local, windows)
                for number, part in enumerate(plan.parts):
                    picked = [
                        left[aligned(block * rows_block + row + offset, size, size), :]
                        for block, offset, size in part.picks
                    ]
                    if phase == 3:
                        other = right[
                            aligned(window * padded, padded, 256),
                            part.column : part.column + part.columns,
                        ]
                    else:
                        other = right[
                            :, aligned(window * width + part.column, part.columns, 128)
                        ]
                    getattr(r, f"part{number}")[slot] = matmul(
                        jnp.concatenate(picked, axis=0), other
                    )

    def result_copy(item, act):
        outs = (r.out_shrink, r.out_expand, r.out_mixer, r.out_joint)
        for (start, count, _, windows), out in zip(plan.phases, outs):

            @pl.when((item >= start) & (item < start + count))
            def _():
                local = item - start
                row = lax.div(local, windows) * chunk
                col = lax.rem(local, windows) * width
                copy = pltpu.make_async_copy(
                    r.whole.at[item],
                    out.at[aligned(row, chunk, chunk), aligned(col, width, 128)],
                    r.out_sems.at[lax.rem(item, 2)],
                )
                if act == "start":
                    copy.start()
                else:
                    copy.wait()

    def vector_exchange(stage):
        return pltpu.make_async_remote_copy(
            src_ref=r.sums if stage == 0 else r.vector_land.at[stage - 1],
            dst_ref=r.vector_land.at[stage],
            send_sem=r.vector_sems.at[0, stage],
            recv_sem=r.vector_sems.at[1, stage],
            device_id=partners[plan.links[stage]],
            device_id_type=MESH,
        )

    def vector_step(tick):
        count = len(plan.links)
        for stage in range(count + 1):

            @pl.when(tick == plan.vector_tick + stage * plan.vector_every)
            def _():
                if stage > 0:
                    vector_exchange(stage - 1).wait()
                    before = r.sums if stage == 1 else r.vector_land.at[stage - 2]
                    r.vector_land[stage - 1] += before[...]
                if stage < count:
                    vector_exchange(stage).start()

    pl.semaphore_wait(barrier, len(plan.links))

    def step(tick, carry):
        @pl.when(tick < plan.chunks)
        def _():
            produce(tick)
            for number in range(len(plan.parts)):
                begin(number, 0, tick)

        for stage in range(plan.stages):
            for number, part in enumerate(plan.parts):
                if stage < len(part.moves):
                    item = tick - part.due[stage]

                    @pl.when((item >= 0) & (item < plan.chunks))
                    def _():
                        settle(number, stage, item)

        ready = tick - plan.depth

        @pl.when((ready >= 0) & (ready < plan.chunks))
        def _():
            result_copy(ready, "start")

        done = tick - 1 - plan.depth

        @pl.when(done >= 0)
        def _():
            result_copy(done, "wait")

        vector_step(tick)
        job = lax.div(tick, plan.stride)

        @pl.when(lax.rem(tick, plan.stride) == 0)
        def _():
            pl.when(job < plan.ff_jobs)(lambda: ff_job(job))
            pl.when(job == plan.norm_job)(norm_job)
            pl.when(job == plan.mix_job)(mix_job)
            pl.when((job >= plan.item_job) & (job < plan.pack_job))(
                lambda: item_job(job - plan.item_job)
            )
            pl.when(job == plan.pack_job)(pack_job)
            pl.when(job == plan.first_job)(first_job)
            pl.when(job == plan.input_job)(input_job)

        return carry

    lax.fori_loop(0, plan.ticks, step, 0)
    r.vector_out[...] = r.vector_land[len(plan.links) - 1]
    layer_copy().wait()
    input_copy().wait()


def shards(
    tokens,
    visible,
    first_gain,
    first_shift,
    joint_weight,
    query_bias,
    value_bias,
    mixer_weight,
    mixer_bias,
    second_gain,
    second_shift,
    expand_weight,
    expand_bias,
    shrink_weight,
    shrink_bias,
    cotangent,
):
    items, slots, width = tokens.shape
    ff = expand_weight.shape[1]
    narrow, wide = lax.axis_size("narrow"), lax.axis_size("wide")
    plan = Plan(narrow, wide, items, slots, width, ff)
    padded, chunk = plan.padded, plan.chunk
    vectors = jnp.stack(
        [
            first_gain,
            first_shift,
            query_bias,
            value_bias,
            mixer_bias,
            second_gain,
            second_shift,
            shrink_bias,
            *expand_bias.reshape(ff // width, width),
        ]
    ).astype(F32)
    hbm = pl.BlockSpec(memory_space=pl.ANY)
    vmem = pl.BlockSpec(memory_space=pltpu.VMEM)
    smem = pl.BlockSpec(memory_space=pltpu.SMEM)
    inputs = {
        "visible": (visible, smem),
        "vec": (vectors, vmem),
        "tok_in": (tokens, hbm),
        "cot_in": (cotangent, hbm),
        "jw_in": (joint_weight, hbm),
        "mw_in": (mixer_weight, hbm),
        "ew_in": (expand_weight, hbm),
        "sw_in": (shrink_weight, hbm),
    }
    block = width // narrow
    outputs = {
        "layer_out": (tokens.shape, BF16, hbm),
        "input_grad": (tokens.shape, BF16, hbm),
        "out_shrink": ((ff // narrow, width), F32, hbm),
        "out_expand": ((block, ff), F32, hbm),
        "out_mixer": ((block, width), F32, hbm),
        "out_joint": ((block, 3 * width), F32, hbm),
        "vector_out": ((plan.vector_rows, width), F32, vmem),
    }
    scratch = {
        "tok": pltpu.VMEM(tokens.shape, BF16),
        "cot": pltpu.VMEM(tokens.shape, BF16),
        "jw": pltpu.VMEM(joint_weight.shape, BF16),
        "mw": pltpu.VMEM(mixer_weight.shape, BF16),
        "ew": pltpu.VMEM(expand_weight.shape, BF16),
        "sw": pltpu.VMEM(shrink_weight.shape, BF16),
        "stage": pltpu.VMEM((padded, width), F32),
        "rowb": pltpu.VMEM((padded, width), BF16),
        "qkv": pltpu.VMEM((padded, 3 * width), F32),
        "attend": pltpu.VMEM((items * plan.pairs, 2 * slots, slots), F32),
        "first_t": pltpu.VMEM((width, padded), BF16),
        "mixed_t": pltpu.VMEM((width, padded), BF16),
        "second": pltpu.VMEM((padded, width), BF16),
        "second_t": pltpu.VMEM((width, padded), BF16),
        "middle": pltpu.VMEM((padded, width), F32),
        "wide_rows": pltpu.VMEM((padded, ff), BF16),
        "active_t": pltpu.VMEM((ff, padded), BF16),
        "grad_out": pltpu.VMEM((padded, width), BF16),
        "acc_out": pltpu.VMEM((padded, width), F32),
        "acc_grad": pltpu.VMEM((padded, width), F32),
        "grad_branch": pltpu.VMEM((padded, width), BF16),
        "sums": pltpu.VMEM((plan.vector_rows, width), F32),
        "expand_sums": pltpu.VMEM((plan.ff_jobs, 1, TILE), F32),
        "whole": pltpu.VMEM((plan.chunks, chunk, width), F32),
        "vector_land": pltpu.VMEM((len(plan.links), plan.vector_rows, width), F32),
        "load_sems": pltpu.SemaphoreType.DMA((6,)),
        "out_sems": pltpu.SemaphoreType.DMA((2,)),
        "vector_sems": pltpu.SemaphoreType.DMA((2, len(plan.links))),
        "send_sems": pltpu.SemaphoreType.DMA((len(plan.parts), plan.stages, plan.slots_most)),
        "recv_sems": pltpu.SemaphoreType.DMA((len(plan.parts), plan.stages, plan.slots_most)),
    }
    for number, part in enumerate(plan.parts):
        scratch[f"part{number}"] = pltpu.VMEM((2, narrow * chunk, part.columns), F32)
        for stage, move in enumerate(part.sums):
            scratch[f"land{number}_{stage}"] = pltpu.VMEM(
                (part.slots(stage), move.length, part.columns), F32
            )
    results = pl.pallas_call(
        functools.partial(layer_kernel, plan, (*inputs, *outputs, *scratch)),
        out_shape=[jax.ShapeDtypeStruct(shape, kind) for shape, kind, _ in outputs.values()],
        in_specs=[spec for _, spec in inputs.values()],
        out_specs=[spec for _, _, spec in outputs.values()],
        scratch_shapes=list(scratch.values()),
        compiler_params=pltpu.CompilerParams(
            has_side_effects=True, vmem_limit_bytes=61 * 2**20, collective_id=0
        ),
        name="layer",
    )(*(value for value, _ in inputs.values()))
    layer_out, input_grad, shrink, expand, mixer, joint, sums = results
    own = lax.axis_index("narrow")
    mine = lax.dynamic_slice_in_dim(sums[:8], own * block, block, axis=1)
    wide_sums = sums[8 : 8 + ff // width].reshape(ff)
    expand_sum = lax.dynamic_slice_in_dim(wide_sums, own * (ff // narrow), ff // narrow)
    return (
        layer_out,
        input_grad,
        mine[0],
        mine[1],
        joint,
        mine[2],
        mine[3],
        mixer,
        mine[4],
        mine[5],
        mine[6],
        expand,
        expand_sum,
        shrink,
        mine[7],
    )


def solution(mesh):
    return jax.shard_map(
        shards,
        mesh=mesh,
        in_specs=(
            P(("wide", "narrow"), None, None),
            P(("wide", "narrow")),
            P(),
            P(),
            P(),
            P(),
            P(),
            P(),
            P(),
            P(),
            P(),
            P(),
            P(),
            P(),
            P(),
            P(("wide", "narrow"), None, None),
        ),
        out_specs=(
            P(("wide", "narrow"), None, None),
            P(("wide", "narrow"), None, None),
            P("narrow"),
            P("narrow"),
            P("narrow", None),
            P("narrow"),
            P("narrow"),
            P("narrow", None),
            P("narrow"),
            P("narrow"),
            P("narrow"),
            P("narrow", None),
            P("narrow"),
            P("narrow", None),
            P("narrow"),
        ),
        check_vma=False,
    )
```

```python
import functools
import types

import jax
import jax.numpy as jnp
from jax import lax
from jax.experimental import pallas as pl
from jax.experimental.pallas import tpu as pltpu
from jax.sharding import PartitionSpec as P

HEAD_DIM = 64
EPSILON = 1e-06
SUB = 8
LAGS = ([1, 2, 2, 2, 2, 2, 2, 2], [1, 2, 2, 2, 2, 2, 2, 2])
MOST = 32
TILE = 256
MESH = pl.DeviceIdType.MESH
ROOT_HALF = 0.5**0.5
PEAK = 0.3989422804014327
BF16 = jnp.bfloat16
F32 = jnp.float32


def bit_of(index, place):
    return lax.rem(lax.div(index, 2**place), 2)


def reversed_bits(value, count):
    out = 0
    for place in range(count):
        out = out * 2 + (value >> place) % 2
    return out


def aligned(start, size, unit):
    return pl.ds(pl.multiple_of(start, unit), size)


def matmul(left, right, contract=((1,), (0,))):
    return lax.dot_general(left, right, (contract, ((), ())), preferred_element_type=F32)


class Move:
    def __init__(self, kind, flips, length, select=None, inner=False):
        self.kind, self.flips, self.length = kind, flips, length
        self.select, self.inner = select, inner


class Part:
    def __init__(self, column, columns, picks, sums, gathers, selects):
        self.column, self.columns, self.picks = column, columns, picks
        self.sums, self.moves = sums, sums + gathers
        self.selects = selects
        self.lags = LAGS[column > 0] if len(self.moves) == 8 else [1] + [2] * (len(self.moves) - 1)
        self.due = [sum(self.lags[: stage + 1]) for stage in range(len(self.moves))]

    def slots(self, stage):
        after = self.lags[stage + 1] if stage + 1 < len(self.sums) else 0
        count = 2 * self.lags[stage] + after + 2
        if self.moves[stage].kind in ("fold", "unfold"):
            kinds = [move.kind for move in self.moves]
            ahead = self.due[kinds.index("unfold")] - self.due[kinds.index("fold") - 1]
            count = max(count, ahead + 2)
        return count


class Plan:
    def __init__(self, narrow, wide, items, slots, width, ff):
        self.narrow, self.wide, self.width, self.ff = narrow, wide, width, ff
        self.items, self.slots = items, slots
        self.rows = items * slots
        self.padded = self.rows + -self.rows % 256
        self.pairs = width // (2 * HEAD_DIM)
        narrow_bits = self.narrow_bits = narrow.bit_length() - 1
        wide_bits = self.wide_bits = wide.bit_length() - 1
        rows = width // narrow
        chunk = SUB
        while rows % (2 * chunk) == 0 and chunk < MOST:
            chunk *= 2
        self.chunk = chunk
        near, mirror = (("wide", 1),), (("wide", 1), ("wide", 2))
        x, y, core = (("wide", 0),), (("narrow", 1),), (("narrow", 0),)
        if (narrow, wide) == (4, 8):
            self.links = (core, y, x, near, mirror)
            half, quarter = chunk // 2, chunk // 4
            z_bit, x_bit, y_bit, core_bit = ("wide", 2), x[0], y[0], core[0]
            one = Part(
                0,
                width // 3 * 2,
                [(spot % 2 * 2 + spot // 2, 0, chunk) for spot in range(4)],
                [
                    Move("halve", core, 2 * chunk, core_bit),
                    Move("halve", y, chunk, y_bit),
                    Move("fold", near, chunk),
                    Move("halve", mirror, half, z_bit, True),
                    Move("halve", x, quarter, x_bit, True),
                ],
                [
                    Move("double", x, quarter, inner=True),
                    Move("double", mirror, half, inner=True),
                    Move("unfold", near, chunk),
                ],
                [(z_bit, half), (x_bit, quarter)],
            )
            two = Part(
                width // 3 * 2,
                width // 3,
                [
                    (2 * (spot % 2) + spot // 4, spot // 2 % 2 * half, half)
                    for spot in range(8)
                ],
                [
                    Move("halve", core, 2 * chunk, core_bit),
                    Move("halve", x, chunk, x_bit),
                    Move("halve", y, half, y_bit),
                    Move("fold", near, half),
                    Move("halve", mirror, quarter, z_bit, True),
                ],
                [
                    Move("double", mirror, quarter, inner=True),
                    Move("unfold", near, half),
                    Move("double", x, half),
                ],
                [(x_bit, half), (z_bit, quarter)],
            )
            self.parts = (one, two)
        else:
            self.links = tuple((("narrow", place),) for place in range(narrow_bits))
            self.links += tuple((("wide", place),) for place in range(wide_bits))
            sums, gathers, selects = [], [], []
            length = narrow * chunk
            for (axis, place), in self.links:
                if length > SUB:
                    length //= 2
                    sums.append(Move("halve", ((axis, place),), length, (axis, place)))
                    if axis == "wide":
                        selects.append(((axis, place), length))
                        gathers.insert(0, Move("double", ((axis, place),), length))
                else:
                    sums.append(Move("add", ((axis, place),), length))
            picks = [(reversed_bits(spot, narrow_bits), 0, chunk) for spot in range(narrow)]
            self.parts = (Part(0, width, picks, sums, gathers, selects),)
        self.stages = max(len(part.moves) for part in self.parts)
        self.depth = max(part.due[-1] for part in self.parts)
        self.slots_most = max(
            part.slots(stage) for part in self.parts for stage in range(len(part.moves))
        )
        self.phases = []
        start = 0
        for rows_block, windows in (
            (ff // narrow, 1),
            (rows, ff // width),
            (rows, 1),
            (rows, 3),
        ):
            count = rows_block // chunk * windows
            self.phases.append((start, count, rows_block, windows))
            start += count
        self.chunks = start
        self.ff_jobs = ff // TILE
        self.norm_job = self.ff_jobs
        self.mix_job = self.norm_job + 1
        self.item_job = self.mix_job + 1
        self.pack_job = self.item_job + items
        self.first_job = self.pack_job + 1
        self.input_job = self.first_job + 1
        self.stride = self.phases[1][0] // self.ff_jobs
        self.vector_tick = (self.input_job + 1) * self.stride
        assert self.stride >= 1
        assert self.phases[2][0] > self.mix_job * self.stride
        assert self.phases[3][0] > self.first_job * self.stride
        self.vector_rows = 8 + ff // width
        self.vector_rows += -self.vector_rows % SUB
        self.ticks = self.chunks + self.depth
        self.vector_every = (self.ticks - 1 - self.vector_tick) // len(self.links)
        assert self.vector_every > 0


def gelu_parts(hidden):
    normal = 0.5 + 0.5 * lax.erf(hidden * ROOT_HALF)
    return normal


def layer_kernel(plan, names, *refs):
    r = types.SimpleNamespace(**dict(zip(names, refs)))
    width, chunk, narrow, slots = plan.width, plan.chunk, plan.narrow, plan.slots
    rows, padded, pairs = plan.rows, plan.padded, plan.pairs
    score_scale = HEAD_DIM ** (-0.5)
    spots = {"narrow": lax.axis_index("narrow"), "wide": lax.axis_index("wide")}
    inner = bit_of(spots["wide"], 1) != bit_of(spots["wide"], 2)
    outer = bit_of(spots["wide"], 1) == bit_of(spots["wide"], 2)

    bits = {
        (axis, place): bit_of(spots[axis], place)
        for axis, count in (("narrow", plan.narrow_bits), ("wide", plan.wide_bits))
        for place in range(count)
    }
    partners = {}
    for flips in plan.links:
        there = dict(spots)
        for axis, place in flips:
            there[axis] = there[axis] + (1 - 2 * bits[axis, place]) * 2**place
        partners[flips] = there

    loads = {}
    for number, name in enumerate(("tok", "jw", "mw", "ew", "sw", "cot")):
        loads[name] = pltpu.make_async_copy(
            getattr(r, name + "_in"), getattr(r, name), r.load_sems.at[number]
        )
        loads[name].start()

    barrier = pltpu.get_barrier_semaphore()
    for flips in plan.links:
        pl.semaphore_signal(barrier, inc=1, device_id=partners[flips], device_id_type=MESH)

    def vector(row):
        return r.vec[row : row + 1, :]

    def item_rows(item):
        return aligned(item * slots, slots, SUB)

    def row_live(item):
        return lax.broadcasted_iota(jnp.int32, (slots, 1), 0) < r.visible[item]

    lanes = lax.broadcasted_iota(jnp.int32, (slots, 2 * HEAD_DIM), 1)
    first_head = lanes < HEAD_DIM

    def both_heads(value):
        zero = jnp.zeros_like(value)
        return jnp.concatenate(
            [jnp.where(first_head, value, zero), jnp.where(first_head, zero, value)], axis=0
        ).astype(BF16)

    def one_head_each(value):
        return jnp.where(first_head, value[:slots], value[slots:])

    def normalized(values):
        center = values - jnp.mean(values, axis=-1, keepdims=True)
        spread = lax.rsqrt(jnp.mean(center * center, axis=-1, keepdims=True) + EPSILON)
        return center * spread, spread

    def norm_backward(grad, unit, spread):
        return spread * (
            grad
            - jnp.mean(grad, axis=-1, keepdims=True)
            - unit * jnp.mean(grad * unit, axis=-1, keepdims=True)
        )

    def each_item(body):
        lax.fori_loop(0, plan.items, lambda item, carry: (body(item), carry)[1], 0)

    def each_tile(count, body):
        lax.fori_loop(0, count, lambda tile, carry: (body(tile), carry)[1], 0)

    def pair_lanes(part, pair):
        start = part * width + pair * 2 * HEAD_DIM
        return slice(start, start + 2 * HEAD_DIM)

    small = (r.g1, r.s1, r.qb, r.vb, r.mb, r.g2, r.s2, r.sb)
    for row, ref in enumerate(small):
        r.vec[row : row + 1, :] = ref[...].astype(F32).reshape(1, width)
    for row in range(plan.ff // width):
        value = r.eb[row * width : (row + 1) * width].astype(F32)
        r.vec[8 + row : 9 + row, :] = value.reshape(1, width)
    r.stage[rows:, :] = jnp.zeros((padded - rows, width), F32)
    r.sums[...] = jnp.zeros_like(r.sums)
    loads["tok"].wait()

    def first_norm(item):
        unit, _ = normalized(r.tok[item].astype(F32))
        r.stage[item_rows(item), :] = unit * vector(0) + vector(1)

    each_item(first_norm)
    r.rowb[...] = r.stage[...].astype(BF16)
    loads["jw"].wait()
    for part, bias in enumerate((2, None, 3)):

        def joint_tile(tile):
            cols = aligned(part * width + tile * TILE, TILE, TILE)
            value = matmul(r.rowb[...], r.jw[:, cols])
            if bias is not None:
                value = value + r.vec[bias : bias + 1, aligned(tile * TILE, TILE, TILE)]
            r.qkv[:, cols] = value.astype(BF16).astype(F32)

        each_tile(width // TILE, joint_tile)
    r.first_t[...] = r.stage[...].T.astype(BF16)
    r.qkv[rows:, :] = jnp.zeros((padded - rows, 3 * width), F32)

    def attend_item(item):
        here = item_rows(item)
        key_live = (
            lax.broadcasted_iota(jnp.int32, (2 * slots, slots), 1) < r.visible[item]
        )
        for pair in range(pairs):
            query = both_heads(r.qkv[here, pair_lanes(0, pair)])
            keys = r.qkv[here, pair_lanes(1, pair)].astype(BF16)
            values = r.qkv[here, pair_lanes(2, pair)].astype(BF16)
            logits = matmul(query, keys, ((1,), (1,))) * score_scale
            logits = jnp.where(key_live, logits, -1000000000.0)
            expo = jnp.exp(logits - jnp.max(logits, axis=-1, keepdims=True))
            attend = expo * (1.0 / jnp.sum(expo, axis=-1, keepdims=True))
            r.attend[item * pairs + pair] = attend
            mixed = one_head_each(matmul(attend.astype(BF16), values))
            r.stage[here, pair_lanes(0, pair)] = mixed

    each_item(attend_item)
    r.rowb[...] = r.stage[...].astype(BF16)
    loads["mw"].wait()

    def mixer_tile(tile):
        cols = aligned(tile * TILE, TILE, TILE)
        r.middle[:, cols] = matmul(r.rowb[...], r.mw[:, cols]) + r.vec[4:5, cols]

    each_tile(width // TILE, mixer_tile)
    r.mixed_t[...] = r.stage[...].T.astype(BF16)

    def second_norm(item):
        here = item_rows(item)
        middle = r.middle[here, :] + r.tok[item].astype(F32)
        r.middle[here, :] = middle
        unit, _ = normalized(middle)
        r.stage[here, :] = unit * vector(5) + vector(6)

    each_item(second_norm)
    r.second[...] = r.stage[...].astype(BF16)
    loads["ew"].wait()

    def expand_bias(tile):
        per_row = width // TILE
        return r.vec[
            pl.ds(8 + lax.div(tile, per_row), 1),
            aligned(lax.rem(tile, per_row) * TILE, TILE, TILE),
        ]

    def expand_tile(tile):
        cols = aligned(tile * TILE, TILE, TILE)
        hidden = matmul(r.second[...], r.ew[:, cols]) + expand_bias(tile)
        active = hidden * gelu_parts(hidden)
        r.wide_rows[:, cols] = active.astype(BF16)
        r.active_t[cols, :] = active.T.astype(BF16)

    each_tile(plan.ff_jobs, expand_tile)
    r.second_t[...] = r.stage[...].T.astype(BF16)
    loads["cot"].wait()

    def mask_cotangent(item):
        grad = r.cot[item].astype(F32)
        r.stage[item_rows(item), :] = jnp.where(row_live(item), grad, 0.0)

    each_item(mask_cotangent)
    r.grad_out[...] = r.stage[...].astype(BF16)
    loads["sw"].wait()

    def ff_job(tile):
        cols = aligned(tile * TILE, TILE, TILE)
        output = matmul(r.wide_rows[:, cols], r.sw[cols, :])
        hidden = matmul(r.second[...], r.ew[:, cols]) + expand_bias(tile)
        grad = matmul(r.grad_out[...], r.sw[cols, :], ((1,), (1,)))
        slope = gelu_parts(hidden) + hidden * (PEAK * jnp.exp(-0.5 * hidden * hidden))
        grad_hidden = (grad * slope).astype(BF16)
        r.wide_rows[:, cols] = grad_hidden
        r.expand_sums[tile] = jnp.sum(grad_hidden.astype(F32), axis=0, keepdims=True)
        grad_second = matmul(grad_hidden, r.ew[:, cols], ((1,), (1,)))

        @pl.when(tile == 0)
        def _():
            r.acc_out[...] = output
            r.acc_grad[...] = grad_second

        @pl.when(tile > 0)
        def _():
            r.acc_out[...] += output
            r.acc_grad[...] += grad_second

    def norm_job():
        def one(item):
            here = item_rows(item)
            live = row_live(item)
            middle = r.middle[here, :]
            grad_out = jnp.where(live, r.cot[item].astype(F32), 0.0)
            layer_out = jnp.where(live, middle + (r.acc_out[here, :] + vector(7)), 0.0)
            r.cot[item] = layer_out.astype(BF16)
            unit, spread = normalized(middle)
            grad = r.acc_grad[here, :]
            r.sums[5:6, :] += jnp.sum(grad * unit, axis=0, keepdims=True)
            r.sums[6:7, :] += jnp.sum(grad, axis=0, keepdims=True)
            r.sums[7:8, :] += jnp.sum(grad_out, axis=0, keepdims=True)
            grad_middle = grad_out + norm_backward(grad * vector(5), unit, spread)
            r.acc_out[here, :] = grad_middle
            r.sums[4:5, :] += jnp.sum(
                grad_middle.astype(BF16).astype(F32), axis=0, keepdims=True
            )

        each_item(one)
        r.grad_branch[:rows_full, :] = r.acc_out[:rows_full, :].astype(BF16)
        tail = jnp.concatenate(
            [r.acc_out[rows_full:rows, :], jnp.zeros((padded - rows, width), F32)], axis=0
        )
        r.grad_branch[rows_full:, :] = tail.astype(BF16)

    rows_full = rows // 16 * 16

    def mix_job():
        def one(tile):
            cols = aligned(tile * TILE, TILE, TILE)
            value = matmul(r.grad_branch[...], r.mw[cols, :], ((1,), (1,)))
            r.stage[:, cols] = value.astype(BF16).astype(F32)

        each_tile(width // TILE, one)

    def item_job(item):
        here = item_rows(item)
        for pair in range(pairs):
            query = both_heads(r.qkv[here, pair_lanes(0, pair)])
            keys = r.qkv[here, pair_lanes(1, pair)].astype(BF16)
            values = r.qkv[here, pair_lanes(2, pair)].astype(BF16)
            grad_mixed = both_heads(r.stage[here, pair_lanes(0, pair)])
            attend = r.attend[item * pairs + pair]
            grad_attend = matmul(grad_mixed, values, ((1,), (1,)))
            grad_value = matmul(attend.astype(BF16), grad_mixed, ((0,), (0,)))
            inner = jnp.sum(attend * grad_attend, axis=-1, keepdims=True)
            grad_logits = (attend * (grad_attend - inner)).astype(BF16)
            grad_query = one_head_each(matmul(grad_logits, keys)) * score_scale
            grad_key = matmul(grad_logits, query, ((0,), (0,))) * score_scale
            r.qkv[here, pair_lanes(0, pair)] = grad_query
            r.qkv[here, pair_lanes(1, pair)] = grad_key
            r.qkv[here, pair_lanes(2, pair)] = grad_value

    def joint_rows(part):
        return slice(part * padded, (part + 1) * padded)

    def pack_job():
        for part in range(3):
            value = r.qkv[:, part * width : (part + 1) * width].astype(BF16)
            r.sw[joint_rows(part), :] = value
            if part != 1:
                row = 2 if part == 0 else 3
                r.sums[row : row + 1, :] = jnp.sum(value.astype(F32), axis=0, keepdims=True)

    def first_job():
        def one(tile):
            cols = aligned(tile * TILE, TILE, TILE)
            total = None
            for part in range(3):
                value = matmul(
                    r.sw[joint_rows(part), :],
                    r.jw[cols, part * width : (part + 1) * width],
                    ((1,), (1,)),
                )
                total = value if total is None else total + value
            r.acc_grad[:, cols] = total

        each_tile(width // TILE, one)

    def input_job():
        def one(item):
            here = item_rows(item)
            unit, spread = normalized(r.tok[item].astype(F32))
            grad = r.acc_grad[here, :]
            r.sums[0:1, :] += jnp.sum(grad * unit, axis=0, keepdims=True)
            r.sums[1:2, :] += jnp.sum(grad, axis=0, keepdims=True)
            total = r.acc_out[here, :] + norm_backward(grad * vector(0), unit, spread)
            r.tok[item] = total.astype(BF16)

        each_item(one)
        per_row = width // TILE
        for tile in range(plan.ff_jobs):
            row, start = 8 + tile // per_row, tile % per_row * TILE
            r.sums[row : row + 1, start : start + TILE] = r.expand_sums[tile]

    def when(condition, action):
        if condition is True:
            action()
        else:
            pl.when(condition)(action)

    def roles(move):
        if move.kind == "fold":
            return outer, inner
        if move.kind == "unfold":
            return inner, outer
        return (inner, inner) if move.inner else (True, True)

    def land(number, stage, item):
        ref = getattr(r, f"land{number}_{stage}")
        return ref.at[lax.rem(item, plan.parts[number].slots(stage))]

    def source(number, stage, item):
        if stage == 0:
            return getattr(r, f"part{number}").at[lax.rem(item, 2)]
        return land(number, stage - 1, item)

    kept, given, regions = {}, {}, {}
    for number, part in enumerate(plan.parts):
        for stage, move in enumerate(part.moves):
            bit = bits[move.select] if move.select else 0
            kept[number, stage] = bit * move.length
            given[number, stage] = (1 - bit) * move.length if move.select else 0
            regions[number, stage] = sum(
                bits[select] * size for select, size in part.selects if size >= move.length
            )

    def in_whole(number, stage, item):
        part = plan.parts[number]
        return (
            item,
            aligned(regions[number, stage], part.moves[stage].length, SUB),
            pl.ds(part.column, part.columns),
        )

    def transfer(number, stage, item):
        part = plan.parts[number]
        move = part.moves[stage]
        slot = lax.rem(item, part.slots(stage))
        if stage < len(part.sums):
            src = source(number, stage, item).at[
                aligned(given[number, stage], move.length, SUB)
            ]
            dst = land(number, stage, item)
        else:
            src = r.whole.at[in_whole(number, stage, item)]
            dst = src
        return pltpu.make_async_remote_copy(
            src_ref=src,
            dst_ref=dst,
            send_sem=r.send_sems.at[number, stage, slot],
            recv_sem=r.recv_sems.at[number, stage, slot],
            device_id=partners[move.flips],
            device_id_type=MESH,
        )

    def begin(number, stage, item):
        sender, _ = roles(plan.parts[number].moves[stage])
        when(sender, lambda: transfer(number, stage, item).start())

    def settle(number, stage, item):
        part = plan.parts[number]
        move = part.moves[stage]
        sender, receiver = roles(move)

        def receive():
            if stage < len(part.sums):
                land(number, stage, item)[...] += source(number, stage, item)[
                    aligned(kept[number, stage], move.length, SUB)
                ]
            if stage == len(part.sums) - 1:
                r.whole[in_whole(number, stage, item)] = land(number, stage, item)[...]

        if move.kind in ("fold", "unfold"):
            when(sender, lambda: transfer(number, stage, item).wait_send())

            def arrive():
                transfer(number, stage, item).wait_recv()
                receive()

        else:

            def arrive():
                transfer(number, stage, item).wait()
                receive()

        when(receiver, arrive)
        if stage + 1 < len(part.moves):
            begin(number, stage + 1, item)

    def rows_of(phase):
        _, count, _, windows = plan.phases[phase]
        return count // windows

    def produce(item):
        slot = lax.rem(item, 2)
        lefts = (r.active_t, r.second_t, r.mixed_t, r.first_t)
        rights = (r.grad_out, r.wide_rows, r.grad_branch, r.sw)
        for phase, (start, count, rows_block, windows) in enumerate(plan.phases):
            left, right = lefts[phase], rights[phase]

            @pl.when((item >= start) & (item < start + count))
            def _():
                local = item - start
                tall = rows_of(phase)
                row = lax.rem(local, tall) * chunk
                window = lax.div(local, tall)
                for number, part in enumerate(plan.parts):
                    picked = [
                        left[aligned(block * rows_block + row + offset, size, size), :]
                        for block, offset, size in part.picks
                    ]
                    if phase == 3:
                        other = right[
                            aligned(window * padded, padded, 256),
                            part.column : part.column + part.columns,
                        ]
                    else:
                        other = right[
                            :, aligned(window * width + part.column, part.columns, 128)
                        ]
                    getattr(r, f"part{number}")[slot] = matmul(
                        jnp.concatenate(picked, axis=0), other
                    )

    def vector_exchange(stage):
        return pltpu.make_async_remote_copy(
            src_ref=r.sums if stage == 0 else r.vector_land.at[stage - 1],
            dst_ref=r.vector_land.at[stage],
            send_sem=r.vector_sems.at[0, stage],
            recv_sem=r.vector_sems.at[1, stage],
            device_id=partners[plan.links[stage]],
            device_id_type=MESH,
        )

    def vector_step(tick):
        count = len(plan.links)
        for stage in range(count + 1):

            @pl.when(tick == plan.vector_tick + stage * plan.vector_every)
            def _():
                if stage > 0:
                    vector_exchange(stage - 1).wait()
                    before = r.sums if stage == 1 else r.vector_land.at[stage - 2]
                    r.vector_land[stage - 1] += before[...]
                if stage < count:
                    vector_exchange(stage).start()

    pl.semaphore_wait(barrier, len(plan.links))

    def step(tick, carry):
        @pl.when(tick < plan.chunks)
        def _():
            produce(tick)
            for number in range(len(plan.parts)):
                begin(number, 0, tick)

        for stage in range(plan.stages):
            for number, part in enumerate(plan.parts):
                if stage < len(part.moves):
                    item = tick - part.due[stage]

                    @pl.when((item >= 0) & (item < plan.chunks))
                    def _():
                        settle(number, stage, item)

        vector_step(tick)
        job = lax.div(tick, plan.stride)

        @pl.when(lax.rem(tick, plan.stride) == 0)
        def _():
            pl.when(job < plan.ff_jobs)(lambda: ff_job(job))
            pl.when(job == plan.norm_job)(norm_job)
            pl.when(job == plan.mix_job)(mix_job)
            pl.when((job >= plan.item_job) & (job < plan.pack_job))(
                lambda: item_job(job - plan.item_job)
            )
            pl.when(job == plan.pack_job)(pack_job)
            pl.when(job == plan.first_job)(first_job)
            pl.when(job == plan.input_job)(input_job)

        return carry

    lax.fori_loop(0, plan.ticks, step, 0)
    r.vector_out[...] = r.vector_land[len(plan.links) - 1]


def write_kernel(plan, tok, cot, whole, sums, *refs):
    outs, sems = refs[:-1], refs[-1]
    copies = [(tok, outs[0]), (cot, outs[1])]
    for (start, count, _, windows), out in zip(plan.phases, outs[2:6]):
        tall = count // windows
        for window in range(windows):
            first = start + window * tall
            cols = pl.ds(window * plan.width, plan.width)
            copies.append((whole.at[first : first + tall], out.at[:, :, cols]))
    copies = [
        pltpu.make_async_copy(source, target, sems.at[number])
        for number, (source, target) in enumerate(copies)
    ]
    for copy in copies:
        copy.start()
    own = lax.axis_index("narrow")
    for place in range(plan.narrow):

        @pl.when(own == place)
        def _():
            for row, out in enumerate(outs[6:14]):
                size = out.shape[0]
                out[...] = sums[row : row + 1, place * size : (place + 1) * size].reshape(size)
            size = outs[14].shape[0]
            row, start = 8 + place * size // plan.width, place * size % plan.width
            outs[14][...] = sums[row : row + 1, start : start + size].reshape(size)

    for copy in copies:
        copy.wait()


def shards(
    tokens,
    visible,
    first_gain,
    first_shift,
    joint_weight,
    query_bias,
    value_bias,
    mixer_weight,
    mixer_bias,
    second_gain,
    second_shift,
    expand_weight,
    expand_bias,
    shrink_weight,
    shrink_bias,
    cotangent,
):
    items, slots, width = tokens.shape
    ff = expand_weight.shape[1]
    narrow, wide = lax.axis_size("narrow"), lax.axis_size("wide")
    plan = Plan(narrow, wide, items, slots, width, ff)
    padded, chunk = plan.padded, plan.chunk
    hbm = pl.BlockSpec(memory_space=pl.ANY)
    vmem = pl.BlockSpec(memory_space=pltpu.VMEM)
    smem = pl.BlockSpec(memory_space=pltpu.SMEM)
    inputs = {
        "visible": (visible, smem),
        "g1": (first_gain, vmem),
        "s1": (first_shift, vmem),
        "qb": (query_bias, vmem),
        "vb": (value_bias, vmem),
        "mb": (mixer_bias, vmem),
        "g2": (second_gain, vmem),
        "s2": (second_shift, vmem),
        "sb": (shrink_bias, vmem),
        "eb": (expand_bias, vmem),
        "tok_in": (tokens, hbm),
        "cot_in": (cotangent, hbm),
        "jw_in": (joint_weight, hbm),
        "mw_in": (mixer_weight, hbm),
        "ew_in": (expand_weight, hbm),
        "sw_in": (shrink_weight, hbm),
    }
    block = width // narrow
    outputs = {
        "tok": (tokens.shape, BF16),
        "cot": (tokens.shape, BF16),
        "whole": ((plan.chunks, chunk, width), F32),
        "vector_out": ((plan.vector_rows, width), F32),
    }
    scratch = {
        "jw": pltpu.VMEM(joint_weight.shape, BF16),
        "mw": pltpu.VMEM(mixer_weight.shape, BF16),
        "ew": pltpu.VMEM(expand_weight.shape, BF16),
        "sw": pltpu.VMEM(shrink_weight.shape, BF16),
        "stage": pltpu.VMEM((padded, width), F32),
        "rowb": pltpu.VMEM((padded, width), BF16),
        "qkv": pltpu.VMEM((padded, 3 * width), F32),
        "attend": pltpu.VMEM((items * plan.pairs, 2 * slots, slots), F32),
        "first_t": pltpu.VMEM((width, padded), BF16),
        "mixed_t": pltpu.VMEM((width, padded), BF16),
        "second": pltpu.VMEM((padded, width), BF16),
        "second_t": pltpu.VMEM((width, padded), BF16),
        "middle": pltpu.VMEM((padded, width), F32),
        "wide_rows": pltpu.VMEM((padded, ff), BF16),
        "active_t": pltpu.VMEM((ff, padded), BF16),
        "grad_out": pltpu.VMEM((padded, width), BF16),
        "acc_out": pltpu.VMEM((padded, width), F32),
        "acc_grad": pltpu.VMEM((padded, width), F32),
        "grad_branch": pltpu.VMEM((padded, width), BF16),
        "vec": pltpu.VMEM((plan.vector_rows, width), F32),
        "sums": pltpu.VMEM((plan.vector_rows, width), F32),
        "expand_sums": pltpu.VMEM((plan.ff_jobs, 1, TILE), F32),
        "vector_land": pltpu.VMEM((len(plan.links), plan.vector_rows, width), F32),
        "load_sems": pltpu.SemaphoreType.DMA((6,)),
        "vector_sems": pltpu.SemaphoreType.DMA((2, len(plan.links))),
        "send_sems": pltpu.SemaphoreType.DMA((len(plan.parts), plan.stages, plan.slots_most)),
        "recv_sems": pltpu.SemaphoreType.DMA((len(plan.parts), plan.stages, plan.slots_most)),
    }
    for number, part in enumerate(plan.parts):
        scratch[f"part{number}"] = pltpu.VMEM((2, narrow * chunk, part.columns), F32)
        for stage, move in enumerate(part.sums):
            scratch[f"land{number}_{stage}"] = pltpu.VMEM(
                (part.slots(stage), move.length, part.columns), F32
            )
    results = pl.pallas_call(
        functools.partial(layer_kernel, plan, (*inputs, *outputs, *scratch)),
        out_shape=[pltpu.VMEM(shape, kind) for shape, kind in outputs.values()],
        in_specs=[spec for _, spec in inputs.values()],
        out_specs=[vmem] * len(outputs),
        scratch_shapes=list(scratch.values()),
        compiler_params=pltpu.CompilerParams(
            has_side_effects=True, vmem_limit_bytes=51 * 2**20, collective_id=0
        ),
        name="layer",
    )(*(value for value, _ in inputs.values()))
    row_counts = [count // windows for _, count, _, windows in plan.phases]
    shapes = [jax.ShapeDtypeStruct(tokens.shape, BF16)] * 2
    shapes += [
        jax.ShapeDtypeStruct((tall, chunk, windows * width), F32)
        for tall, (_, _, _, windows) in zip(row_counts, plan.phases)
    ]
    shapes += [jax.ShapeDtypeStruct((block,), F32)] * 8
    shapes += [jax.ShapeDtypeStruct((ff // narrow,), F32)]
    copies = 2 + sum(windows for _, _, _, windows in plan.phases)
    outs = pl.pallas_call(
        functools.partial(write_kernel, plan),
        out_shape=shapes,
        in_specs=[vmem] * len(results),
        out_specs=[hbm] * 6 + [vmem] * 9,
        scratch_shapes=[pltpu.SemaphoreType.DMA((copies,))],
        compiler_params=pltpu.CompilerParams(vmem_limit_bytes=4 * 2**20),
        name="write",
    )(*(pltpu.with_memory_space_constraint(value, pltpu.VMEM) for value in results))
    input_grad, layer_out = outs[:2]
    shrink, expand, mixer, joint = (
        out.reshape(-1, out.shape[-1]) for out in outs[2:6]
    )
    vectors = outs[6:]
    return (
        layer_out,
        input_grad,
        vectors[0],
        vectors[1],
        joint,
        vectors[2],
        vectors[3],
        mixer,
        vectors[4],
        vectors[5],
        vectors[6],
        expand,
        vectors[8],
        shrink,
        vectors[7],
    )


def solution(mesh):
    return jax.shard_map(
        shards,
        mesh=mesh,
        in_specs=(
            P(("wide", "narrow"), None, None),
            P(("wide", "narrow")),
            P(),
            P(),
            P(),
            P(),
            P(),
            P(),
            P(),
            P(),
            P(),
            P(),
            P(),
            P(),
            P(),
            P(("wide", "narrow"), None, None),
        ),
        out_specs=(
            P(("wide", "narrow"), None, None),
            P(("wide", "narrow"), None, None),
            P("narrow"),
            P("narrow"),
            P("narrow", None),
            P("narrow"),
            P("narrow"),
            P("narrow", None),
            P("narrow"),
            P("narrow"),
            P("narrow"),
            P("narrow", None),
            P("narrow"),
            P("narrow", None),
            P("narrow"),
        ),
        check_vma=False,
    )
```

```python
import functools
import types

import jax
import jax.numpy as jnp
from jax import lax
from jax.experimental import pallas as pl
from jax.experimental.pallas import tpu as pltpu
from jax.sharding import PartitionSpec as P

HEAD_DIM = 64
EPSILON = 1e-06
SUB = 8
LAGS = ([1, 2, 2, 2, 2, 2, 2, 2], [1, 2, 2, 2, 2, 2, 2, 2])
MOST = 32
TILE = 256
MESH = pl.DeviceIdType.MESH
ROOT_HALF = 0.5**0.5
PEAK = 0.3989422804014327
BF16 = jnp.bfloat16
F32 = jnp.float32


def bit_of(index, place):
    return lax.rem(lax.div(index, 2**place), 2)


def reversed_bits(value, count):
    out = 0
    for place in range(count):
        out = out * 2 + (value >> place) % 2
    return out


def aligned(start, size, unit):
    return pl.ds(pl.multiple_of(start, unit), size)


def matmul(left, right, contract=((1,), (0,))):
    return lax.dot_general(left, right, (contract, ((), ())), preferred_element_type=F32)


class Move:
    def __init__(self, kind, flips, length, select=None, inner=False):
        self.kind, self.flips, self.length = kind, flips, length
        self.select, self.inner = select, inner


class Part:
    def __init__(self, column, columns, picks, sums, gathers, selects):
        self.column, self.columns, self.picks = column, columns, picks
        self.sums, self.moves = sums, sums + gathers
        self.selects = selects
        self.lags = LAGS[column > 0] if len(self.moves) == 8 else [1] + [2] * (len(self.moves) - 1)
        self.due = [sum(self.lags[: stage + 1]) for stage in range(len(self.moves))]

    def slots(self, stage):
        after = self.lags[stage + 1] if stage + 1 < len(self.sums) else 0
        count = 2 * self.lags[stage] + after + 2
        if self.moves[stage].kind in ("fold", "unfold"):
            kinds = [move.kind for move in self.moves]
            ahead = self.due[kinds.index("unfold")] - self.due[kinds.index("fold") - 1]
            count = max(count, ahead + 2)
        return count


class Plan:
    def __init__(self, narrow, wide, items, slots, width, ff):
        self.narrow, self.wide, self.width, self.ff = narrow, wide, width, ff
        self.items, self.slots = items, slots
        self.rows = items * slots
        self.padded = self.rows + -self.rows % 256
        self.pairs = width // (2 * HEAD_DIM)
        narrow_bits = self.narrow_bits = narrow.bit_length() - 1
        wide_bits = self.wide_bits = wide.bit_length() - 1
        rows = width // narrow
        chunk = SUB
        while rows % (2 * chunk) == 0 and chunk < MOST:
            chunk *= 2
        self.chunk = chunk
        near, mirror = (("wide", 1),), (("wide", 1), ("wide", 2))
        x, y, core = (("wide", 0),), (("narrow", 1),), (("narrow", 0),)
        if (narrow, wide) == (4, 8):
            self.links = (core, y, x, near, mirror)
            half, quarter = chunk // 2, chunk // 4
            z_bit, x_bit, y_bit, core_bit = ("wide", 2), x[0], y[0], core[0]
            one = Part(
                0,
                width // 3 * 2,
                [(spot % 2 * 2 + spot // 2, 0, chunk) for spot in range(4)],
                [
                    Move("halve", core, 2 * chunk, core_bit),
                    Move("halve", y, chunk, y_bit),
                    Move("fold", near, chunk),
                    Move("halve", mirror, half, z_bit, True),
                    Move("halve", x, quarter, x_bit, True),
                ],
                [
                    Move("double", x, quarter, inner=True),
                    Move("double", mirror, half, inner=True),
                    Move("unfold", near, chunk),
                ],
                [(z_bit, half), (x_bit, quarter)],
            )
            two = Part(
                width // 3 * 2,
                width // 3,
                [
                    (2 * (spot % 2) + spot // 4, spot // 2 % 2 * half, half)
                    for spot in range(8)
                ],
                [
                    Move("halve", core, 2 * chunk, core_bit),
                    Move("halve", x, chunk, x_bit),
                    Move("halve", y, half, y_bit),
                    Move("fold", near, half),
                    Move("halve", mirror, quarter, z_bit, True),
                ],
                [
                    Move("double", mirror, quarter, inner=True),
                    Move("unfold", near, half),
                    Move("double", x, half),
                ],
                [(x_bit, half), (z_bit, quarter)],
            )
            self.parts = (one, two)
        else:
            self.links = tuple((("narrow", place),) for place in range(narrow_bits))
            self.links += tuple((("wide", place),) for place in range(wide_bits))
            sums, gathers, selects = [], [], []
            length = narrow * chunk
            for (axis, place), in self.links:
                if length > SUB:
                    length //= 2
                    sums.append(Move("halve", ((axis, place),), length, (axis, place)))
                    if axis == "wide":
                        selects.append(((axis, place), length))
                        gathers.insert(0, Move("double", ((axis, place),), length))
                else:
                    sums.append(Move("add", ((axis, place),), length))
            picks = [(reversed_bits(spot, narrow_bits), 0, chunk) for spot in range(narrow)]
            self.parts = (Part(0, width, picks, sums, gathers, selects),)
        self.stages = max(len(part.moves) for part in self.parts)
        self.depth = max(part.due[-1] for part in self.parts)
        self.slots_most = max(
            part.slots(stage) for part in self.parts for stage in range(len(part.moves))
        )
        self.phases = []
        start = 0
        for rows_block, windows in (
            (ff // narrow, 1),
            (rows, ff // width),
            (rows, 1),
            (rows, 3),
        ):
            count = rows_block // chunk * windows
            self.phases.append((start, count, rows_block, windows))
            start += count
        self.chunks = start
        self.ff_tiles = ff // TILE
        self.split = self.phases[1][0] // self.ff_tiles
        assert self.split >= 1
        tall = ff // narrow
        self.groups = tall // TILE if tall % TILE == 0 else 1
        self.blocks = self.ff_tiles // self.groups
        self.jobs = {}
        tick = 0
        for name, count in (
            ("ff", self.ff_tiles * self.split),
            ("norm", self.split),
            ("mix", 1),
            ("item", items * self.split),
            ("pack", 1),
            ("first", self.split),
            ("input", self.split),
        ):
            self.jobs[name] = (tick, count)
            tick += count
        self.vector_tick = tick
        assert self.phases[2][0] >= self.jobs["item"][0]
        assert self.phases[3][0] >= self.jobs["first"][0]
        self.vector_rows = 8 + ff // width
        self.vector_rows += -self.vector_rows % SUB
        self.ticks = self.chunks + self.depth
        self.vector_every = (self.ticks - 1 - self.vector_tick) // len(self.links)
        assert self.vector_every > 0


def layer_kernel(plan, names, *refs):
    r = types.SimpleNamespace(**dict(zip(names, refs)))
    width, chunk, narrow, slots = plan.width, plan.chunk, plan.narrow, plan.slots
    rows, padded, pairs = plan.rows, plan.padded, plan.pairs
    score_scale = HEAD_DIM ** (-0.5)
    spots = {"narrow": lax.axis_index("narrow"), "wide": lax.axis_index("wide")}
    inner = bit_of(spots["wide"], 1) != bit_of(spots["wide"], 2)
    outer = bit_of(spots["wide"], 1) == bit_of(spots["wide"], 2)

    bits = {
        (axis, place): bit_of(spots[axis], place)
        for axis, count in (("narrow", plan.narrow_bits), ("wide", plan.wide_bits))
        for place in range(count)
    }
    partners = {}
    for flips in plan.links:
        there = dict(spots)
        for axis, place in flips:
            there[axis] = there[axis] + (1 - 2 * bits[axis, place]) * 2**place
        partners[flips] = there

    loads = {}
    for number, name in enumerate(("tok", "jw", "mw", "ew", "cot", "sw")):
        loads[name] = pltpu.make_async_copy(
            getattr(r, name + "_in"), getattr(r, name), r.load_sems.at[number]
        )
    loads["tok"].start()
    loads["jw"].start()

    barrier = pltpu.get_barrier_semaphore()
    for flips in plan.links:
        pl.semaphore_signal(barrier, inc=1, device_id=partners[flips], device_id_type=MESH)

    def vector(row):
        return r.vec[row : row + 1, :]

    def item_rows(item):
        return aligned(item * slots, slots, SUB)

    def row_live(item):
        return lax.broadcasted_iota(jnp.int32, (slots, 1), 0) < r.visible[item]

    lanes = lax.broadcasted_iota(jnp.int32, (slots, 2 * HEAD_DIM), 1)
    first_head = lanes < HEAD_DIM

    def both_heads(value):
        zero = jnp.zeros_like(value)
        return jnp.concatenate(
            [jnp.where(first_head, value, zero), jnp.where(first_head, zero, value)], axis=0
        ).astype(BF16)

    def one_head_each(value):
        return jnp.where(first_head, value[:slots], value[slots:])

    def normalized(values):
        center = values - jnp.mean(values, axis=-1, keepdims=True)
        spread = lax.rsqrt(jnp.mean(center * center, axis=-1, keepdims=True) + EPSILON)
        return center * spread, spread

    def norm_backward(grad, unit, spread):
        return spread * (
            grad
            - jnp.mean(grad, axis=-1, keepdims=True)
            - unit * jnp.mean(grad * unit, axis=-1, keepdims=True)
        )

    def each_item(body):
        lax.fori_loop(0, plan.items, lambda item, carry: (body(item), carry)[1], 0)

    def each_tile(count, body):
        lax.fori_loop(0, count, lambda tile, carry: (body(tile), carry)[1], 0)

    def pair_lanes(part, pair):
        start = part * width + pair * 2 * HEAD_DIM
        return slice(start, start + 2 * HEAD_DIM)

    small = (r.g1, r.s1, r.qb, r.vb, r.mb, r.g2, r.s2, r.sb)
    for row, ref in enumerate(small):
        r.vec[row : row + 1, :] = ref[...].astype(F32).reshape(1, width)
    for row in range(plan.ff // width):
        value = r.eb[row * width : (row + 1) * width].astype(F32)
        r.vec[8 + row : 9 + row, :] = value.reshape(1, width)
    r.stage[rows:, :] = jnp.zeros((padded - rows, width), F32)
    r.sums[...] = jnp.zeros_like(r.sums)
    r.expand_sums[...] = jnp.zeros_like(r.expand_sums)
    loads["tok"].wait()

    def first_norm(item):
        unit, _ = normalized(r.tok[item].astype(F32))
        r.stage[item_rows(item), :] = unit * vector(0) + vector(1)

    each_item(first_norm)
    for name in ("mw", "ew", "cot", "sw"):
        loads[name].start()
    r.rowb[...] = r.stage[...].astype(BF16)
    loads["jw"].wait()
    for part, bias in enumerate((2, None, 3)):

        def joint_tile(tile):
            cols = aligned(part * width + tile * TILE, TILE, TILE)
            value = matmul(r.rowb[...], r.jw[:, cols])
            if bias is not None:
                value = value + r.vec[bias : bias + 1, aligned(tile * TILE, TILE, TILE)]
            r.qkv[:, cols] = value.astype(BF16).astype(F32)

        each_tile(width // TILE, joint_tile)
    r.first_t[...] = r.stage[...].T.astype(BF16)
    r.qkv[rows:, :] = jnp.zeros((padded - rows, 3 * width), F32)

    def attend_item(item):
        here = item_rows(item)
        key_live = (
            lax.broadcasted_iota(jnp.int32, (2 * slots, slots), 1) < r.visible[item]
        )
        for pair in range(pairs):
            query = both_heads(r.qkv[here, pair_lanes(0, pair)])
            keys = r.qkv[here, pair_lanes(1, pair)].astype(BF16)
            values = r.qkv[here, pair_lanes(2, pair)].astype(BF16)
            logits = matmul(query, keys, ((1,), (1,))) * score_scale
            logits = jnp.where(key_live, logits, -1000000000.0)
            expo = jnp.exp(logits - jnp.max(logits, axis=-1, keepdims=True))
            attend = expo * (1.0 / jnp.sum(expo, axis=-1, keepdims=True))
            r.attend[item * pairs + pair] = attend
            mixed = one_head_each(matmul(attend.astype(BF16), values))
            r.stage[here, pair_lanes(0, pair)] = mixed

    each_item(attend_item)
    r.rowb[...] = r.stage[...].astype(BF16)
    loads["mw"].wait()

    def mixer_tile(tile):
        cols = aligned(tile * TILE, TILE, TILE)
        r.middle[:, cols] = matmul(r.rowb[...], r.mw[:, cols]) + r.vec[4:5, cols]

    each_tile(width // TILE, mixer_tile)
    r.mixed_t[...] = r.stage[...].T.astype(BF16)

    def second_norm(item):
        here = item_rows(item)
        middle = r.middle[here, :] + r.tok[item].astype(F32)
        r.middle[here, :] = middle
        unit, _ = normalized(middle)
        r.stage[here, :] = unit * vector(5) + vector(6)

    each_item(second_norm)
    r.second[...] = r.stage[...].astype(BF16)
    loads["ew"].wait()

    def expand_bias(tile):
        per_row = width // TILE
        return r.vec[
            pl.ds(8 + lax.div(tile, per_row), 1),
            aligned(lax.rem(tile, per_row) * TILE, TILE, TILE),
        ]

    every_row = slice(0, padded)

    def hidden_tile(tile, some):
        cols = aligned(tile * TILE, TILE, TILE)
        hidden = matmul(r.second[some, :], r.ew[:, cols]) + expand_bias(tile)
        return hidden, 0.5 + 0.5 * lax.erf(hidden * ROOT_HALF)

    def activate(tile, some, hidden, normal):
        cols = aligned(tile * TILE, TILE, TILE)
        active = hidden * normal
        r.wide_rows[some, cols] = active.astype(BF16)
        r.active_t[cols, some] = active.T.astype(BF16)

    def expand_tile(place):
        tile = place * plan.groups
        activate(tile, every_row, *hidden_tile(tile, every_row))

    each_tile(plan.blocks, expand_tile)
    r.second_t[...] = r.stage[...].T.astype(BF16)
    loads["cot"].wait()

    def mask_cotangent(item):
        grad = r.cot[item].astype(F32)
        r.stage[item_rows(item), :] = jnp.where(row_live(item), grad, 0.0)

    each_item(mask_cotangent)
    r.grad_out[...] = r.stage[...].astype(BF16)
    loads["sw"].wait()

    rows_full = rows // 16 * 16

    def share(count, turn, body):
        size = -(-count // plan.split)
        first = turn * size
        last = jnp.minimum(first + size, count)
        lax.fori_loop(first, last, lambda place, carry: (body(place), carry)[1], 0)

    def ff_job(turn):
        step_number, half = lax.div(turn, plan.split), lax.rem(turn, plan.split)
        group = lax.rem(lax.div(step_number, plan.blocks) + 1, plan.groups)
        tile = lax.rem(step_number, plan.blocks) * plan.groups + group
        size = padded // plan.split
        some = aligned(half * size, size, size)
        cols = aligned(tile * TILE, TILE, TILE)
        hidden, normal = hidden_tile(tile, some)

        @pl.when(step_number < plan.ff_tiles - plan.blocks)
        def _():
            activate(tile, some, hidden, normal)

        grad = matmul(r.grad_out[some, :], r.sw[cols, :], ((1,), (1,)))
        slope = normal + hidden * (PEAK * jnp.exp(-0.5 * hidden * hidden))
        grad_hidden = (grad * slope).astype(BF16)
        output = matmul(r.wide_rows[some, cols], r.sw[cols, :])
        r.wide_rows[some, cols] = grad_hidden
        r.expand_sums[tile] += jnp.sum(grad_hidden.astype(F32), axis=0, keepdims=True)
        grad_second = matmul(grad_hidden, r.ew[:, cols], ((1,), (1,)))

        @pl.when(step_number == 0)
        def _():
            r.acc_out[some, :] = output
            r.acc_grad[some, :] = grad_second

        @pl.when(step_number > 0)
        def _():
            r.acc_out[some, :] += output
            r.acc_grad[some, :] += grad_second

    def norm_job(turn):
        def one(item):
            here = item_rows(item)
            live = row_live(item)
            middle = r.middle[here, :]
            grad_out = jnp.where(live, r.cot[item].astype(F32), 0.0)
            layer_out = jnp.where(live, middle + (r.acc_out[here, :] + vector(7)), 0.0)
            r.cot[item] = layer_out.astype(BF16)
            unit, spread = normalized(middle)
            grad = r.acc_grad[here, :]
            r.sums[5:6, :] += jnp.sum(grad * unit, axis=0, keepdims=True)
            r.sums[6:7, :] += jnp.sum(grad, axis=0, keepdims=True)
            r.sums[7:8, :] += jnp.sum(grad_out, axis=0, keepdims=True)
            grad_middle = grad_out + norm_backward(grad * vector(5), unit, spread)
            r.acc_out[here, :] = grad_middle
            r.sums[4:5, :] += jnp.sum(
                grad_middle.astype(BF16).astype(F32), axis=0, keepdims=True
            )

        share(plan.items, turn, one)

    def mix_job(turn):
        r.grad_branch[:rows_full, :] = r.acc_out[:rows_full, :].astype(BF16)
        tail = jnp.concatenate(
            [r.acc_out[rows_full:rows, :], jnp.zeros((padded - rows, width), F32)], axis=0
        )
        r.grad_branch[rows_full:, :] = tail.astype(BF16)

        def one(tile):
            cols = aligned(tile * TILE, TILE, TILE)
            value = matmul(r.grad_branch[...], r.mw[cols, :], ((1,), (1,)))
            r.stage[:, cols] = value.astype(BF16).astype(F32)

        each_tile(width // TILE, one)

    def item_job(turn):
        item, half = lax.div(turn, plan.split), lax.rem(turn, plan.split)
        here = item_rows(item)
        size = pairs // plan.split

        def lanes_of(part, pair):
            start = part * width + (half * size + pair) * 2 * HEAD_DIM
            return aligned(start, 2 * HEAD_DIM, 2 * HEAD_DIM)

        for pair in range(size):
            query = both_heads(r.qkv[here, lanes_of(0, pair)])
            keys = r.qkv[here, lanes_of(1, pair)].astype(BF16)
            values = r.qkv[here, lanes_of(2, pair)].astype(BF16)
            grad_mixed = both_heads(r.stage[here, lanes_of(0, pair)])
            attend = r.attend[item * pairs + half * size + pair]
            grad_attend = matmul(grad_mixed, values, ((1,), (1,)))
            grad_value = matmul(attend.astype(BF16), grad_mixed, ((0,), (0,)))
            inner_sum = jnp.sum(attend * grad_attend, axis=-1, keepdims=True)
            grad_logits = (attend * (grad_attend - inner_sum)).astype(BF16)
            grad_query = one_head_each(matmul(grad_logits, keys)) * score_scale
            grad_key = matmul(grad_logits, query, ((0,), (0,))) * score_scale
            r.qkv[here, lanes_of(0, pair)] = grad_query
            r.qkv[here, lanes_of(1, pair)] = grad_key
            r.qkv[here, lanes_of(2, pair)] = grad_value

    def joint_rows(part):
        return slice(part * padded, (part + 1) * padded)

    def pack_job(turn):
        for part in range(3):
            value = r.qkv[:, part * width : (part + 1) * width].astype(BF16)
            r.sw[joint_rows(part), :] = value
            if part != 1:
                row = 2 if part == 0 else 3
                r.sums[row : row + 1, :] = jnp.sum(value.astype(F32), axis=0, keepdims=True)

    def first_job(turn):
        def one(tile):
            cols = aligned(tile * TILE, TILE, TILE)
            total = None
            for part in range(3):
                value = matmul(
                    r.sw[joint_rows(part), :],
                    r.jw[cols, part * width : (part + 1) * width],
                    ((1,), (1,)),
                )
                total = value if total is None else total + value
            r.acc_grad[:, cols] = total

        share(width // TILE, turn, one)

    def input_job(turn):
        def one(item):
            here = item_rows(item)
            unit, spread = normalized(r.tok[item].astype(F32))
            grad = r.acc_grad[here, :]
            r.sums[0:1, :] += jnp.sum(grad * unit, axis=0, keepdims=True)
            r.sums[1:2, :] += jnp.sum(grad, axis=0, keepdims=True)
            total = r.acc_out[here, :] + norm_backward(grad * vector(0), unit, spread)
            r.tok[item] = total.astype(BF16)

        share(plan.items, turn, one)

        @pl.when(turn == 0)
        def _():
            per_row = width // TILE
            for tile in range(plan.ff_tiles):
                row, start = 8 + tile // per_row, tile % per_row * TILE
                r.sums[row : row + 1, start : start + TILE] = r.expand_sums[tile]

    def when(condition, action):
        if condition is True:
            action()
        else:
            pl.when(condition)(action)

    def roles(move):
        if move.kind == "fold":
            return outer, inner
        if move.kind == "unfold":
            return inner, outer
        return (inner, inner) if move.inner else (True, True)

    def land(number, stage, item):
        ref = getattr(r, f"land{number}_{stage}")
        return ref.at[lax.rem(item, plan.parts[number].slots(stage))]

    def source(number, stage, item):
        if stage == 0:
            return getattr(r, f"part{number}").at[lax.rem(item, 2)]
        return land(number, stage - 1, item)

    kept, given, regions = {}, {}, {}
    for number, part in enumerate(plan.parts):
        for stage, move in enumerate(part.moves):
            bit = bits[move.select] if move.select else 0
            kept[number, stage] = bit * move.length
            given[number, stage] = (1 - bit) * move.length if move.select else 0
            regions[number, stage] = sum(
                bits[select] * size for select, size in part.selects if size >= move.length
            )

    def in_whole(number, stage, item):
        part = plan.parts[number]
        return (
            item,
            aligned(regions[number, stage], part.moves[stage].length, SUB),
            pl.ds(part.column, part.columns),
        )

    def transfer(number, stage, item):
        part = plan.parts[number]
        move = part.moves[stage]
        slot = lax.rem(item, part.slots(stage))
        if stage < len(part.sums):
            src = source(number, stage, item).at[
                aligned(given[number, stage], move.length, SUB)
            ]
            dst = land(number, stage, item)
        else:
            src = r.whole.at[in_whole(number, stage, item)]
            dst = src
        return pltpu.make_async_remote_copy(
            src_ref=src,
            dst_ref=dst,
            send_sem=r.send_sems.at[number, stage, slot],
            recv_sem=r.recv_sems.at[number, stage, slot],
            device_id=partners[move.flips],
            device_id_type=MESH,
        )

    def begin(number, stage, item):
        sender, _ = roles(plan.parts[number].moves[stage])
        when(sender, lambda: transfer(number, stage, item).start())

    def settle(number, stage, item):
        part = plan.parts[number]
        move = part.moves[stage]
        sender, receiver = roles(move)

        def receive():
            if stage < len(part.sums):
                land(number, stage, item)[...] += source(number, stage, item)[
                    aligned(kept[number, stage], move.length, SUB)
                ]
            if stage == len(part.sums) - 1:
                r.whole[in_whole(number, stage, item)] = land(number, stage, item)[...]

        if move.kind in ("fold", "unfold"):
            when(sender, lambda: transfer(number, stage, item).wait_send())

            def arrive():
                transfer(number, stage, item).wait_recv()
                receive()

        else:

            def arrive():
                transfer(number, stage, item).wait()
                receive()

        when(receiver, arrive)
        if stage + 1 < len(part.moves):
            begin(number, stage + 1, item)

    def rows_of(phase):
        _, count, _, windows = plan.phases[phase]
        return count // windows

    def produce(item):
        slot = lax.rem(item, 2)
        lefts = (r.active_t, r.second_t, r.mixed_t, r.first_t)
        rights = (r.grad_out, r.wide_rows, r.grad_branch, r.sw)
        for phase, (start, count, rows_block, windows) in enumerate(plan.phases):
            left, right = lefts[phase], rights[phase]

            @pl.when((item >= start) & (item < start + count))
            def _():
                local = item - start
                tall = rows_of(phase)
                row = lax.rem(local, tall) * chunk
                window = lax.div(local, tall)
                for number, part in enumerate(plan.parts):
                    picked = [
                        left[aligned(block * rows_block + row + offset, size, size), :]
                        for block, offset, size in part.picks
                    ]
                    if phase == 3:
                        other = right[
                            aligned(window * padded, padded, 256),
                            part.column : part.column + part.columns,
                        ]
                    else:
                        other = right[
                            :, aligned(window * width + part.column, part.columns, 128)
                        ]
                    getattr(r, f"part{number}")[slot] = matmul(
                        jnp.concatenate(picked, axis=0), other
                    )

    def vector_exchange(stage):
        return pltpu.make_async_remote_copy(
            src_ref=r.sums if stage == 0 else r.vector_land.at[stage - 1],
            dst_ref=r.vector_land.at[stage],
            send_sem=r.vector_sems.at[0, stage],
            recv_sem=r.vector_sems.at[1, stage],
            device_id=partners[plan.links[stage]],
            device_id_type=MESH,
        )

    def vector_step(tick):
        count = len(plan.links)
        for stage in range(count + 1):

            @pl.when(tick == plan.vector_tick + stage * plan.vector_every)
            def _():
                if stage > 0:
                    vector_exchange(stage - 1).wait()
                    before = r.sums if stage == 1 else r.vector_land.at[stage - 2]
                    r.vector_land[stage - 1] += before[...]
                if stage < count:
                    vector_exchange(stage).start()

    pl.semaphore_wait(barrier, len(plan.links))

    def step(tick, carry):
        @pl.when(tick < plan.chunks)
        def _():
            produce(tick)
            for number in range(len(plan.parts)):
                begin(number, 0, tick)

        for stage in range(plan.stages):
            for number, part in enumerate(plan.parts):
                if stage < len(part.moves):
                    item = tick - part.due[stage]

                    @pl.when((item >= 0) & (item < plan.chunks))
                    def _():
                        settle(number, stage, item)

        vector_step(tick)
        run = {
            "ff": ff_job,
            "norm": norm_job,
            "mix": mix_job,
            "item": item_job,
            "pack": pack_job,
            "first": first_job,
            "input": input_job,
        }
        for name, (start, count) in plan.jobs.items():
            job = functools.partial(run[name], tick - start)
            pl.when((tick >= start) & (tick < start + count))(job)

        return carry

    lax.fori_loop(0, plan.ticks, step, 0)
    r.vector_out[...] = r.vector_land[len(plan.links) - 1]


def write_kernel(plan, tok, cot, whole, sums, *refs):
    outs, sems = refs[:-1], refs[-1]
    copies = [(tok, outs[0]), (cot, outs[1])]
    for (start, count, _, windows), out in zip(plan.phases, outs[2:6]):
        tall = count // windows
        for window in range(windows):
            first = start + window * tall
            cols = pl.ds(window * plan.width, plan.width)
            copies.append((whole.at[first : first + tall], out.at[:, :, cols]))
    copies = [
        pltpu.make_async_copy(source, target, sems.at[number])
        for number, (source, target) in enumerate(copies)
    ]
    for copy in copies:
        copy.start()
    own = lax.axis_index("narrow")
    for place in range(plan.narrow):

        @pl.when(own == place)
        def _():
            for row, out in enumerate(outs[6:14]):
                size = out.shape[0]
                out[...] = sums[row : row + 1, place * size : (place + 1) * size].reshape(size)
            size = outs[14].shape[0]
            row, start = 8 + place * size // plan.width, place * size % plan.width
            outs[14][...] = sums[row : row + 1, start : start + size].reshape(size)

    for copy in copies:
        copy.wait()


def shards(
    tokens,
    visible,
    first_gain,
    first_shift,
    joint_weight,
    query_bias,
    value_bias,
    mixer_weight,
    mixer_bias,
    second_gain,
    second_shift,
    expand_weight,
    expand_bias,
    shrink_weight,
    shrink_bias,
    cotangent,
):
    items, slots, width = tokens.shape
    ff = expand_weight.shape[1]
    narrow, wide = lax.axis_size("narrow"), lax.axis_size("wide")
    plan = Plan(narrow, wide, items, slots, width, ff)
    padded, chunk = plan.padded, plan.chunk
    hbm = pl.BlockSpec(memory_space=pl.ANY)
    vmem = pl.BlockSpec(memory_space=pltpu.VMEM)
    smem = pl.BlockSpec(memory_space=pltpu.SMEM)
    inputs = {
        "visible": (visible, smem),
        "g1": (first_gain, vmem),
        "s1": (first_shift, vmem),
        "qb": (query_bias, vmem),
        "vb": (value_bias, vmem),
        "mb": (mixer_bias, vmem),
        "g2": (second_gain, vmem),
        "s2": (second_shift, vmem),
        "sb": (shrink_bias, vmem),
        "eb": (expand_bias, vmem),
        "tok_in": (tokens, hbm),
        "cot_in": (cotangent, hbm),
        "jw_in": (joint_weight, hbm),
        "mw_in": (mixer_weight, hbm),
        "ew_in": (expand_weight, hbm),
        "sw_in": (shrink_weight, hbm),
    }
    block = width // narrow
    outputs = {
        "tok": (tokens.shape, BF16),
        "cot": (tokens.shape, BF16),
        "whole": ((plan.chunks, chunk, width), F32),
        "vector_out": ((plan.vector_rows, width), F32),
    }
    scratch = {
        "jw": pltpu.VMEM(joint_weight.shape, BF16),
        "mw": pltpu.VMEM(mixer_weight.shape, BF16),
        "ew": pltpu.VMEM(expand_weight.shape, BF16),
        "sw": pltpu.VMEM(shrink_weight.shape, BF16),
        "stage": pltpu.VMEM((padded, width), F32),
        "rowb": pltpu.VMEM((padded, width), BF16),
        "qkv": pltpu.VMEM((padded, 3 * width), F32),
        "attend": pltpu.VMEM((items * plan.pairs, 2 * slots, slots), F32),
        "first_t": pltpu.VMEM((width, padded), BF16),
        "mixed_t": pltpu.VMEM((width, padded), BF16),
        "second": pltpu.VMEM((padded, width), BF16),
        "second_t": pltpu.VMEM((width, padded), BF16),
        "middle": pltpu.VMEM((padded, width), F32),
        "wide_rows": pltpu.VMEM((padded, ff), BF16),
        "active_t": pltpu.VMEM((ff, padded), BF16),
        "grad_out": pltpu.VMEM((padded, width), BF16),
        "acc_out": pltpu.VMEM((padded, width), F32),
        "acc_grad": pltpu.VMEM((padded, width), F32),
        "grad_branch": pltpu.VMEM((padded, width), BF16),
        "vec": pltpu.VMEM((plan.vector_rows, width), F32),
        "sums": pltpu.VMEM((plan.vector_rows, width), F32),
        "expand_sums": pltpu.VMEM((plan.ff_tiles, 1, TILE), F32),
        "vector_land": pltpu.VMEM((len(plan.links), plan.vector_rows, width), F32),
        "load_sems": pltpu.SemaphoreType.DMA((6,)),
        "vector_sems": pltpu.SemaphoreType.DMA((2, len(plan.links))),
        "send_sems": pltpu.SemaphoreType.DMA((len(plan.parts), plan.stages, plan.slots_most)),
        "recv_sems": pltpu.SemaphoreType.DMA((len(plan.parts), plan.stages, plan.slots_most)),
    }
    for number, part in enumerate(plan.parts):
        scratch[f"part{number}"] = pltpu.VMEM((2, narrow * chunk, part.columns), F32)
        for stage, move in enumerate(part.sums):
            scratch[f"land{number}_{stage}"] = pltpu.VMEM(
                (part.slots(stage), move.length, part.columns), F32
            )
    results = pl.pallas_call(
        functools.partial(layer_kernel, plan, (*inputs, *outputs, *scratch)),
        out_shape=[pltpu.VMEM(shape, kind) for shape, kind in outputs.values()],
        in_specs=[spec for _, spec in inputs.values()],
        out_specs=[vmem] * len(outputs),
        scratch_shapes=list(scratch.values()),
        compiler_params=pltpu.CompilerParams(
            has_side_effects=True, vmem_limit_bytes=51 * 2**20, collective_id=0
        ),
        name="layer",
    )(*(value for value, _ in inputs.values()))
    row_counts = [count // windows for _, count, _, windows in plan.phases]
    shapes = [jax.ShapeDtypeStruct(tokens.shape, BF16)] * 2
    shapes += [
        jax.ShapeDtypeStruct((tall, chunk, windows * width), F32)
        for tall, (_, _, _, windows) in zip(row_counts, plan.phases)
    ]
    shapes += [jax.ShapeDtypeStruct((block,), F32)] * 8
    shapes += [jax.ShapeDtypeStruct((ff // narrow,), F32)]
    copies = 2 + sum(windows for _, _, _, windows in plan.phases)
    outs = pl.pallas_call(
        functools.partial(write_kernel, plan),
        out_shape=shapes,
        in_specs=[vmem] * len(results),
        out_specs=[hbm] * 6 + [vmem] * 9,
        scratch_shapes=[pltpu.SemaphoreType.DMA((copies,))],
        compiler_params=pltpu.CompilerParams(vmem_limit_bytes=4 * 2**20),
        name="write",
    )(*(pltpu.with_memory_space_constraint(value, pltpu.VMEM) for value in results))
    input_grad, layer_out = outs[:2]
    shrink, expand, mixer, joint = (
        out.reshape(-1, out.shape[-1]) for out in outs[2:6]
    )
    vectors = outs[6:]
    return (
        layer_out,
        input_grad,
        vectors[0],
        vectors[1],
        joint,
        vectors[2],
        vectors[3],
        mixer,
        vectors[4],
        vectors[5],
        vectors[6],
        expand,
        vectors[8],
        shrink,
        vectors[7],
    )


def solution(mesh):
    return jax.shard_map(
        shards,
        mesh=mesh,
        in_specs=(
            P(("wide", "narrow"), None, None),
            P(("wide", "narrow")),
            P(),
            P(),
            P(),
            P(),
            P(),
            P(),
            P(),
            P(),
            P(),
            P(),
            P(),
            P(),
            P(),
            P(("wide", "narrow"), None, None),
        ),
        out_specs=(
            P(("wide", "narrow"), None, None),
            P(("wide", "narrow"), None, None),
            P("narrow"),
            P("narrow"),
            P("narrow", None),
            P("narrow"),
            P("narrow"),
            P("narrow", None),
            P("narrow"),
            P("narrow"),
            P("narrow"),
            P("narrow", None),
            P("narrow"),
            P("narrow", None),
            P("narrow"),
        ),
        check_vma=False,
    )
```

```python
import functools
import types

import jax
import jax.numpy as jnp
from jax import lax
from jax.experimental import pallas as pl
from jax.experimental.pallas import tpu as pltpu
from jax.sharding import PartitionSpec as P

HEAD_DIM = 64
EPSILON = 1e-06
SUB = 8
LAGS = ([1, 2, 2, 2, 2, 2, 2, 2], [1, 2, 2, 2, 2, 2, 2, 2])
MOST = 32
TILE = 256
MESH = pl.DeviceIdType.MESH
ROOT_HALF = 0.5**0.5
PEAK = 0.3989422804014327
BF16 = jnp.bfloat16
F32 = jnp.float32


def bit_of(index, place):
    return lax.rem(lax.div(index, 2**place), 2)


def reversed_bits(value, count):
    out = 0
    for place in range(count):
        out = out * 2 + (value >> place) % 2
    return out


def aligned(start, size, unit):
    return pl.ds(pl.multiple_of(start, unit), size)


def matmul(left, right, contract=((1,), (0,))):
    return lax.dot_general(left, right, (contract, ((), ())), preferred_element_type=F32)


class Move:
    def __init__(self, kind, flips, length, select=None, inner=False):
        self.kind, self.flips, self.length = kind, flips, length
        self.select, self.inner = select, inner


class Part:
    def __init__(self, column, columns, picks, sums, gathers, selects):
        self.column, self.columns, self.picks = column, columns, picks
        self.sums, self.moves = sums, sums + gathers
        self.selects = selects
        self.lags = LAGS[column > 0] if len(self.moves) == 8 else [1] + [2] * (len(self.moves) - 1)
        self.due = [sum(self.lags[: stage + 1]) for stage in range(len(self.moves))]

    def slots(self, stage):
        after = self.lags[stage + 1] if stage + 1 < len(self.sums) else 0
        count = 2 * self.lags[stage] + after + 2
        if self.moves[stage].kind in ("fold", "unfold"):
            kinds = [move.kind for move in self.moves]
            ahead = self.due[kinds.index("unfold")] - self.due[kinds.index("fold") - 1]
            count = max(count, ahead + 2)
        return count


class Plan:
    def __init__(self, narrow, wide, items, slots, width, ff):
        self.narrow, self.wide, self.width, self.ff = narrow, wide, width, ff
        self.items, self.slots = items, slots
        self.rows = items * slots
        self.padded = self.rows + -self.rows % 256
        self.pairs = width // (2 * HEAD_DIM)
        narrow_bits = self.narrow_bits = narrow.bit_length() - 1
        wide_bits = self.wide_bits = wide.bit_length() - 1
        rows = width // narrow
        chunk = SUB
        while rows % (2 * chunk) == 0 and chunk < MOST:
            chunk *= 2
        self.chunk = chunk
        near, mirror = (("wide", 1),), (("wide", 1), ("wide", 2))
        x, y, core = (("wide", 0),), (("narrow", 1),), (("narrow", 0),)
        if (narrow, wide) == (4, 8):
            self.links = (core, y, x, near, mirror)
            half, quarter = chunk // 2, chunk // 4
            z_bit, x_bit, y_bit, core_bit = ("wide", 2), x[0], y[0], core[0]
            one = Part(
                0,
                width // 3 * 2,
                [(spot % 2 * 2 + spot // 2, 0, chunk) for spot in range(4)],
                [
                    Move("halve", core, 2 * chunk, core_bit),
                    Move("halve", y, chunk, y_bit),
                    Move("fold", near, chunk),
                    Move("halve", mirror, half, z_bit, True),
                    Move("halve", x, quarter, x_bit, True),
                ],
                [
                    Move("double", x, quarter, inner=True),
                    Move("double", mirror, half, inner=True),
                    Move("unfold", near, chunk),
                ],
                [(z_bit, half), (x_bit, quarter)],
            )
            two = Part(
                width // 3 * 2,
                width // 3,
                [
                    (2 * (spot % 2) + spot // 4, spot // 2 % 2 * half, half)
                    for spot in range(8)
                ],
                [
                    Move("halve", core, 2 * chunk, core_bit),
                    Move("halve", x, chunk, x_bit),
                    Move("halve", y, half, y_bit),
                    Move("fold", near, half),
                    Move("halve", mirror, quarter, z_bit, True),
                ],
                [
                    Move("double", mirror, quarter, inner=True),
                    Move("unfold", near, half),
                    Move("double", x, half),
                ],
                [(x_bit, half), (z_bit, quarter)],
            )
            self.parts = (one, two)
        else:
            self.links = tuple((("narrow", place),) for place in range(narrow_bits))
            self.links += tuple((("wide", place),) for place in range(wide_bits))
            sums, gathers, selects = [], [], []
            length = narrow * chunk
            for (axis, place), in self.links:
                if length > SUB:
                    length //= 2
                    sums.append(Move("halve", ((axis, place),), length, (axis, place)))
                    if axis == "wide":
                        selects.append(((axis, place), length))
                        gathers.insert(0, Move("double", ((axis, place),), length))
                else:
                    sums.append(Move("add", ((axis, place),), length))
            picks = [(reversed_bits(spot, narrow_bits), 0, chunk) for spot in range(narrow)]
            self.parts = (Part(0, width, picks, sums, gathers, selects),)
        self.stages = max(len(part.moves) for part in self.parts)
        self.depth = max(part.due[-1] for part in self.parts)
        self.slots_most = max(
            part.slots(stage) for part in self.parts for stage in range(len(part.moves))
        )
        self.phases = []
        start = 0
        for rows_block, windows in (
            (ff // narrow, 1),
            (rows, ff // width),
            (rows, 1),
            (rows, 3),
        ):
            count = rows_block // chunk * windows
            self.phases.append((start, count, rows_block, windows))
            start += count
        self.chunks = start
        self.ff_tiles = ff // TILE
        self.split = self.phases[1][0] // self.ff_tiles
        assert self.split in (1, 2)
        tall = ff // narrow
        self.groups = tall // TILE if tall % TILE == 0 else 1
        self.blocks = self.ff_tiles // self.groups
        self.jobs = {}
        tick = 0
        for name, count in (
            ("ff", self.ff_tiles * self.split),
            ("norm", self.split),
            ("mix", 1),
            ("item", items * self.split),
            ("pack", 1),
            ("first", self.split),
            ("input", self.split),
        ):
            self.jobs[name] = (tick, count)
            tick += count
        self.vector_tick = tick
        assert self.phases[2][0] >= self.jobs["item"][0]
        assert self.phases[3][0] >= self.jobs["first"][0]
        self.vector_rows = 8 + ff // width
        self.vector_rows += -self.vector_rows % SUB
        self.ticks = self.chunks + self.depth
        self.vector_every = (self.ticks - 1 - self.vector_tick) // len(self.links)
        assert self.vector_every > 0


def layer_kernel(plan, names, *refs):
    r = types.SimpleNamespace(**dict(zip(names, refs)))
    width, chunk, narrow, slots = plan.width, plan.chunk, plan.narrow, plan.slots
    rows, padded, pairs = plan.rows, plan.padded, plan.pairs
    score_scale = HEAD_DIM ** (-0.5)
    spots = {"narrow": lax.axis_index("narrow"), "wide": lax.axis_index("wide")}
    inner = bit_of(spots["wide"], 1) != bit_of(spots["wide"], 2)
    outer = bit_of(spots["wide"], 1) == bit_of(spots["wide"], 2)

    bits = {
        (axis, place): bit_of(spots[axis], place)
        for axis, count in (("narrow", plan.narrow_bits), ("wide", plan.wide_bits))
        for place in range(count)
    }
    partners = {}
    for flips in plan.links:
        there = dict(spots)
        for axis, place in flips:
            there[axis] = there[axis] + (1 - 2 * bits[axis, place]) * 2**place
        partners[flips] = there

    loads = {}
    for number, name in enumerate(("tok", "jw", "mw", "ew", "cot", "sw")):
        loads[name] = pltpu.make_async_copy(
            getattr(r, name + "_in"), getattr(r, name), r.load_sems.at[number]
        )
    loads["tok"].start()
    loads["jw"].start()

    barrier = pltpu.get_barrier_semaphore()
    for flips in plan.links:
        pl.semaphore_signal(barrier, inc=1, device_id=partners[flips], device_id_type=MESH)

    def vector(row):
        return r.vec[row : row + 1, :]

    def item_rows(item):
        return aligned(item * slots, slots, SUB)

    def row_live(item):
        return lax.broadcasted_iota(jnp.int32, (slots, 1), 0) < r.visible[item]

    lanes = lax.broadcasted_iota(jnp.int32, (slots, 2 * HEAD_DIM), 1)
    first_head = lanes < HEAD_DIM

    def both_heads(value):
        zero = jnp.zeros_like(value)
        return jnp.concatenate(
            [jnp.where(first_head, value, zero), jnp.where(first_head, zero, value)], axis=0
        ).astype(BF16)

    def one_head_each(value):
        return jnp.where(first_head, value[:slots], value[slots:])

    def normalized(values):
        center = values - jnp.mean(values, axis=-1, keepdims=True)
        spread = lax.rsqrt(jnp.mean(center * center, axis=-1, keepdims=True) + EPSILON)
        return center * spread, spread

    def norm_backward(grad, unit, spread):
        return spread * (
            grad
            - jnp.mean(grad, axis=-1, keepdims=True)
            - unit * jnp.mean(grad * unit, axis=-1, keepdims=True)
        )

    def each_item(body):
        lax.fori_loop(0, plan.items, lambda item, carry: (body(item), carry)[1], 0)

    def each_tile(count, body):
        lax.fori_loop(0, count, lambda tile, carry: (body(tile), carry)[1], 0)

    def pair_lanes(part, pair):
        start = part * width + pair * 2 * HEAD_DIM
        return slice(start, start + 2 * HEAD_DIM)

    small = (r.g1, r.s1, r.qb, r.vb, r.mb, r.g2, r.s2, r.sb)
    for row, ref in enumerate(small):
        r.vec[row : row + 1, :] = ref[...].astype(F32).reshape(1, width)
    for row in range(plan.ff // width):
        value = r.eb[row * width : (row + 1) * width].astype(F32)
        r.vec[8 + row : 9 + row, :] = value.reshape(1, width)
    r.stage[rows:, :] = jnp.zeros((padded - rows, width), F32)
    for ref in (r.sums, r.acc_out, r.acc_grad):
        ref[...] = jnp.zeros_like(ref)
    loads["tok"].wait()

    def first_norm(item):
        unit, _ = normalized(r.tok[item].astype(F32))
        r.stage[item_rows(item), :] = unit * vector(0) + vector(1)

    each_item(first_norm)
    r.first_rows[...] = r.stage[...].astype(BF16)
    for name in ("mw", "ew", "cot", "sw"):
        loads[name].start()
    loads["jw"].wait()
    for part, bias in enumerate((2, None, 3)):

        cols = slice(part * width, (part + 1) * width)
        value = matmul(r.first_rows[...], r.jw[:, cols])
        if bias is not None:
            value = value + vector(bias)
        r.qkv[:, cols] = value.astype(BF16).astype(F32)
    r.qkv[rows:, :] = jnp.zeros((padded - rows, 3 * width), F32)

    def attend_item(item):
        here = item_rows(item)
        key_live = (
            lax.broadcasted_iota(jnp.int32, (2 * slots, slots), 1) < r.visible[item]
        )
        every = range(pairs)
        queries = [both_heads(r.qkv[here, pair_lanes(0, pair)]) for pair in every]
        keys = [r.qkv[here, pair_lanes(1, pair)].astype(BF16) for pair in every]
        values = [r.qkv[here, pair_lanes(2, pair)].astype(BF16) for pair in every]
        logits = [matmul(queries[pair], keys[pair], ((1,), (1,))) for pair in every]
        logits = [jnp.where(key_live, value * score_scale, -1000000000.0) for value in logits]
        tops = [jnp.max(value, axis=-1, keepdims=True) for value in logits]
        expos = [jnp.exp(logits[pair] - tops[pair]) for pair in every]
        totals = [jnp.sum(value, axis=-1, keepdims=True) for value in expos]
        attends = [expos[pair] * (1.0 / totals[pair]) for pair in every]
        mixed = [matmul(attends[pair].astype(BF16), values[pair]) for pair in every]
        for pair in every:
            r.attend[item * pairs + pair] = attends[pair]
            r.stage[here, pair_lanes(0, pair)] = one_head_each(mixed[pair])

    each_item(attend_item)
    r.mixed_rows[...] = r.stage[...].astype(BF16)
    loads["mw"].wait()

    r.middle[...] = matmul(r.mixed_rows[...], r.mw[...]) + vector(4)

    def second_norm(item):
        here = item_rows(item)
        middle = r.middle[here, :] + r.tok[item].astype(F32)
        r.middle[here, :] = middle
        unit, _ = normalized(middle)
        r.stage[here, :] = unit * vector(5) + vector(6)

    each_item(second_norm)
    r.second[...] = r.stage[...].astype(BF16)
    loads["ew"].wait()

    def expand_bias(tile):
        per_row = width // TILE
        return r.vec[
            pl.ds(8 + lax.div(tile, per_row), 1),
            aligned(lax.rem(tile, per_row) * TILE, TILE, TILE),
        ]

    def hidden_tile(tile):
        cols = aligned(tile * TILE, TILE, TILE)
        hidden = matmul(r.second[...], r.ew[:, cols]) + expand_bias(tile)
        return hidden, 0.5 + 0.5 * lax.erf(hidden * ROOT_HALF)

    def expand_tile(place):
        tile = place * plan.groups
        hidden, normal = hidden_tile(tile)
        r.active_t[aligned(tile * TILE, TILE, TILE), :] = (hidden * normal).astype(BF16).T

    each_tile(plan.blocks, expand_tile)
    loads["cot"].wait()

    def mask_cotangent(item):
        grad = r.cot[item].astype(F32)
        r.stage[item_rows(item), :] = jnp.where(row_live(item), grad, 0.0)

    each_item(mask_cotangent)
    r.grad_out[...] = r.stage[...].astype(BF16)
    loads["sw"].wait()

    rows_full = rows // 16 * 16

    def share(count, turn, body):
        size = -(-count // plan.split)
        first = turn * size
        last = jnp.minimum(first + size, count)
        lax.fori_loop(first, last, lambda place, carry: (body(place), carry)[1], 0)

    def in_turns(turn, first_half, second_half):
        number = lax.div(turn, plan.split)
        if plan.split == 1:
            first_half(number)
            second_half(number)
        else:
            half = lax.rem(turn, plan.split)
            pl.when(half == 0)(lambda: first_half(number))
            pl.when(half == 1)(lambda: second_half(number))

    def ff_job(turn):
        def tile_job(number):
            group = lax.rem(lax.div(number, plan.blocks) + 1, plan.groups)
            tile = lax.rem(number, plan.blocks) * plan.groups + group
            cols = aligned(tile * TILE, TILE, TILE)
            hidden, normal = hidden_tile(tile)
            active = (hidden * normal).astype(BF16)
            r.active_t[cols, :] = active.T
            slope = normal + hidden * (PEAK * jnp.exp(-0.5 * hidden * hidden))
            grad = matmul(r.grad_out[...], r.sw[cols, :], ((1,), (1,)))
            grad_hidden = (grad * slope).astype(BF16)
            r.grad_hidden[:, cols] = grad_hidden
            r.expand_sums[tile] = jnp.sum(grad_hidden.astype(F32), axis=0, keepdims=True)
            r.acc_out[...] += matmul(active, r.sw[cols, :])
            r.acc_grad[...] += matmul(grad_hidden, r.ew[:, cols], ((1,), (1,)))

        def turn_rows(number):
            for place, (rows_ref, turned) in enumerate(
                (
                    (r.second, r.second_t),
                    (r.mixed_rows, r.mixed_t),
                    (r.first_rows, r.first_t),
                )
            ):

                @pl.when(number == place)
                def _():
                    turned[...] = rows_ref[...].T

        in_turns(turn, tile_job, turn_rows)

    def norm_job(turn):
        def one(item):
            here = item_rows(item)
            live = row_live(item)
            middle = r.middle[here, :]
            grad_out = jnp.where(live, r.cot[item].astype(F32), 0.0)
            layer_out = jnp.where(live, middle + (r.acc_out[here, :] + vector(7)), 0.0)
            r.cot[item] = layer_out.astype(BF16)
            unit, spread = normalized(middle)
            grad = r.acc_grad[here, :]
            r.sums[5:6, :] += jnp.sum(grad * unit, axis=0, keepdims=True)
            r.sums[6:7, :] += jnp.sum(grad, axis=0, keepdims=True)
            r.sums[7:8, :] += jnp.sum(grad_out, axis=0, keepdims=True)
            grad_middle = grad_out + norm_backward(grad * vector(5), unit, spread)
            r.acc_out[here, :] = grad_middle
            r.sums[4:5, :] += jnp.sum(
                grad_middle.astype(BF16).astype(F32), axis=0, keepdims=True
            )

        share(plan.items, turn, one)

    def mix_job(turn):
        r.grad_branch[:rows_full, :] = r.acc_out[:rows_full, :].astype(BF16)
        tail = jnp.concatenate(
            [r.acc_out[rows_full:rows, :], jnp.zeros((padded - rows, width), F32)], axis=0
        )
        r.grad_branch[rows_full:, :] = tail.astype(BF16)

        def one(tile):
            cols = aligned(tile * TILE, TILE, TILE)
            value = matmul(r.grad_branch[...], r.mw[cols, :], ((1,), (1,)))
            r.stage[:, cols] = value.astype(BF16).astype(F32)

        each_tile(width // TILE, one)

    def item_job(turn):
        def scores(item):
            here = item_rows(item)
            for pair in range(pairs):
                values = r.qkv[here, pair_lanes(2, pair)].astype(BF16)
                grad_mixed = both_heads(r.stage[here, pair_lanes(0, pair)])
                attend = r.attend[item * pairs + pair]
                grad_attend = matmul(grad_mixed, values, ((1,), (1,)))
                inner_sum = jnp.sum(attend * grad_attend, axis=-1, keepdims=True)
                r.grad_logits[pair] = (attend * (grad_attend - inner_sum)).astype(BF16)
                r.qkv[here, pair_lanes(2, pair)] = matmul(
                    attend.astype(BF16), grad_mixed, ((0,), (0,))
                )

        def inputs(item):
            here = item_rows(item)
            for pair in range(pairs):
                query = both_heads(r.qkv[here, pair_lanes(0, pair)])
                keys = r.qkv[here, pair_lanes(1, pair)].astype(BF16)
                grad_logits = r.grad_logits[pair]
                grad_query = one_head_each(matmul(grad_logits, keys)) * score_scale
                grad_key = matmul(grad_logits, query, ((0,), (0,))) * score_scale
                r.qkv[here, pair_lanes(0, pair)] = grad_query
                r.qkv[here, pair_lanes(1, pair)] = grad_key

        in_turns(turn, scores, inputs)

    def joint_rows(part):
        return slice(part * padded, (part + 1) * padded)

    def pack_job(turn):
        for part in range(3):
            value = r.qkv[:, part * width : (part + 1) * width].astype(BF16)
            r.sw[joint_rows(part), :] = value
            if part != 1:
                row = 2 if part == 0 else 3
                r.sums[row : row + 1, :] = jnp.sum(value.astype(F32), axis=0, keepdims=True)

    def first_job(turn):
        def one(tile):
            cols = aligned(tile * TILE, TILE, TILE)
            total = None
            for part in range(3):
                value = matmul(
                    r.sw[joint_rows(part), :],
                    r.jw[cols, part * width : (part + 1) * width],
                    ((1,), (1,)),
                )
                total = value if total is None else total + value
            r.acc_grad[:, cols] = total

        share(width // TILE, turn, one)

    def input_job(turn):
        def one(item):
            here = item_rows(item)
            unit, spread = normalized(r.tok[item].astype(F32))
            grad = r.acc_grad[here, :]
            r.sums[0:1, :] += jnp.sum(grad * unit, axis=0, keepdims=True)
            r.sums[1:2, :] += jnp.sum(grad, axis=0, keepdims=True)
            total = r.acc_out[here, :] + norm_backward(grad * vector(0), unit, spread)
            r.tok[item] = total.astype(BF16)

        share(plan.items, turn, one)

        @pl.when(turn == 0)
        def _():
            per_row = width // TILE
            for tile in range(plan.ff_tiles):
                row, start = 8 + tile // per_row, tile % per_row * TILE
                r.sums[row : row + 1, start : start + TILE] = r.expand_sums[tile]

    def when(condition, action):
        if condition is True:
            action()
        else:
            pl.when(condition)(action)

    def roles(move):
        if move.kind == "fold":
            return outer, inner
        if move.kind == "unfold":
            return inner, outer
        return (inner, inner) if move.inner else (True, True)

    def land(number, stage, item):
        ref = getattr(r, f"land{number}_{stage}")
        return ref.at[lax.rem(item, plan.parts[number].slots(stage))]

    def source(number, stage, item):
        if stage == 0:
            return getattr(r, f"part{number}").at[lax.rem(item, 2)]
        return land(number, stage - 1, item)

    kept, given, regions = {}, {}, {}
    for number, part in enumerate(plan.parts):
        for stage, move in enumerate(part.moves):
            bit = bits[move.select] if move.select else 0
            kept[number, stage] = bit * move.length
            given[number, stage] = (1 - bit) * move.length if move.select else 0
            regions[number, stage] = sum(
                bits[select] * size for select, size in part.selects if size >= move.length
            )

    def in_whole(number, stage, item):
        part = plan.parts[number]
        return (
            item,
            aligned(regions[number, stage], part.moves[stage].length, SUB),
            pl.ds(part.column, part.columns),
        )

    def transfer(number, stage, item):
        part = plan.parts[number]
        move = part.moves[stage]
        slot = lax.rem(item, part.slots(stage))
        if stage < len(part.sums):
            src = source(number, stage, item).at[
                aligned(given[number, stage], move.length, SUB)
            ]
            dst = land(number, stage, item)
        else:
            src = r.whole.at[in_whole(number, stage, item)]
            dst = src
        return pltpu.make_async_remote_copy(
            src_ref=src,
            dst_ref=dst,
            send_sem=r.send_sems.at[number, stage, slot],
            recv_sem=r.recv_sems.at[number, stage, slot],
            device_id=partners[move.flips],
            device_id_type=MESH,
        )

    def begin(number, stage, item):
        sender, _ = roles(plan.parts[number].moves[stage])
        when(sender, lambda: transfer(number, stage, item).start())

    def settle(number, stage, item):
        part = plan.parts[number]
        move = part.moves[stage]
        sender, receiver = roles(move)

        def receive():
            if stage < len(part.sums):
                land(number, stage, item)[...] += source(number, stage, item)[
                    aligned(kept[number, stage], move.length, SUB)
                ]
            if stage == len(part.sums) - 1:
                r.whole[in_whole(number, stage, item)] = land(number, stage, item)[...]

        if move.kind in ("fold", "unfold"):
            when(sender, lambda: transfer(number, stage, item).wait_send())

            def arrive():
                transfer(number, stage, item).wait_recv()
                receive()

        else:

            def arrive():
                transfer(number, stage, item).wait()
                receive()

        when(receiver, arrive)
        if stage + 1 < len(part.moves):
            begin(number, stage + 1, item)

    def rows_of(phase):
        _, count, _, windows = plan.phases[phase]
        return count // windows

    def produce(item):
        slot = lax.rem(item, 2)
        lefts = (r.active_t, r.second_t, r.mixed_t, r.first_t)
        rights = (r.grad_out, r.grad_hidden, r.grad_branch, r.sw)
        for phase, (start, count, rows_block, windows) in enumerate(plan.phases):
            left, right = lefts[phase], rights[phase]

            @pl.when((item >= start) & (item < start + count))
            def _():
                local = item - start
                tall = rows_of(phase)
                row = lax.rem(local, tall) * chunk
                window = lax.div(local, tall)
                for number, part in enumerate(plan.parts):
                    picked = [
                        left[aligned(block * rows_block + row + offset, size, size), :]
                        for block, offset, size in part.picks
                    ]
                    if phase == 3:
                        other = right[
                            aligned(window * padded, padded, 256),
                            part.column : part.column + part.columns,
                        ]
                    else:
                        other = right[
                            :, aligned(window * width + part.column, part.columns, 128)
                        ]
                    getattr(r, f"part{number}")[slot] = matmul(
                        jnp.concatenate(picked, axis=0), other
                    )

    def vector_exchange(stage):
        return pltpu.make_async_remote_copy(
            src_ref=r.sums if stage == 0 else r.vector_land.at[stage - 1],
            dst_ref=r.vector_land.at[stage],
            send_sem=r.vector_sems.at[0, stage],
            recv_sem=r.vector_sems.at[1, stage],
            device_id=partners[plan.links[stage]],
            device_id_type=MESH,
        )

    def vector_step(tick):
        count = len(plan.links)
        for stage in range(count + 1):

            @pl.when(tick == plan.vector_tick + stage * plan.vector_every)
            def _():
                if stage > 0:
                    vector_exchange(stage - 1).wait()
                    before = r.sums if stage == 1 else r.vector_land.at[stage - 2]
                    r.vector_land[stage - 1] += before[...]
                if stage < count:
                    vector_exchange(stage).start()

    pl.semaphore_wait(barrier, len(plan.links))

    def step(tick, carry):
        @pl.when(tick < plan.chunks)
        def _():
            produce(tick)
            for number in range(len(plan.parts)):
                begin(number, 0, tick)

        for stage in range(plan.stages):
            for number, part in enumerate(plan.parts):
                if stage < len(part.moves):
                    item = tick - part.due[stage]

                    @pl.when((item >= 0) & (item < plan.chunks))
                    def _():
                        settle(number, stage, item)

        vector_step(tick)
        run = {
            "ff": ff_job,
            "norm": norm_job,
            "mix": mix_job,
            "item": item_job,
            "pack": pack_job,
            "first": first_job,
            "input": input_job,
        }
        for name, (start, count) in plan.jobs.items():
            job = functools.partial(run[name], tick - start)
            pl.when((tick >= start) & (tick < start + count))(job)

        return carry

    lax.fori_loop(0, plan.ticks, step, 0)
    r.vector_out[...] = r.vector_land[len(plan.links) - 1]


def write_kernel(plan, tok, cot, whole, sums, *refs):
    outs, sems = refs[:-1], refs[-1]
    copies = [(tok, outs[0]), (cot, outs[1])]
    for (start, count, _, windows), out in zip(plan.phases, outs[2:6]):
        tall = count // windows
        for window in range(windows):
            first = start + window * tall
            cols = pl.ds(window * plan.width, plan.width)
            copies.append((whole.at[first : first + tall], out.at[:, :, cols]))
    copies = [
        pltpu.make_async_copy(source, target, sems.at[number])
        for number, (source, target) in enumerate(copies)
    ]
    for copy in copies:
        copy.start()
    own = lax.axis_index("narrow")
    for place in range(plan.narrow):

        @pl.when(own == place)
        def _():
            for row, out in enumerate(outs[6:14]):
                size = out.shape[0]
                out[...] = sums[row : row + 1, place * size : (place + 1) * size].reshape(size)
            size = outs[14].shape[0]
            row, start = 8 + place * size // plan.width, place * size % plan.width
            outs[14][...] = sums[row : row + 1, start : start + size].reshape(size)

    for copy in copies:
        copy.wait()


def shards(
    tokens,
    visible,
    first_gain,
    first_shift,
    joint_weight,
    query_bias,
    value_bias,
    mixer_weight,
    mixer_bias,
    second_gain,
    second_shift,
    expand_weight,
    expand_bias,
    shrink_weight,
    shrink_bias,
    cotangent,
):
    items, slots, width = tokens.shape
    ff = expand_weight.shape[1]
    narrow, wide = lax.axis_size("narrow"), lax.axis_size("wide")
    plan = Plan(narrow, wide, items, slots, width, ff)
    padded, chunk = plan.padded, plan.chunk
    hbm = pl.BlockSpec(memory_space=pl.ANY)
    vmem = pl.BlockSpec(memory_space=pltpu.VMEM)
    smem = pl.BlockSpec(memory_space=pltpu.SMEM)
    inputs = {
        "visible": (visible, smem),
        "g1": (first_gain, vmem),
        "s1": (first_shift, vmem),
        "qb": (query_bias, vmem),
        "vb": (value_bias, vmem),
        "mb": (mixer_bias, vmem),
        "g2": (second_gain, vmem),
        "s2": (second_shift, vmem),
        "sb": (shrink_bias, vmem),
        "eb": (expand_bias, vmem),
        "tok_in": (tokens, hbm),
        "cot_in": (cotangent, hbm),
        "jw_in": (joint_weight, hbm),
        "mw_in": (mixer_weight, hbm),
        "ew_in": (expand_weight, hbm),
        "sw_in": (shrink_weight, hbm),
    }
    block = width // narrow
    outputs = {
        "tok": (tokens.shape, BF16),
        "cot": (tokens.shape, BF16),
        "whole": ((plan.chunks, chunk, width), F32),
        "vector_out": ((plan.vector_rows, width), F32),
    }
    scratch = {
        "jw": pltpu.VMEM(joint_weight.shape, BF16),
        "mw": pltpu.VMEM(mixer_weight.shape, BF16),
        "ew": pltpu.VMEM(expand_weight.shape, BF16),
        "sw": pltpu.VMEM(shrink_weight.shape, BF16),
        "stage": pltpu.VMEM((padded, width), F32),
        "first_rows": pltpu.VMEM((padded, width), BF16),
        "mixed_rows": pltpu.VMEM((padded, width), BF16),
        "qkv": pltpu.VMEM((padded, 3 * width), F32),
        "attend": pltpu.VMEM((items * plan.pairs, 2 * slots, slots), F32),
        "first_t": pltpu.VMEM((width, padded), BF16),
        "mixed_t": pltpu.VMEM((width, padded), BF16),
        "second": pltpu.VMEM((padded, width), BF16),
        "second_t": pltpu.VMEM((width, padded), BF16),
        "middle": pltpu.VMEM((padded, width), F32),
        "grad_hidden": pltpu.VMEM((padded, ff), BF16),
        "active_t": pltpu.VMEM((ff, padded), BF16),
        "grad_out": pltpu.VMEM((padded, width), BF16),
        "acc_out": pltpu.VMEM((padded, width), F32),
        "acc_grad": pltpu.VMEM((padded, width), F32),
        "grad_branch": pltpu.VMEM((padded, width), BF16),
        "vec": pltpu.VMEM((plan.vector_rows, width), F32),
        "grad_logits": pltpu.VMEM((plan.pairs, 2 * slots, slots), BF16),
        "sums": pltpu.VMEM((plan.vector_rows, width), F32),
        "expand_sums": pltpu.VMEM((plan.ff_tiles, 1, TILE), F32),
        "vector_land": pltpu.VMEM((len(plan.links), plan.vector_rows, width), F32),
        "load_sems": pltpu.SemaphoreType.DMA((6,)),
        "vector_sems": pltpu.SemaphoreType.DMA((2, len(plan.links))),
        "send_sems": pltpu.SemaphoreType.DMA((len(plan.parts), plan.stages, plan.slots_most)),
        "recv_sems": pltpu.SemaphoreType.DMA((len(plan.parts), plan.stages, plan.slots_most)),
    }
    for number, part in enumerate(plan.parts):
        scratch[f"part{number}"] = pltpu.VMEM((2, narrow * chunk, part.columns), F32)
        for stage, move in enumerate(part.sums):
            scratch[f"land{number}_{stage}"] = pltpu.VMEM(
                (part.slots(stage), move.length, part.columns), F32
            )
    results = pl.pallas_call(
        functools.partial(layer_kernel, plan, (*inputs, *outputs, *scratch)),
        out_shape=[pltpu.VMEM(shape, kind) for shape, kind in outputs.values()],
        in_specs=[spec for _, spec in inputs.values()],
        out_specs=[vmem] * len(outputs),
        scratch_shapes=list(scratch.values()),
        compiler_params=pltpu.CompilerParams(
            has_side_effects=True, vmem_limit_bytes=52 * 2**20, collective_id=0
        ),
        name="layer",
    )(*(value for value, _ in inputs.values()))
    row_counts = [count // windows for _, count, _, windows in plan.phases]
    shapes = [jax.ShapeDtypeStruct(tokens.shape, BF16)] * 2
    shapes += [
        jax.ShapeDtypeStruct((tall, chunk, windows * width), F32)
        for tall, (_, _, _, windows) in zip(row_counts, plan.phases)
    ]
    shapes += [jax.ShapeDtypeStruct((block,), F32)] * 8
    shapes += [jax.ShapeDtypeStruct((ff // narrow,), F32)]
    copies = 2 + sum(windows for _, _, _, windows in plan.phases)
    outs = pl.pallas_call(
        functools.partial(write_kernel, plan),
        out_shape=shapes,
        in_specs=[vmem] * len(results),
        out_specs=[hbm] * 6 + [vmem] * 9,
        scratch_shapes=[pltpu.SemaphoreType.DMA((copies,))],
        compiler_params=pltpu.CompilerParams(vmem_limit_bytes=4 * 2**20),
        name="write",
    )(*(pltpu.with_memory_space_constraint(value, pltpu.VMEM) for value in results))
    input_grad, layer_out = outs[:2]
    shrink, expand, mixer, joint = (
        out.reshape(-1, out.shape[-1]) for out in outs[2:6]
    )
    vectors = outs[6:]
    return (
        layer_out,
        input_grad,
        vectors[0],
        vectors[1],
        joint,
        vectors[2],
        vectors[3],
        mixer,
        vectors[4],
        vectors[5],
        vectors[6],
        expand,
        vectors[8],
        shrink,
        vectors[7],
    )


def solution(mesh):
    return jax.shard_map(
        shards,
        mesh=mesh,
        in_specs=(
            P(("wide", "narrow"), None, None),
            P(("wide", "narrow")),
            P(),
            P(),
            P(),
            P(),
            P(),
            P(),
            P(),
            P(),
            P(),
            P(),
            P(),
            P(),
            P(),
            P(("wide", "narrow"), None, None),
        ),
        out_specs=(
            P(("wide", "narrow"), None, None),
            P(("wide", "narrow"), None, None),
            P("narrow"),
            P("narrow"),
            P("narrow", None),
            P("narrow"),
            P("narrow"),
            P("narrow", None),
            P("narrow"),
            P("narrow"),
            P("narrow"),
            P("narrow", None),
            P("narrow"),
            P("narrow", None),
            P("narrow"),
        ),
        check_vma=False,
    )
```

```python
import functools
import types

import jax
import jax.numpy as jnp
from jax import lax
from jax.experimental import pallas as pl
from jax.experimental.pallas import tpu as pltpu
from jax.sharding import PartitionSpec as P

HEAD_DIM = 64
EPSILON = 1e-06
SUB = 8
LAGS = ([1] + [2] * 15, [1] + [2] * 15)
MOST = 32
TILE = 256
MESH = pl.DeviceIdType.MESH
ROOT_HALF = 0.5**0.5
PEAK = 0.3989422804014327
BF16 = jnp.bfloat16
F32 = jnp.float32


def bit_of(index, place):
    return lax.rem(lax.div(index, 2**place), 2)


def reversed_bits(value, count):
    out = 0
    for place in range(count):
        out = out * 2 + (value >> place) % 2
    return out


def aligned(start, size, unit):
    return pl.ds(pl.multiple_of(start, unit), size)


def matmul(left, right, contract=((1,), (0,))):
    return lax.dot_general(left, right, (contract, ((), ())), preferred_element_type=F32)


class Move:
    def __init__(self, kind, flips, length, select=None, inner=False):
        self.kind, self.flips, self.length = kind, flips, length
        self.select, self.inner = select, inner


class Part:
    def __init__(self, column, columns, picks, sums, gathers, selects):
        self.column, self.columns, self.picks = column, columns, picks
        self.sums, self.moves = sums, sums + gathers
        self.selects = selects
        self.lags = LAGS[column > 0][: len(self.moves)]
        self.due = [sum(self.lags[: stage + 1]) for stage in range(len(self.moves))]

    def flights(self, stage):
        return self.lags[stage] + 1

    def slots(self, stage):
        after = self.lags[stage + 1] if stage + 1 < len(self.sums) else 0
        count = 2 * self.lags[stage] + after + 2
        if self.moves[stage].kind in ("fold", "unfold"):
            kinds = [move.kind for move in self.moves]
            ahead = self.due[kinds.index("unfold")] - self.due[kinds.index("fold") - 1]
            count = max(count, ahead + 2)
        return count


class Plan:
    def __init__(self, narrow, wide, items, slots, width, ff):
        self.narrow, self.wide, self.width, self.ff = narrow, wide, width, ff
        self.items, self.slots = items, slots
        self.rows = items * slots
        self.padded = self.rows + -self.rows % 256
        self.pairs = width // (2 * HEAD_DIM)
        narrow_bits = self.narrow_bits = narrow.bit_length() - 1
        wide_bits = self.wide_bits = wide.bit_length() - 1
        rows = width // narrow
        chunk = SUB
        while rows % (2 * chunk) == 0 and chunk < MOST:
            chunk *= 2
        self.chunk = chunk
        near, mirror = (("wide", 1),), (("wide", 1), ("wide", 2))
        x, y, core = (("wide", 0),), (("narrow", 1),), (("narrow", 0),)
        if (narrow, wide) == (4, 8):
            self.links = (core, y, x, near, mirror)
            half = chunk // 2
            z_bit, x_bit, y_bit, core_bit = ("wide", 2), x[0], y[0], core[0]
            one = Part(
                0,
                width // 3 * 2,
                [(spot % 2 * 2 + spot // 2, 0, chunk) for spot in range(4)],
                [
                    Move("halve", core, 2 * chunk, core_bit),
                    Move("halve", y, chunk, y_bit),
                    Move("fold", near, chunk),
                    Move("halve", mirror, half, z_bit, True),
                    Move("add", x, half, inner=True),
                ],
                [
                    Move("double", mirror, half, inner=True),
                    Move("unfold", near, chunk),
                ],
                [(z_bit, half)],
            )
            two = Part(
                width // 3 * 2,
                width // 3,
                [
                    (2 * (spot % 2) + spot // 4, spot // 2 % 2 * half, half)
                    for spot in range(8)
                ],
                [
                    Move("halve", core, 2 * chunk, core_bit),
                    Move("halve", x, chunk, x_bit),
                    Move("halve", y, half, y_bit),
                    Move("fold", near, half),
                    Move("add", mirror, half, inner=True),
                ],
                [
                    Move("unfold", near, half),
                    Move("double", x, half),
                ],
                [(x_bit, half)],
            )
            self.parts = (one, two)
        else:
            self.links = tuple((("narrow", place),) for place in range(narrow_bits))
            self.links += tuple((("wide", place),) for place in range(wide_bits))
            sums, gathers, selects = [], [], []
            length = narrow * chunk
            for (axis, place), in self.links:
                if length > SUB:
                    length //= 2
                    sums.append(Move("halve", ((axis, place),), length, (axis, place)))
                    if axis == "wide":
                        selects.append(((axis, place), length))
                        gathers.insert(0, Move("double", ((axis, place),), length))
                else:
                    sums.append(Move("add", ((axis, place),), length))
            picks = [(reversed_bits(spot, narrow_bits), 0, chunk) for spot in range(narrow)]
            self.parts = (Part(0, width, picks, sums, gathers, selects),)
        self.stages = max(len(part.moves) for part in self.parts)
        self.depth = max(part.due[-1] for part in self.parts)
        self.arrivals, self.sends, self.arrival_at, self.send_at = 0, 0, {}, {}
        for number, part in enumerate(self.parts):
            for stage in range(len(part.moves)):
                self.arrival_at[number, stage] = self.arrivals
                self.send_at[number, stage] = self.sends
                self.arrivals += part.slots(stage)
                self.sends += part.flights(stage)
        self.phases = []
        start = 0
        for rows_block, windows in (
            (ff // narrow, 1),
            (rows, ff // width),
            (rows, 1),
            (rows, 3),
        ):
            count = rows_block // chunk * windows
            self.phases.append((start, count, rows_block, windows))
            start += count
        self.chunks = start
        self.ff_tiles = ff // TILE
        self.split = self.phases[1][0] // self.ff_tiles
        assert self.split in (1, 2)
        tall = ff // narrow
        self.groups = tall // TILE if tall % TILE == 0 else 1
        self.blocks = self.ff_tiles // self.groups
        self.jobs = {}
        tick = self.split - 1
        for name, count in (
            ("ff", self.ff_tiles * self.split),
            ("norm", self.split),
            ("mix", 1),
            ("item", items * self.split),
            ("pack", 1),
            ("first", self.split),
            ("input", self.split),
        ):
            self.jobs[name] = (tick, count)
            tick += count
        self.vector_tick = tick
        assert self.phases[2][0] >= self.jobs["item"][0]
        assert self.phases[3][0] >= self.jobs["first"][0]
        self.vector_rows = 8 + ff // width
        self.vector_rows += -self.vector_rows % SUB
        self.ticks = self.chunks + self.depth
        self.vector_every = (self.ticks - 1 - self.vector_tick) // len(self.links)
        assert self.vector_every > 0


def layer_kernel(plan, names, *refs):
    r = types.SimpleNamespace(**dict(zip(names, refs)))
    width, chunk, narrow, slots = plan.width, plan.chunk, plan.narrow, plan.slots
    rows, padded, pairs = plan.rows, plan.padded, plan.pairs
    score_scale = HEAD_DIM ** (-0.5)
    spots = {"narrow": lax.axis_index("narrow"), "wide": lax.axis_index("wide")}
    inner = bit_of(spots["wide"], 1) != bit_of(spots["wide"], 2)
    outer = bit_of(spots["wide"], 1) == bit_of(spots["wide"], 2)

    bits = {
        (axis, place): bit_of(spots[axis], place)
        for axis, count in (("narrow", plan.narrow_bits), ("wide", plan.wide_bits))
        for place in range(count)
    }
    partners = {}
    for flips in plan.links:
        there = dict(spots)
        for axis, place in flips:
            there[axis] = there[axis] + (1 - 2 * bits[axis, place]) * 2**place
        partners[flips] = there

    loads = {}
    for number, name in enumerate(("tok", "jw", "mw", "ew", "cot", "sw")):
        loads[name] = pltpu.make_async_copy(
            getattr(r, name + "_in"), getattr(r, name), r.load_sems.at[number]
        )
    loads["tok"].start()
    loads["jw"].start()

    barrier = pltpu.get_barrier_semaphore()
    for flips in plan.links:
        pl.semaphore_signal(barrier, inc=1, device_id=partners[flips], device_id_type=MESH)

    def vector(row):
        return r.vec[row : row + 1, :]

    def item_rows(item):
        return aligned(item * slots, slots, SUB)

    def row_live(item):
        return lax.broadcasted_iota(jnp.int32, (slots, 1), 0) < r.visible[item]

    lanes = lax.broadcasted_iota(jnp.int32, (slots, 2 * HEAD_DIM), 1)
    first_head = lanes < HEAD_DIM

    def both_heads(value):
        zero = jnp.zeros_like(value)
        return jnp.concatenate(
            [jnp.where(first_head, value, zero), jnp.where(first_head, zero, value)], axis=0
        ).astype(BF16)

    def one_head_each(value):
        return jnp.where(first_head, value[:slots], value[slots:])

    def normalized(values):
        center = values - jnp.mean(values, axis=-1, keepdims=True)
        spread = lax.rsqrt(jnp.mean(center * center, axis=-1, keepdims=True) + EPSILON)
        return center * spread, spread

    def norm_backward(grad, unit, spread):
        return spread * (
            grad
            - jnp.mean(grad, axis=-1, keepdims=True)
            - unit * jnp.mean(grad * unit, axis=-1, keepdims=True)
        )

    def each_item(body):
        lax.fori_loop(0, plan.items, lambda item, carry: (body(item), carry)[1], 0)

    def each_tile(count, body):
        lax.fori_loop(0, count, lambda tile, carry: (body(tile), carry)[1], 0)

    def pair_lanes(part, pair):
        start = part * width + pair * 2 * HEAD_DIM
        return slice(start, start + 2 * HEAD_DIM)

    small = (r.g1, r.s1, r.qb, r.vb, r.mb, r.g2, r.s2, r.sb)
    for row, ref in enumerate(small):
        r.vec[row : row + 1, :] = ref[...].astype(F32).reshape(1, width)
    for row in range(plan.ff // width):
        value = r.eb[row * width : (row + 1) * width].astype(F32)
        r.vec[8 + row : 9 + row, :] = value.reshape(1, width)
    r.stage[rows:, :] = jnp.zeros((padded - rows, width), F32)
    for ref in (r.sums, r.acc_out, r.acc_grad):
        ref[...] = jnp.zeros_like(ref)
    loads["tok"].wait()

    def first_norm(item):
        unit, _ = normalized(r.tok[item].astype(F32))
        r.stage[item_rows(item), :] = unit * vector(0) + vector(1)

    each_item(first_norm)
    r.first_rows[...] = r.stage[...].astype(BF16)
    for name in ("mw", "ew", "cot", "sw"):
        loads[name].start()
    loads["jw"].wait()
    for part, bias in enumerate((2, None, 3)):

        cols = slice(part * width, (part + 1) * width)
        value = matmul(r.first_rows[...], r.jw[:, cols])
        if bias is not None:
            value = value + vector(bias)
        r.qkv[:, cols] = value.astype(BF16).astype(F32)
    r.qkv[rows:, :] = jnp.zeros((padded - rows, 3 * width), F32)

    def attend_item(item):
        here = item_rows(item)
        key_live = (
            lax.broadcasted_iota(jnp.int32, (2 * slots, slots), 1) < r.visible[item]
        )
        every = range(pairs)
        queries = [both_heads(r.qkv[here, pair_lanes(0, pair)]) for pair in every]
        keys = [r.qkv[here, pair_lanes(1, pair)].astype(BF16) for pair in every]
        values = [r.qkv[here, pair_lanes(2, pair)].astype(BF16) for pair in every]
        logits = [matmul(queries[pair], keys[pair], ((1,), (1,))) for pair in every]
        logits = [jnp.where(key_live, value * score_scale, -1000000000.0) for value in logits]
        tops = [jnp.max(value, axis=-1, keepdims=True) for value in logits]
        expos = [jnp.exp(logits[pair] - tops[pair]) for pair in every]
        totals = [jnp.sum(value, axis=-1, keepdims=True) for value in expos]
        attends = [expos[pair] * (1.0 / totals[pair]) for pair in every]
        mixed = [matmul(attends[pair].astype(BF16), values[pair]) for pair in every]
        for pair in every:
            r.attend[item * pairs + pair] = attends[pair]
            r.stage[here, pair_lanes(0, pair)] = one_head_each(mixed[pair])

    each_item(attend_item)
    r.mixed_rows[...] = r.stage[...].astype(BF16)
    loads["mw"].wait()

    r.middle[...] = matmul(r.mixed_rows[...], r.mw[...]) + vector(4)

    def second_norm(item):
        here = item_rows(item)
        middle = r.middle[here, :] + r.tok[item].astype(F32)
        r.middle[here, :] = middle
        unit, _ = normalized(middle)
        r.stage[here, :] = unit * vector(5) + vector(6)

    each_item(second_norm)
    r.second[...] = r.stage[...].astype(BF16)
    loads["ew"].wait()

    def expand_bias(tile):
        per_row = width // TILE
        return r.vec[
            pl.ds(8 + lax.div(tile, per_row), 1),
            aligned(lax.rem(tile, per_row) * TILE, TILE, TILE),
        ]

    def hidden_tile(tile):
        cols = aligned(tile * TILE, TILE, TILE)
        hidden = matmul(r.second[...], r.ew[:, cols]) + expand_bias(tile)
        return hidden, 0.5 + 0.5 * lax.erf(hidden * ROOT_HALF)

    def expand_tile(place):
        tile = place * plan.groups
        hidden, normal = hidden_tile(tile)
        r.active_t[aligned(tile * TILE, TILE, TILE), :] = (hidden * normal).astype(BF16).T

    each_tile(plan.blocks, expand_tile)
    loads["cot"].wait()

    def mask_cotangent(item):
        grad = r.cot[item].astype(F32)
        r.stage[item_rows(item), :] = jnp.where(row_live(item), grad, 0.0)

    each_item(mask_cotangent)
    r.grad_out[...] = r.stage[...].astype(BF16)
    loads["sw"].wait()

    rows_full = rows // 16 * 16

    def share(count, turn, body):
        size = -(-count // plan.split)
        first = turn * size
        last = jnp.minimum(first + size, count)
        lax.fori_loop(first, last, lambda place, carry: (body(place), carry)[1], 0)

    def in_turns(turn, first_half, second_half):
        number = lax.div(turn, plan.split)
        if plan.split == 1:
            first_half(number)
            second_half(number)
        else:
            half = lax.rem(turn, plan.split)
            pl.when(half == 0)(lambda: first_half(number))
            pl.when(half == 1)(lambda: second_half(number))

    def ff_job(turn):
        def tile_job(number):
            group = lax.rem(lax.div(number, plan.blocks) + 1, plan.groups)
            tile = lax.rem(number, plan.blocks) * plan.groups + group
            cols = aligned(tile * TILE, TILE, TILE)
            hidden, normal = hidden_tile(tile)
            active = (hidden * normal).astype(BF16)
            r.active_t[cols, :] = active.T
            slope = normal + hidden * (PEAK * jnp.exp(-0.5 * hidden * hidden))
            grad = matmul(r.grad_out[...], r.sw[cols, :], ((1,), (1,)))
            grad_hidden = (grad * slope).astype(BF16)
            r.grad_hidden[:, cols] = grad_hidden
            r.expand_sums[tile] = jnp.sum(grad_hidden.astype(F32), axis=0, keepdims=True)
            r.acc_out[...] += matmul(active, r.sw[cols, :])
            r.acc_grad[...] += matmul(grad_hidden, r.ew[:, cols], ((1,), (1,)))

        def turn_rows(number):
            for place, (rows_ref, turned) in enumerate(
                (
                    (r.second, r.second_t),
                    (r.mixed_rows, r.mixed_t),
                    (r.first_rows, r.first_t),
                )
            ):

                @pl.when(number == place)
                def _():
                    turned[...] = rows_ref[...].T

        in_turns(turn, tile_job, turn_rows)

    def norm_job(turn):
        def one(item):
            here = item_rows(item)
            live = row_live(item)
            middle = r.middle[here, :]
            grad_out = jnp.where(live, r.cot[item].astype(F32), 0.0)
            layer_out = jnp.where(live, middle + (r.acc_out[here, :] + vector(7)), 0.0)
            r.cot[item] = layer_out.astype(BF16)
            unit, spread = normalized(middle)
            grad = r.acc_grad[here, :]
            r.sums[5:6, :] += jnp.sum(grad * unit, axis=0, keepdims=True)
            r.sums[6:7, :] += jnp.sum(grad, axis=0, keepdims=True)
            r.sums[7:8, :] += jnp.sum(grad_out, axis=0, keepdims=True)
            grad_middle = grad_out + norm_backward(grad * vector(5), unit, spread)
            r.acc_out[here, :] = grad_middle
            r.sums[4:5, :] += jnp.sum(
                grad_middle.astype(BF16).astype(F32), axis=0, keepdims=True
            )

        share(plan.items, turn, one)

    def mix_job(turn):
        r.grad_branch[:rows_full, :] = r.acc_out[:rows_full, :].astype(BF16)
        tail = jnp.concatenate(
            [r.acc_out[rows_full:rows, :], jnp.zeros((padded - rows, width), F32)], axis=0
        )
        r.grad_branch[rows_full:, :] = tail.astype(BF16)

        def one(tile):
            cols = aligned(tile * TILE, TILE, TILE)
            value = matmul(r.grad_branch[...], r.mw[cols, :], ((1,), (1,)))
            r.stage[:, cols] = value.astype(BF16).astype(F32)

        each_tile(width // TILE, one)

    def item_job(turn):
        def scores(item):
            here = item_rows(item)
            for pair in range(pairs):
                values = r.qkv[here, pair_lanes(2, pair)].astype(BF16)
                grad_mixed = both_heads(r.stage[here, pair_lanes(0, pair)])
                attend = r.attend[item * pairs + pair]
                grad_attend = matmul(grad_mixed, values, ((1,), (1,)))
                inner_sum = jnp.sum(attend * grad_attend, axis=-1, keepdims=True)
                r.grad_logits[pair] = (attend * (grad_attend - inner_sum)).astype(BF16)
                r.qkv[here, pair_lanes(2, pair)] = matmul(
                    attend.astype(BF16), grad_mixed, ((0,), (0,))
                )

        def inputs(item):
            here = item_rows(item)
            for pair in range(pairs):
                query = both_heads(r.qkv[here, pair_lanes(0, pair)])
                keys = r.qkv[here, pair_lanes(1, pair)].astype(BF16)
                grad_logits = r.grad_logits[pair]
                grad_query = one_head_each(matmul(grad_logits, keys)) * score_scale
                grad_key = matmul(grad_logits, query, ((0,), (0,))) * score_scale
                r.qkv[here, pair_lanes(0, pair)] = grad_query
                r.qkv[here, pair_lanes(1, pair)] = grad_key

        in_turns(turn, scores, inputs)

    def joint_rows(part):
        return slice(part * padded, (part + 1) * padded)

    def pack_job(turn):
        for part in range(3):
            value = r.qkv[:, part * width : (part + 1) * width].astype(BF16)
            r.sw[joint_rows(part), :] = value
            if part != 1:
                row = 2 if part == 0 else 3
                r.sums[row : row + 1, :] = jnp.sum(value.astype(F32), axis=0, keepdims=True)

    def first_job(turn):
        def one(tile):
            cols = aligned(tile * TILE, TILE, TILE)
            total = None
            for part in range(3):
                value = matmul(
                    r.sw[joint_rows(part), :],
                    r.jw[cols, part * width : (part + 1) * width],
                    ((1,), (1,)),
                )
                total = value if total is None else total + value
            r.acc_grad[:, cols] = total

        share(width // TILE, turn, one)

    def input_job(turn):
        def one(item):
            here = item_rows(item)
            unit, spread = normalized(r.tok[item].astype(F32))
            grad = r.acc_grad[here, :]
            r.sums[0:1, :] += jnp.sum(grad * unit, axis=0, keepdims=True)
            r.sums[1:2, :] += jnp.sum(grad, axis=0, keepdims=True)
            total = r.acc_out[here, :] + norm_backward(grad * vector(0), unit, spread)
            r.tok[item] = total.astype(BF16)

        share(plan.items, turn, one)

        @pl.when(turn == 0)
        def _():
            per_row = width // TILE
            for tile in range(plan.ff_tiles):
                row, start = 8 + tile // per_row, tile % per_row * TILE
                r.sums[row : row + 1, start : start + TILE] = r.expand_sums[tile]

    def when(condition, action):
        if condition is True:
            action()
        else:
            pl.when(condition)(action)

    def roles(move):
        if move.kind == "fold":
            return outer, inner
        if move.kind == "unfold":
            return inner, outer
        return (inner, inner) if move.inner else (True, True)

    def land(number, stage, item):
        ref = getattr(r, f"land{number}_{stage}")
        return ref.at[lax.rem(item, plan.parts[number].slots(stage))]

    def source(number, stage, item):
        if stage == 0:
            return getattr(r, f"part{number}").at[lax.rem(item, 2)]
        return land(number, stage - 1, item)

    kept, given, regions = {}, {}, {}
    for number, part in enumerate(plan.parts):
        for stage, move in enumerate(part.moves):
            bit = bits[move.select] if move.select else 0
            kept[number, stage] = bit * move.length
            given[number, stage] = (1 - bit) * move.length if move.select else 0
            regions[number, stage] = sum(
                bits[select] * size for select, size in part.selects if size >= move.length
            )

    def in_whole(number, stage, item):
        part = plan.parts[number]
        return (
            item,
            aligned(regions[number, stage], part.moves[stage].length, SUB),
            pl.ds(part.column, part.columns),
        )

    def transfer(number, stage, item):
        part = plan.parts[number]
        move = part.moves[stage]
        arrival = plan.arrival_at[number, stage] + lax.rem(item, part.slots(stage))
        send = plan.send_at[number, stage] + lax.rem(item, part.flights(stage))
        if stage < len(part.sums):
            src = source(number, stage, item).at[
                aligned(given[number, stage], move.length, SUB)
            ]
            dst = land(number, stage, item)
        else:
            src = r.whole.at[in_whole(number, stage, item)]
            dst = src
        return pltpu.make_async_remote_copy(
            src_ref=src,
            dst_ref=dst,
            send_sem=r.send_sems.at[send],
            recv_sem=r.recv_sems.at[arrival],
            device_id=partners[move.flips],
            device_id_type=MESH,
        )

    def begin(number, stage, item):
        sender, _ = roles(plan.parts[number].moves[stage])
        when(sender, lambda: transfer(number, stage, item).start())

    def settle(number, stage, item):
        part = plan.parts[number]
        move = part.moves[stage]
        sender, receiver = roles(move)

        def receive():
            if stage < len(part.sums):
                land(number, stage, item)[...] += source(number, stage, item)[
                    aligned(kept[number, stage], move.length, SUB)
                ]
            if stage == len(part.sums) - 1:
                r.whole[in_whole(number, stage, item)] = land(number, stage, item)[...]

        if move.kind in ("fold", "unfold"):
            when(sender, lambda: transfer(number, stage, item).wait_send())

            def arrive():
                transfer(number, stage, item).wait_recv()
                receive()

        else:

            def arrive():
                transfer(number, stage, item).wait()
                receive()

        when(receiver, arrive)
        if stage + 1 < len(part.moves):
            begin(number, stage + 1, item)

    def rows_of(phase):
        _, count, _, windows = plan.phases[phase]
        return count // windows

    def produce(item):
        slot = lax.rem(item, 2)
        lefts = (r.active_t, r.second_t, r.mixed_t, r.first_t)
        rights = (r.grad_out, r.grad_hidden, r.grad_branch, r.sw)
        for phase, (start, count, rows_block, windows) in enumerate(plan.phases):
            left, right = lefts[phase], rights[phase]

            @pl.when((item >= start) & (item < start + count))
            def _():
                local = item - start
                tall = rows_of(phase)
                row = lax.rem(local, tall) * chunk
                window = lax.div(local, tall)
                for number, part in enumerate(plan.parts):
                    picked = [
                        left[aligned(block * rows_block + row + offset, size, size), :]
                        for block, offset, size in part.picks
                    ]
                    if phase == 3:
                        other = right[
                            aligned(window * padded, padded, 256),
                            part.column : part.column + part.columns,
                        ]
                    else:
                        other = right[
                            :, aligned(window * width + part.column, part.columns, 128)
                        ]
                    getattr(r, f"part{number}")[slot] = matmul(
                        jnp.concatenate(picked, axis=0), other
                    )

    def vector_exchange(stage):
        return pltpu.make_async_remote_copy(
            src_ref=r.sums if stage == 0 else r.vector_land.at[stage - 1],
            dst_ref=r.vector_land.at[stage],
            send_sem=r.vector_sems.at[0, stage],
            recv_sem=r.vector_sems.at[1, stage],
            device_id=partners[plan.links[stage]],
            device_id_type=MESH,
        )

    def vector_step(tick):
        count = len(plan.links)
        for stage in range(count + 1):

            @pl.when(tick == plan.vector_tick + stage * plan.vector_every)
            def _():
                if stage > 0:
                    vector_exchange(stage - 1).wait()
                    before = r.sums if stage == 1 else r.vector_land.at[stage - 2]
                    r.vector_land[stage - 1] += before[...]
                if stage < count:
                    vector_exchange(stage).start()

    pl.semaphore_wait(barrier, len(plan.links))

    def step(tick, carry):
        @pl.when(tick < plan.chunks)
        def _():
            produce(tick)
            for number in range(len(plan.parts)):
                begin(number, 0, tick)

        for stage in range(plan.stages):
            for number, part in enumerate(plan.parts):
                if stage < len(part.moves):
                    item = tick - part.due[stage]

                    @pl.when((item >= 0) & (item < plan.chunks))
                    def _():
                        settle(number, stage, item)

        vector_step(tick)
        run = {
            "ff": ff_job,
            "norm": norm_job,
            "mix": mix_job,
            "item": item_job,
            "pack": pack_job,
            "first": first_job,
            "input": input_job,
        }
        for name, (start, count) in plan.jobs.items():
            job = functools.partial(run[name], tick - start)
            pl.when((tick >= start) & (tick < start + count))(job)

        return carry

    lax.fori_loop(0, plan.ticks, step, 0)
    r.vector_out[...] = r.vector_land[len(plan.links) - 1]


def write_kernel(plan, tok, cot, whole, sums, *refs):
    outs, sems = refs[:-1], refs[-1]
    copies = [(tok, outs[0]), (cot, outs[1])]
    for (start, count, _, windows), out in zip(plan.phases, outs[2:6]):
        tall = count // windows
        for window in range(windows):
            first = start + window * tall
            cols = pl.ds(window * plan.width, plan.width)
            copies.append((whole.at[first : first + tall], out.at[:, :, cols]))
    copies = [
        pltpu.make_async_copy(source, target, sems.at[number])
        for number, (source, target) in enumerate(copies)
    ]
    for copy in copies:
        copy.start()
    own = lax.axis_index("narrow")
    for place in range(plan.narrow):

        @pl.when(own == place)
        def _():
            for row, out in enumerate(outs[6:14]):
                size = out.shape[0]
                out[...] = sums[row : row + 1, place * size : (place + 1) * size].reshape(size)
            size = outs[14].shape[0]
            row, start = 8 + place * size // plan.width, place * size % plan.width
            outs[14][...] = sums[row : row + 1, start : start + size].reshape(size)

    for copy in copies:
        copy.wait()


def shards(
    tokens,
    visible,
    first_gain,
    first_shift,
    joint_weight,
    query_bias,
    value_bias,
    mixer_weight,
    mixer_bias,
    second_gain,
    second_shift,
    expand_weight,
    expand_bias,
    shrink_weight,
    shrink_bias,
    cotangent,
):
    items, slots, width = tokens.shape
    ff = expand_weight.shape[1]
    narrow, wide = lax.axis_size("narrow"), lax.axis_size("wide")
    plan = Plan(narrow, wide, items, slots, width, ff)
    padded, chunk = plan.padded, plan.chunk
    hbm = pl.BlockSpec(memory_space=pl.ANY)
    vmem = pl.BlockSpec(memory_space=pltpu.VMEM)
    smem = pl.BlockSpec(memory_space=pltpu.SMEM)
    inputs = {
        "visible": (visible, smem),
        "g1": (first_gain, vmem),
        "s1": (first_shift, vmem),
        "qb": (query_bias, vmem),
        "vb": (value_bias, vmem),
        "mb": (mixer_bias, vmem),
        "g2": (second_gain, vmem),
        "s2": (second_shift, vmem),
        "sb": (shrink_bias, vmem),
        "eb": (expand_bias, vmem),
        "tok_in": (tokens, hbm),
        "cot_in": (cotangent, hbm),
        "jw_in": (joint_weight, hbm),
        "mw_in": (mixer_weight, hbm),
        "ew_in": (expand_weight, hbm),
        "sw_in": (shrink_weight, hbm),
    }
    block = width // narrow
    outputs = {
        "tok": (tokens.shape, BF16),
        "cot": (tokens.shape, BF16),
        "whole": ((plan.chunks, chunk, width), F32),
        "vector_out": ((plan.vector_rows, width), F32),
    }
    scratch = {
        "jw": pltpu.VMEM(joint_weight.shape, BF16),
        "mw": pltpu.VMEM(mixer_weight.shape, BF16),
        "ew": pltpu.VMEM(expand_weight.shape, BF16),
        "sw": pltpu.VMEM(shrink_weight.shape, BF16),
        "stage": pltpu.VMEM((padded, width), F32),
        "first_rows": pltpu.VMEM((padded, width), BF16),
        "mixed_rows": pltpu.VMEM((padded, width), BF16),
        "qkv": pltpu.VMEM((padded, 3 * width), F32),
        "attend": pltpu.VMEM((items * plan.pairs, 2 * slots, slots), F32),
        "first_t": pltpu.VMEM((width, padded), BF16),
        "mixed_t": pltpu.VMEM((width, padded), BF16),
        "second": pltpu.VMEM((padded, width), BF16),
        "second_t": pltpu.VMEM((width, padded), BF16),
        "middle": pltpu.VMEM((padded, width), F32),
        "grad_hidden": pltpu.VMEM((padded, ff), BF16),
        "active_t": pltpu.VMEM((ff, padded), BF16),
        "grad_out": pltpu.VMEM((padded, width), BF16),
        "acc_out": pltpu.VMEM((padded, width), F32),
        "acc_grad": pltpu.VMEM((padded, width), F32),
        "grad_branch": pltpu.VMEM((padded, width), BF16),
        "vec": pltpu.VMEM((plan.vector_rows, width), F32),
        "grad_logits": pltpu.VMEM((plan.pairs, 2 * slots, slots), BF16),
        "sums": pltpu.VMEM((plan.vector_rows, width), F32),
        "expand_sums": pltpu.VMEM((plan.ff_tiles, 1, TILE), F32),
        "vector_land": pltpu.VMEM((len(plan.links), plan.vector_rows, width), F32),
        "load_sems": pltpu.SemaphoreType.DMA((6,)),
        "vector_sems": pltpu.SemaphoreType.DMA((2, len(plan.links))),
        "send_sems": pltpu.SemaphoreType.DMA((plan.sends,)),
        "recv_sems": pltpu.SemaphoreType.DMA((plan.arrivals,)),
    }
    for number, part in enumerate(plan.parts):
        scratch[f"part{number}"] = pltpu.VMEM((2, narrow * chunk, part.columns), F32)
        for stage, move in enumerate(part.sums):
            scratch[f"land{number}_{stage}"] = pltpu.VMEM(
                (part.slots(stage), move.length, part.columns), F32
            )
    results = pl.pallas_call(
        functools.partial(layer_kernel, plan, (*inputs, *outputs, *scratch)),
        out_shape=[pltpu.VMEM(shape, kind) for shape, kind in outputs.values()],
        in_specs=[spec for _, spec in inputs.values()],
        out_specs=[vmem] * len(outputs),
        scratch_shapes=list(scratch.values()),
        compiler_params=pltpu.CompilerParams(
            has_side_effects=True, vmem_limit_bytes=52 * 2**20, collective_id=0
        ),
        name="layer",
    )(*(value for value, _ in inputs.values()))
    row_counts = [count // windows for _, count, _, windows in plan.phases]
    shapes = [jax.ShapeDtypeStruct(tokens.shape, BF16)] * 2
    shapes += [
        jax.ShapeDtypeStruct((tall, chunk, windows * width), F32)
        for tall, (_, _, _, windows) in zip(row_counts, plan.phases)
    ]
    shapes += [jax.ShapeDtypeStruct((block,), F32)] * 8
    shapes += [jax.ShapeDtypeStruct((ff // narrow,), F32)]
    copies = 2 + sum(windows for _, _, _, windows in plan.phases)
    outs = pl.pallas_call(
        functools.partial(write_kernel, plan),
        out_shape=shapes,
        in_specs=[vmem] * len(results),
        out_specs=[hbm] * 6 + [vmem] * 9,
        scratch_shapes=[pltpu.SemaphoreType.DMA((copies,))],
        compiler_params=pltpu.CompilerParams(vmem_limit_bytes=4 * 2**20),
        name="write",
    )(*(pltpu.with_memory_space_constraint(value, pltpu.VMEM) for value in results))
    input_grad, layer_out = outs[:2]
    shrink, expand, mixer, joint = (
        out.reshape(-1, out.shape[-1]) for out in outs[2:6]
    )
    vectors = outs[6:]
    return (
        layer_out,
        input_grad,
        vectors[0],
        vectors[1],
        joint,
        vectors[2],
        vectors[3],
        mixer,
        vectors[4],
        vectors[5],
        vectors[6],
        expand,
        vectors[8],
        shrink,
        vectors[7],
    )


def solution(mesh):
    return jax.shard_map(
        shards,
        mesh=mesh,
        in_specs=(
            P(("wide", "narrow"), None, None),
            P(("wide", "narrow")),
            P(),
            P(),
            P(),
            P(),
            P(),
            P(),
            P(),
            P(),
            P(),
            P(),
            P(),
            P(),
            P(),
            P(("wide", "narrow"), None, None),
        ),
        out_specs=(
            P(("wide", "narrow"), None, None),
            P(("wide", "narrow"), None, None),
            P("narrow"),
            P("narrow"),
            P("narrow", None),
            P("narrow"),
            P("narrow"),
            P("narrow", None),
            P("narrow"),
            P("narrow"),
            P("narrow"),
            P("narrow", None),
            P("narrow"),
            P("narrow", None),
            P("narrow"),
        ),
        check_vma=False,
    )
```

```python
import functools
import types

import jax
import jax.numpy as jnp
from jax import lax
from jax.experimental import pallas as pl
from jax.experimental.pallas import tpu as pltpu
from jax.sharding import PartitionSpec as P

HEAD_DIM = 64
EPSILON = 1e-06
SUB = 8
LAGS = ([1] + [2] * 15, [1] + [2] * 15)
MOST = 32
TILE = 256
U1 = 7
U2 = 7
U3 = 7
U4 = 7
U5 = 4
MESH = pl.DeviceIdType.MESH
ROOT_HALF = 0.5**0.5
PEAK = 0.3989422804014327
BF16 = jnp.bfloat16
F32 = jnp.float32


def bit_of(index, place):
    return lax.rem(lax.div(index, 2**place), 2)


def reversed_bits(value, count):
    out = 0
    for place in range(count):
        out = out * 2 + (value >> place) % 2
    return out


def aligned(start, size, unit):
    return pl.ds(pl.multiple_of(start, unit), size)


def matmul(left, right, contract=((1,), (0,))):
    return lax.dot_general(left, right, (contract, ((), ())), preferred_element_type=F32)


class Move:
    def __init__(self, kind, flips, length, select=None, inner=False):
        self.kind, self.flips, self.length = kind, flips, length
        self.select, self.inner = select, inner


class Part:
    def __init__(self, column, columns, picks, sums, gathers, selects):
        self.column, self.columns, self.picks = column, columns, picks
        self.sums, self.moves = sums, sums + gathers
        self.selects = selects
        self.lags = LAGS[column > 0][: len(self.moves)]
        self.due = [sum(self.lags[: stage + 1]) for stage in range(len(self.moves))]

    def flights(self, stage):
        return self.lags[stage] + 1

    def slots(self, stage):
        after = self.lags[stage + 1] if stage + 1 < len(self.sums) else 0
        count = 2 * self.lags[stage] + after + 2
        if self.moves[stage].kind in ("fold", "unfold"):
            kinds = [move.kind for move in self.moves]
            ahead = self.due[kinds.index("unfold")] - self.due[kinds.index("fold") - 1]
            count = max(count, ahead + 2)
        return count


class Plan:
    def __init__(self, narrow, wide, items, slots, width, ff):
        self.narrow, self.wide, self.width, self.ff = narrow, wide, width, ff
        self.items, self.slots = items, slots
        self.rows = items * slots
        self.padded = self.rows + -self.rows % 256
        self.pairs = width // (2 * HEAD_DIM)
        narrow_bits = self.narrow_bits = narrow.bit_length() - 1
        wide_bits = self.wide_bits = wide.bit_length() - 1
        rows = width // narrow
        chunk = SUB
        while rows % (2 * chunk) == 0 and chunk < MOST:
            chunk *= 2
        self.chunk = chunk
        near, mirror = (("wide", 1),), (("wide", 1), ("wide", 2))
        x, y, core = (("wide", 0),), (("narrow", 1),), (("narrow", 0),)
        if (narrow, wide) == (4, 8):
            self.links = (core, y, x, near, mirror)
            half = chunk // 2
            z_bit, x_bit, y_bit, core_bit = ("wide", 2), x[0], y[0], core[0]
            one = Part(
                0,
                width // 3 * 2,
                [(spot % 2 * 2 + spot // 2, 0, chunk) for spot in range(4)],
                [
                    Move("halve", core, 2 * chunk, core_bit),
                    Move("halve", y, chunk, y_bit),
                    Move("fold", near, chunk),
                    Move("halve", mirror, half, z_bit, True),
                    Move("add", x, half, inner=True),
                ],
                [
                    Move("double", mirror, half, inner=True),
                    Move("unfold", near, chunk),
                ],
                [(z_bit, half)],
            )
            two = Part(
                width // 3 * 2,
                width // 3,
                [
                    (2 * (spot % 2) + spot // 4, spot // 2 % 2 * half, half)
                    for spot in range(8)
                ],
                [
                    Move("halve", core, 2 * chunk, core_bit),
                    Move("halve", x, chunk, x_bit),
                    Move("halve", y, half, y_bit),
                    Move("fold", near, half),
                    Move("add", mirror, half, inner=True),
                ],
                [
                    Move("unfold", near, half),
                    Move("double", x, half),
                ],
                [(x_bit, half)],
            )
            self.parts = (one, two)
        else:
            self.links = tuple((("narrow", place),) for place in range(narrow_bits))
            self.links += tuple((("wide", place),) for place in range(wide_bits))
            sums, gathers, selects = [], [], []
            length = narrow * chunk
            for (axis, place), in self.links:
                if length > SUB:
                    length //= 2
                    sums.append(Move("halve", ((axis, place),), length, (axis, place)))
                    if axis == "wide":
                        selects.append(((axis, place), length))
                        gathers.insert(0, Move("double", ((axis, place),), length))
                else:
                    sums.append(Move("add", ((axis, place),), length))
            picks = [(reversed_bits(spot, narrow_bits), 0, chunk) for spot in range(narrow)]
            self.parts = (Part(0, width, picks, sums, gathers, selects),)
        self.stages = max(len(part.moves) for part in self.parts)
        self.depth = max(part.due[-1] for part in self.parts)
        self.arrivals, self.sends, self.arrival_at, self.send_at = 0, 0, {}, {}
        for number, part in enumerate(self.parts):
            for stage in range(len(part.moves)):
                self.arrival_at[number, stage] = self.arrivals
                self.send_at[number, stage] = self.sends
                self.arrivals += part.slots(stage)
                self.sends += part.flights(stage)
        self.phases = []
        start = 0
        for rows_block, windows in (
            (ff // narrow, 1),
            (rows, ff // width),
            (rows, 1),
            (rows, 3),
        ):
            count = rows_block // chunk * windows
            self.phases.append((start, count, rows_block, windows))
            start += count
        self.chunks = start
        self.ff_tiles = ff // TILE
        self.split = self.phases[1][0] // self.ff_tiles
        assert self.split in (1, 2)
        tall = ff // narrow
        self.groups = tall // TILE if tall % TILE == 0 else 1
        self.blocks = self.ff_tiles // self.groups
        self.jobs = {}
        tick = self.split - 1
        for name, count in (
            ("ff", self.ff_tiles * self.split),
            ("norm", 1 if self.split == 1 else 4),
            ("mix", 1 if self.split == 1 else 3),
            ("item", items * self.split),
            ("pack", 1 if self.split == 1 else 3),
            ("first", 1 if self.split == 1 else 3),
            ("input", 1 if self.split == 1 else 4),
        ):
            self.jobs[name] = (tick, count)
            tick += count
        self.vector_tick = tick
        assert self.phases[2][0] >= self.jobs["item"][0]
        assert self.phases[3][0] >= self.jobs["first"][0]
        self.vector_rows = 8 + ff // width
        self.vector_rows += -self.vector_rows % SUB
        self.ticks = self.chunks + self.depth
        self.vector_every = (self.ticks - 1 - self.vector_tick) // len(self.links)
        assert self.vector_every > 0


def layer_kernel(plan, names, *refs):
    r = types.SimpleNamespace(**dict(zip(names, refs)))
    width, chunk, narrow, slots = plan.width, plan.chunk, plan.narrow, plan.slots
    rows, padded, pairs = plan.rows, plan.padded, plan.pairs
    score_scale = HEAD_DIM ** (-0.5)
    spots = {"narrow": lax.axis_index("narrow"), "wide": lax.axis_index("wide")}
    inner = bit_of(spots["wide"], 1) != bit_of(spots["wide"], 2)
    outer = bit_of(spots["wide"], 1) == bit_of(spots["wide"], 2)

    bits = {
        (axis, place): bit_of(spots[axis], place)
        for axis, count in (("narrow", plan.narrow_bits), ("wide", plan.wide_bits))
        for place in range(count)
    }
    partners = {}
    for flips in plan.links:
        there = dict(spots)
        for axis, place in flips:
            there[axis] = there[axis] + (1 - 2 * bits[axis, place]) * 2**place
        partners[flips] = there

    loads = {}
    for number, name in enumerate(("tok", "jw", "mw", "ew", "cot", "sw")):
        loads[name] = pltpu.make_async_copy(
            getattr(r, name + "_in"), getattr(r, name), r.load_sems.at[number]
        )
    loads["tok"].start()
    loads["cot"].start()
    loads["jw"].start()

    barrier = pltpu.get_barrier_semaphore()
    for flips in plan.links:
        pl.semaphore_signal(barrier, inc=1, device_id=partners[flips], device_id_type=MESH)

    def vector(row):
        return r.vec[row : row + 1, :]

    def item_rows(item):
        return aligned(item * slots, slots, SUB)

    def row_live(item):
        return lax.broadcasted_iota(jnp.int32, (slots, 1), 0) < r.visible[item]

    lanes = lax.broadcasted_iota(jnp.int32, (slots, 2 * HEAD_DIM), 1)
    first_head = lanes < HEAD_DIM

    def both_heads(value):
        zero = jnp.zeros_like(value)
        return jnp.concatenate(
            [jnp.where(first_head, value, zero), jnp.where(first_head, zero, value)], axis=0
        ).astype(BF16)

    def one_head_each(value):
        return jnp.where(first_head, value[:slots], value[slots:])

    def normalized(values):
        center = values - jnp.mean(values, axis=-1, keepdims=True)
        spread = lax.rsqrt(jnp.mean(center * center, axis=-1, keepdims=True) + EPSILON)
        return center * spread, spread

    def norm_backward(grad, unit, spread):
        return spread * (
            grad
            - jnp.mean(grad, axis=-1, keepdims=True)
            - unit * jnp.mean(grad * unit, axis=-1, keepdims=True)
        )

    def each_item(body, unroll=1):
        lax.fori_loop(
            0, plan.items, lambda item, carry: (body(item), carry)[1], 0, unroll=unroll
        )

    def each_tile(count, body, unroll=1):
        lax.fori_loop(
            0, count, lambda tile, carry: (body(tile), carry)[1], 0, unroll=unroll
        )

    def pair_lanes(part, pair):
        start = part * width + pair * 2 * HEAD_DIM
        return slice(start, start + 2 * HEAD_DIM)

    small = (r.g1, r.s1, r.qb, r.vb, r.mb, r.g2, r.s2, r.sb)
    for row, ref in enumerate(small):
        r.vec[row : row + 1, :] = ref[...].astype(F32).reshape(1, width)
    for row in range(plan.ff // width):
        value = r.eb[row * width : (row + 1) * width].astype(F32)
        r.vec[8 + row : 9 + row, :] = value.reshape(1, width)
    r.stage[rows:, :] = jnp.zeros((padded - rows, width), F32)
    r.sums[...] = jnp.zeros_like(r.sums)
    loads["tok"].wait()

    def first_norm(item):
        unit, _ = normalized(r.tok[item].astype(F32))
        r.stage[item_rows(item), :] = unit * vector(0) + vector(1)

    each_item(first_norm, U1)
    r.first_rows[...] = r.stage[...].astype(BF16)
    for name in ("mw", "ew", "sw"):
        loads[name].start()
    loads["cot"].wait()

    def mask_cotangent(item):
        grad = r.cot[item].astype(F32)
        r.stage[item_rows(item), :] = jnp.where(row_live(item), grad, 0.0)

    each_item(mask_cotangent, U3)
    r.grad_out[...] = r.stage[...].astype(BF16)
    loads["jw"].wait()
    for part, bias in enumerate((2, None, 3)):

        cols = slice(part * width, (part + 1) * width)
        value = matmul(r.first_rows[...], r.jw[:, cols])
        if bias is not None:
            value = value + vector(bias)
        r.qkv[:, cols] = value.astype(BF16).astype(F32)
    r.qkv[rows:, :] = jnp.zeros((padded - rows, 3 * width), F32)

    def attend_item(item):
        here = item_rows(item)
        key_live = (
            lax.broadcasted_iota(jnp.int32, (2 * slots, slots), 1) < r.visible[item]
        )
        every = range(pairs)
        queries = [both_heads(r.qkv[here, pair_lanes(0, pair)]) for pair in every]
        keys = [r.qkv[here, pair_lanes(1, pair)].astype(BF16) for pair in every]
        values = [r.qkv[here, pair_lanes(2, pair)].astype(BF16) for pair in every]
        logits = [matmul(queries[pair], keys[pair], ((1,), (1,))) for pair in every]
        logits = [jnp.where(key_live, value * score_scale, -1000000000.0) for value in logits]
        tops = [jnp.max(value, axis=-1, keepdims=True) for value in logits]
        expos = [jnp.exp(logits[pair] - tops[pair]) for pair in every]
        totals = [jnp.sum(value, axis=-1, keepdims=True) for value in expos]
        attends = [expos[pair] * (1.0 / totals[pair]) for pair in every]
        mixed = [matmul(attends[pair].astype(BF16), values[pair]) for pair in every]
        for pair in every:
            r.attend[item * pairs + pair] = attends[pair]
            r.stage[here, pair_lanes(0, pair)] = one_head_each(mixed[pair])

    each_item(attend_item, U4)
    r.mixed_rows[...] = r.stage[...].astype(BF16)
    loads["mw"].wait()

    r.middle[...] = matmul(r.mixed_rows[...], r.mw[...]) + vector(4)

    def second_norm(item):
        here = item_rows(item)
        middle = r.middle[here, :] + r.tok[item].astype(F32)
        r.middle[here, :] = middle
        unit, _ = normalized(middle)
        r.stage[here, :] = unit * vector(5) + vector(6)

    each_item(second_norm, U2)
    r.second[...] = r.stage[...].astype(BF16)
    loads["ew"].wait()

    def expand_bias(tile):
        per_row = width // TILE
        return r.vec[
            pl.ds(8 + lax.div(tile, per_row), 1),
            aligned(lax.rem(tile, per_row) * TILE, TILE, TILE),
        ]

    def hidden_tile(tile):
        cols = aligned(tile * TILE, TILE, TILE)
        hidden = matmul(r.second[...], r.ew[:, cols]) + expand_bias(tile)
        return hidden, 0.5 + 0.5 * lax.erf(hidden * ROOT_HALF)

    def expand_tile(place):
        tile = place * plan.groups
        hidden, normal = hidden_tile(tile)
        r.active_t[aligned(tile * TILE, TILE, TILE), :] = (hidden * normal).astype(BF16).T

    each_tile(plan.blocks, expand_tile, U5)
    loads["sw"].wait()

    rows_full = rows // 16 * 16

    def share(name, count, turn, body):
        size = -(-count // plan.jobs[name][1])
        first = turn * size
        last = jnp.minimum(first + size, count)
        lax.fori_loop(first, last, lambda place, carry: (body(place), carry)[1], 0)

    def in_turns(turn, first_half, second_half):
        number = lax.div(turn, plan.split)
        if plan.split == 1:
            first_half(number)
            second_half(number)
        else:
            half = lax.rem(turn, plan.split)
            pl.when(half == 0)(lambda: first_half(number))
            pl.when(half == 1)(lambda: second_half(number))

    def ff_job(turn):
        def tile_job(number):
            group = lax.rem(lax.div(number, plan.blocks) + 1, plan.groups)
            tile = lax.rem(number, plan.blocks) * plan.groups + group
            cols = aligned(tile * TILE, TILE, TILE)
            hidden, normal = hidden_tile(tile)
            active = (hidden * normal).astype(BF16)
            r.active_t[cols, :] = active.T
            slope = normal + hidden * (PEAK * jnp.exp(-0.5 * hidden * hidden))
            grad = matmul(r.grad_out[...], r.sw[cols, :], ((1,), (1,)))
            grad_hidden = (grad * slope).astype(BF16)
            r.grad_hidden[:, cols] = grad_hidden
            r.expand_sums[tile] = jnp.sum(grad_hidden.astype(F32), axis=0, keepdims=True)
            r.acc_out[...] += matmul(active, r.sw[cols, :])
            r.acc_grad[...] += matmul(grad_hidden, r.ew[:, cols], ((1,), (1,)))

        in_turns(turn, tile_job, turn_rows)

    def turn_rows(turn):
        for place, (rows_ref, turned) in enumerate(
            (
                (r.second, r.second_t),
                (r.mixed_rows, r.mixed_t),
                (r.first_rows, r.first_t),
            )
        ):

            @pl.when(turn == place)
            def _():
                turned[...] = rows_ref[...].T

    def norm_job(turn):
        def one(item):
            here = item_rows(item)
            live = row_live(item)
            middle = r.middle[here, :]
            grad_out = jnp.where(live, r.cot[item].astype(F32), 0.0)
            layer_out = jnp.where(live, middle + (r.acc_out[here, :] + vector(7)), 0.0)
            r.cot[item] = layer_out.astype(BF16)
            unit, spread = normalized(middle)
            grad = r.acc_grad[here, :]
            r.sums[5:6, :] += jnp.sum(grad * unit, axis=0, keepdims=True)
            r.sums[6:7, :] += jnp.sum(grad, axis=0, keepdims=True)
            r.sums[7:8, :] += jnp.sum(grad_out, axis=0, keepdims=True)
            grad_middle = grad_out + norm_backward(grad * vector(5), unit, spread)
            r.acc_out[here, :] = grad_middle
            r.sums[4:5, :] += jnp.sum(
                grad_middle.astype(BF16).astype(F32), axis=0, keepdims=True
            )

        share("norm", plan.items, turn, one)

    def mix_job(turn):
        pl.when(turn == 0)(pack_branch)

        def one(tile):
            cols = aligned(tile * TILE, TILE, TILE)
            value = matmul(r.grad_branch[...], r.mw[cols, :], ((1,), (1,)))
            r.stage[:, cols] = value.astype(BF16).astype(F32)

        share("mix", width // TILE, turn, one)

    def pack_branch():
        r.grad_branch[:rows_full, :] = r.acc_out[:rows_full, :].astype(BF16)
        tail = jnp.concatenate(
            [r.acc_out[rows_full:rows, :], jnp.zeros((padded - rows, width), F32)], axis=0
        )
        r.grad_branch[rows_full:, :] = tail.astype(BF16)

    def item_job(turn):
        def scores(item):
            here = item_rows(item)
            for pair in range(pairs):
                values = r.qkv[here, pair_lanes(2, pair)].astype(BF16)
                grad_mixed = both_heads(r.stage[here, pair_lanes(0, pair)])
                attend = r.attend[item * pairs + pair]
                grad_attend = matmul(grad_mixed, values, ((1,), (1,)))
                inner_sum = jnp.sum(attend * grad_attend, axis=-1, keepdims=True)
                r.grad_logits[pair] = (attend * (grad_attend - inner_sum)).astype(BF16)
                r.qkv[here, pair_lanes(2, pair)] = matmul(
                    attend.astype(BF16), grad_mixed, ((0,), (0,))
                )

        def inputs(item):
            here = item_rows(item)
            for pair in range(pairs):
                query = both_heads(r.qkv[here, pair_lanes(0, pair)])
                keys = r.qkv[here, pair_lanes(1, pair)].astype(BF16)
                grad_logits = r.grad_logits[pair]
                grad_query = one_head_each(matmul(grad_logits, keys)) * score_scale
                grad_key = matmul(grad_logits, query, ((0,), (0,))) * score_scale
                r.qkv[here, pair_lanes(0, pair)] = grad_query
                r.qkv[here, pair_lanes(1, pair)] = grad_key

        in_turns(turn, scores, inputs)

    def joint_rows(part):
        return slice(part * padded, (part + 1) * padded)

    def pack_job(turn):
        for part in range(3):

            @pl.when(turn == part * (plan.jobs["pack"][1] > 1))
            def _():
                value = r.qkv[:, part * width : (part + 1) * width].astype(BF16)
                r.sw[joint_rows(part), :] = value
                if part != 1:
                    row = 2 if part == 0 else 3
                    r.sums[row : row + 1, :] = jnp.sum(value.astype(F32), axis=0, keepdims=True)

    def first_job(turn):
        def one(tile):
            cols = aligned(tile * TILE, TILE, TILE)
            total = None
            for part in range(3):
                value = matmul(
                    r.sw[joint_rows(part), :],
                    r.jw[cols, part * width : (part + 1) * width],
                    ((1,), (1,)),
                )
                total = value if total is None else total + value
            r.acc_grad[:, cols] = total

        share("first", width // TILE, turn, one)

    def input_job(turn):
        def one(item):
            here = item_rows(item)
            unit, spread = normalized(r.tok[item].astype(F32))
            grad = r.acc_grad[here, :]
            r.sums[0:1, :] += jnp.sum(grad * unit, axis=0, keepdims=True)
            r.sums[1:2, :] += jnp.sum(grad, axis=0, keepdims=True)
            total = r.acc_out[here, :] + norm_backward(grad * vector(0), unit, spread)
            r.tok[item] = total.astype(BF16)

        share("input", plan.items, turn, one)

        @pl.when(turn == 0)
        def _():
            per_row = width // TILE
            for tile in range(plan.ff_tiles):
                row, start = 8 + tile // per_row, tile % per_row * TILE
                r.sums[row : row + 1, start : start + TILE] = r.expand_sums[tile]

    def when(condition, action):
        if condition is True:
            action()
        else:
            pl.when(condition)(action)

    def roles(move):
        if move.kind == "fold":
            return outer, inner
        if move.kind == "unfold":
            return inner, outer
        return (inner, inner) if move.inner else (True, True)

    def land(number, stage, item):
        ref = getattr(r, f"land{number}_{stage}")
        return ref.at[lax.rem(item, plan.parts[number].slots(stage))]

    def source(number, stage, item):
        if stage == 0:
            return getattr(r, f"part{number}").at[lax.rem(item, 2)]
        return land(number, stage - 1, item)

    kept, given, regions = {}, {}, {}
    for number, part in enumerate(plan.parts):
        for stage, move in enumerate(part.moves):
            bit = bits[move.select] if move.select else 0
            kept[number, stage] = bit * move.length
            given[number, stage] = (1 - bit) * move.length if move.select else 0
            regions[number, stage] = sum(
                bits[select] * size for select, size in part.selects if size >= move.length
            )

    def in_whole(number, stage, item):
        part = plan.parts[number]
        return (
            item,
            aligned(regions[number, stage], part.moves[stage].length, SUB),
            pl.ds(part.column, part.columns),
        )

    def transfer(number, stage, item):
        part = plan.parts[number]
        move = part.moves[stage]
        arrival = plan.arrival_at[number, stage] + lax.rem(item, part.slots(stage))
        send = plan.send_at[number, stage] + lax.rem(item, part.flights(stage))
        if stage < len(part.sums):
            src = source(number, stage, item).at[
                aligned(given[number, stage], move.length, SUB)
            ]
            dst = land(number, stage, item)
        else:
            src = r.whole.at[in_whole(number, stage, item)]
            dst = src
        return pltpu.make_async_remote_copy(
            src_ref=src,
            dst_ref=dst,
            send_sem=r.send_sems.at[send],
            recv_sem=r.recv_sems.at[arrival],
            device_id=partners[move.flips],
            device_id_type=MESH,
        )

    def begin(number, stage, item):
        sender, _ = roles(plan.parts[number].moves[stage])
        when(sender, lambda: transfer(number, stage, item).start())

    def settle(number, stage, item):
        part = plan.parts[number]
        move = part.moves[stage]
        sender, receiver = roles(move)

        def receive():
            if stage < len(part.sums):
                land(number, stage, item)[...] += source(number, stage, item)[
                    aligned(kept[number, stage], move.length, SUB)
                ]
            if stage == len(part.sums) - 1:
                r.whole[in_whole(number, stage, item)] = land(number, stage, item)[...]

        if move.kind in ("fold", "unfold"):
            when(sender, lambda: transfer(number, stage, item).wait_send())

            def arrive():
                transfer(number, stage, item).wait_recv()
                receive()

        else:

            def arrive():
                transfer(number, stage, item).wait()
                receive()

        when(receiver, arrive)
        if stage + 1 < len(part.moves):
            begin(number, stage + 1, item)

    def rows_of(phase):
        _, count, _, windows = plan.phases[phase]
        return count // windows

    def produce(item):
        slot = lax.rem(item, 2)
        lefts = (r.active_t, r.second_t, r.mixed_t, r.first_t)
        rights = (r.grad_out, r.grad_hidden, r.grad_branch, r.sw)
        for phase, (start, count, rows_block, windows) in enumerate(plan.phases):
            left, right = lefts[phase], rights[phase]

            @pl.when((item >= start) & (item < start + count))
            def _():
                local = item - start
                tall = rows_of(phase)
                row = lax.rem(local, tall) * chunk
                window = lax.div(local, tall)
                for number, part in enumerate(plan.parts):
                    picked = [
                        left[aligned(block * rows_block + row + offset, size, size), :]
                        for block, offset, size in part.picks
                    ]
                    if phase == 3:
                        other = right[
                            aligned(window * padded, padded, 256),
                            part.column : part.column + part.columns,
                        ]
                    else:
                        other = right[
                            :, aligned(window * width + part.column, part.columns, 128)
                        ]
                    getattr(r, f"part{number}")[slot] = matmul(
                        jnp.concatenate(picked, axis=0), other
                    )

    def vector_exchange(stage):
        return pltpu.make_async_remote_copy(
            src_ref=r.sums if stage == 0 else r.vector_land.at[stage - 1],
            dst_ref=r.vector_land.at[stage],
            send_sem=r.vector_sems.at[0, stage],
            recv_sem=r.vector_sems.at[1, stage],
            device_id=partners[plan.links[stage]],
            device_id_type=MESH,
        )

    def vector_step(tick):
        count = len(plan.links)
        for stage in range(count + 1):

            @pl.when(tick == plan.vector_tick + stage * plan.vector_every)
            def _():
                if stage > 0:
                    vector_exchange(stage - 1).wait()
                    before = r.sums if stage == 1 else r.vector_land.at[stage - 2]
                    r.vector_land[stage - 1] += before[...]
                if stage < count:
                    vector_exchange(stage).start()

    pl.semaphore_wait(barrier, len(plan.links))

    def step(tick, carry):
        @pl.when(tick < plan.chunks)
        def _():
            produce(tick)
            for number in range(len(plan.parts)):
                begin(number, 0, tick)

        for stage in range(plan.stages):
            for number, part in enumerate(plan.parts):
                if stage < len(part.moves):
                    item = tick - part.due[stage]

                    @pl.when((item >= 0) & (item < plan.chunks))
                    def _():
                        settle(number, stage, item)

        vector_step(tick)
        @pl.when(tick == 0)
        def _():
            for ref in (r.acc_out, r.acc_grad):
                ref[...] = jnp.zeros_like(ref)

        run = {
            "ff": ff_job,
            "norm": norm_job,
            "mix": mix_job,
            "item": item_job,
            "pack": pack_job,
            "first": first_job,
            "input": input_job,
        }
        for name, (start, count) in plan.jobs.items():
            job = functools.partial(run[name], tick - start)
            pl.when((tick >= start) & (tick < start + count))(job)

        return carry

    lax.fori_loop(0, plan.ticks, step, 0)
    r.vector_out[...] = r.vector_land[len(plan.links) - 1]


def write_kernel(plan, tok, cot, whole, sums, *refs):
    outs, sems = refs[:-1], refs[-1]
    copies = [(tok, outs[0]), (cot, outs[1])]
    for (start, count, _, windows), out in zip(plan.phases, outs[2:6]):
        tall = count // windows
        for window in range(windows):
            first = start + window * tall
            cols = pl.ds(window * plan.width, plan.width)
            copies.append((whole.at[first : first + tall], out.at[:, :, cols]))
    copies = [
        pltpu.make_async_copy(source, target, sems.at[number])
        for number, (source, target) in enumerate(copies)
    ]
    for copy in copies:
        copy.start()
    own = lax.axis_index("narrow")
    for place in range(plan.narrow):

        @pl.when(own == place)
        def _():
            for row, out in enumerate(outs[6:14]):
                size = out.shape[0]
                out[...] = sums[row : row + 1, place * size : (place + 1) * size].reshape(size)
            size = outs[14].shape[0]
            row, start = 8 + place * size // plan.width, place * size % plan.width
            outs[14][...] = sums[row : row + 1, start : start + size].reshape(size)

    for copy in copies:
        copy.wait()


def shards(
    tokens,
    visible,
    first_gain,
    first_shift,
    joint_weight,
    query_bias,
    value_bias,
    mixer_weight,
    mixer_bias,
    second_gain,
    second_shift,
    expand_weight,
    expand_bias,
    shrink_weight,
    shrink_bias,
    cotangent,
):
    items, slots, width = tokens.shape
    ff = expand_weight.shape[1]
    narrow, wide = lax.axis_size("narrow"), lax.axis_size("wide")
    plan = Plan(narrow, wide, items, slots, width, ff)
    padded, chunk = plan.padded, plan.chunk
    hbm = pl.BlockSpec(memory_space=pl.ANY)
    vmem = pl.BlockSpec(memory_space=pltpu.VMEM)
    smem = pl.BlockSpec(memory_space=pltpu.SMEM)
    inputs = {
        "visible": (visible, smem),
        "g1": (first_gain, vmem),
        "s1": (first_shift, vmem),
        "qb": (query_bias, vmem),
        "vb": (value_bias, vmem),
        "mb": (mixer_bias, vmem),
        "g2": (second_gain, vmem),
        "s2": (second_shift, vmem),
        "sb": (shrink_bias, vmem),
        "eb": (expand_bias, vmem),
        "tok_in": (tokens, hbm),
        "cot_in": (cotangent, hbm),
        "jw_in": (joint_weight, hbm),
        "mw_in": (mixer_weight, hbm),
        "ew_in": (expand_weight, hbm),
        "sw_in": (shrink_weight, hbm),
    }
    block = width // narrow
    outputs = {
        "tok": (tokens.shape, BF16),
        "cot": (tokens.shape, BF16),
        "whole": ((plan.chunks, chunk, width), F32),
        "vector_out": ((plan.vector_rows, width), F32),
    }
    scratch = {
        "jw": pltpu.VMEM(joint_weight.shape, BF16),
        "mw": pltpu.VMEM(mixer_weight.shape, BF16),
        "ew": pltpu.VMEM(expand_weight.shape, BF16),
        "sw": pltpu.VMEM(shrink_weight.shape, BF16),
        "stage": pltpu.VMEM((padded, width), F32),
        "first_rows": pltpu.VMEM((padded, width), BF16),
        "mixed_rows": pltpu.VMEM((padded, width), BF16),
        "qkv": pltpu.VMEM((padded, 3 * width), F32),
        "attend": pltpu.VMEM((items * plan.pairs, 2 * slots, slots), F32),
        "first_t": pltpu.VMEM((width, padded), BF16),
        "mixed_t": pltpu.VMEM((width, padded), BF16),
        "second": pltpu.VMEM((padded, width), BF16),
        "second_t": pltpu.VMEM((width, padded), BF16),
        "middle": pltpu.VMEM((padded, width), F32),
        "grad_hidden": pltpu.VMEM((padded, ff), BF16),
        "active_t": pltpu.VMEM((ff, padded), BF16),
        "grad_out": pltpu.VMEM((padded, width), BF16),
        "acc_out": pltpu.VMEM((padded, width), F32),
        "acc_grad": pltpu.VMEM((padded, width), F32),
        "grad_branch": pltpu.VMEM((padded, width), BF16),
        "vec": pltpu.VMEM((plan.vector_rows, width), F32),
        "grad_logits": pltpu.VMEM((plan.pairs, 2 * slots, slots), BF16),
        "sums": pltpu.VMEM((plan.vector_rows, width), F32),
        "expand_sums": pltpu.VMEM((plan.ff_tiles, 1, TILE), F32),
        "vector_land": pltpu.VMEM((len(plan.links), plan.vector_rows, width), F32),
        "load_sems": pltpu.SemaphoreType.DMA((6,)),
        "vector_sems": pltpu.SemaphoreType.DMA((2, len(plan.links))),
        "send_sems": pltpu.SemaphoreType.DMA((plan.sends,)),
        "recv_sems": pltpu.SemaphoreType.DMA((plan.arrivals,)),
    }
    for number, part in enumerate(plan.parts):
        scratch[f"part{number}"] = pltpu.VMEM((2, narrow * chunk, part.columns), F32)
        for stage, move in enumerate(part.sums):
            scratch[f"land{number}_{stage}"] = pltpu.VMEM(
                (part.slots(stage), move.length, part.columns), F32
            )
    results = pl.pallas_call(
        functools.partial(layer_kernel, plan, (*inputs, *outputs, *scratch)),
        out_shape=[pltpu.VMEM(shape, kind) for shape, kind in outputs.values()],
        in_specs=[spec for _, spec in inputs.values()],
        out_specs=[vmem] * len(outputs),
        scratch_shapes=list(scratch.values()),
        compiler_params=pltpu.CompilerParams(
            has_side_effects=True, vmem_limit_bytes=52 * 2**20, collective_id=0
        ),
        name="layer",
    )(*(value for value, _ in inputs.values()))
    row_counts = [count // windows for _, count, _, windows in plan.phases]
    shapes = [jax.ShapeDtypeStruct(tokens.shape, BF16)] * 2
    shapes += [
        jax.ShapeDtypeStruct((tall, chunk, windows * width), F32)
        for tall, (_, _, _, windows) in zip(row_counts, plan.phases)
    ]
    shapes += [jax.ShapeDtypeStruct((block,), F32)] * 8
    shapes += [jax.ShapeDtypeStruct((ff // narrow,), F32)]
    copies = 2 + sum(windows for _, _, _, windows in plan.phases)
    outs = pl.pallas_call(
        functools.partial(write_kernel, plan),
        out_shape=shapes,
        in_specs=[vmem] * len(results),
        out_specs=[hbm] * 6 + [vmem] * 9,
        scratch_shapes=[pltpu.SemaphoreType.DMA((copies,))],
        compiler_params=pltpu.CompilerParams(vmem_limit_bytes=4 * 2**20),
        name="write",
    )(*(pltpu.with_memory_space_constraint(value, pltpu.VMEM) for value in results))
    input_grad, layer_out = outs[:2]
    shrink, expand, mixer, joint = (
        out.reshape(-1, out.shape[-1]) for out in outs[2:6]
    )
    vectors = outs[6:]
    return (
        layer_out,
        input_grad,
        vectors[0],
        vectors[1],
        joint,
        vectors[2],
        vectors[3],
        mixer,
        vectors[4],
        vectors[5],
        vectors[6],
        expand,
        vectors[8],
        shrink,
        vectors[7],
    )


def solution(mesh):
    return jax.shard_map(
        shards,
        mesh=mesh,
        in_specs=(
            P(("wide", "narrow"), None, None),
            P(("wide", "narrow")),
            P(),
            P(),
            P(),
            P(),
            P(),
            P(),
            P(),
            P(),
            P(),
            P(),
            P(),
            P(),
            P(),
            P(("wide", "narrow"), None, None),
        ),
        out_specs=(
            P(("wide", "narrow"), None, None),
            P(("wide", "narrow"), None, None),
            P("narrow"),
            P("narrow"),
            P("narrow", None),
            P("narrow"),
            P("narrow"),
            P("narrow", None),
            P("narrow"),
            P("narrow"),
            P("narrow"),
            P("narrow", None),
            P("narrow"),
            P("narrow", None),
            P("narrow"),
        ),
        check_vma=False,
    )
```

```python
import functools
import types

import jax
import jax.numpy as jnp
from jax import lax
from jax.experimental import pallas as pl
from jax.experimental.pallas import tpu as pltpu
from jax.sharding import PartitionSpec as P

HEAD_DIM = 64
EPSILON = 1e-06
SUB = 8
LAGS = ([1] + [2] * 15, [1] + [2] * 15)
MOST = 32
TILE = 256
U1 = 7
U2 = 7
U3 = 7
U4 = 7
U5 = 4
MESH = pl.DeviceIdType.MESH
ROOT_HALF = 0.5**0.5
PEAK = 0.3989422804014327
BF16 = jnp.bfloat16
F32 = jnp.float32


def bit_of(index, place):
    return lax.rem(lax.div(index, 2**place), 2)


def reversed_bits(value, count):
    out = 0
    for place in range(count):
        out = out * 2 + (value >> place) % 2
    return out


def aligned(start, size, unit):
    return pl.ds(pl.multiple_of(start, unit), size)


def matmul(left, right, contract=((1,), (0,))):
    return lax.dot_general(left, right, (contract, ((), ())), preferred_element_type=F32)


class Move:
    def __init__(self, kind, flips, length, select=None, inner=False):
        self.kind, self.flips, self.length = kind, flips, length
        self.select, self.inner = select, inner


class Part:
    def __init__(self, column, columns, picks, sums, gathers, selects):
        self.column, self.columns, self.picks = column, columns, picks
        self.sums, self.moves = sums, sums + gathers
        self.selects = selects
        self.lags = LAGS[column > 0][: len(self.moves)]
        self.due = [sum(self.lags[: stage + 1]) for stage in range(len(self.moves))]

    def flights(self, stage):
        return self.lags[stage] + 1

    def slots(self, stage):
        after = self.lags[stage + 1] if stage + 1 < len(self.sums) else 0
        count = 2 * self.lags[stage] + after + 2
        if self.moves[stage].kind in ("fold", "unfold"):
            kinds = [move.kind for move in self.moves]
            ahead = self.due[kinds.index("unfold")] - self.due[kinds.index("fold") - 1]
            count = max(count, ahead + 2)
        return count


class Plan:
    def __init__(self, narrow, wide, items, slots, width, ff):
        self.narrow, self.wide, self.width, self.ff = narrow, wide, width, ff
        self.items, self.slots = items, slots
        self.rows = items * slots
        self.padded = self.rows + -self.rows % 256
        self.pairs = width // (2 * HEAD_DIM)
        narrow_bits = self.narrow_bits = narrow.bit_length() - 1
        wide_bits = self.wide_bits = wide.bit_length() - 1
        rows = width // narrow
        chunk = SUB
        while rows % (2 * chunk) == 0 and chunk < MOST:
            chunk *= 2
        self.chunk = chunk
        near, mirror = (("wide", 1),), (("wide", 1), ("wide", 2))
        x, y, core = (("wide", 0),), (("narrow", 1),), (("narrow", 0),)
        if (narrow, wide) == (4, 8):
            self.links = (core, y, x, near, mirror)
            half = chunk // 2
            z_bit, x_bit, y_bit, core_bit = ("wide", 2), x[0], y[0], core[0]
            one = Part(
                0,
                width // 3 * 2,
                [(spot % 2 * 2 + spot // 2, 0, chunk) for spot in range(4)],
                [
                    Move("halve", core, 2 * chunk, core_bit),
                    Move("halve", y, chunk, y_bit),
                    Move("fold", near, chunk),
                    Move("halve", mirror, half, z_bit, True),
                    Move("add", x, half, inner=True),
                ],
                [
                    Move("double", mirror, half, inner=True),
                    Move("unfold", near, chunk),
                ],
                [(z_bit, half)],
            )
            two = Part(
                width // 3 * 2,
                width // 3,
                [
                    (2 * (spot % 2) + spot // 4, spot // 2 % 2 * half, half)
                    for spot in range(8)
                ],
                [
                    Move("halve", core, 2 * chunk, core_bit),
                    Move("halve", x, chunk, x_bit),
                    Move("halve", y, half, y_bit),
                    Move("fold", near, half),
                    Move("add", mirror, half, inner=True),
                ],
                [
                    Move("unfold", near, half),
                    Move("double", x, half),
                ],
                [(x_bit, half)],
            )
            self.parts = (one, two)
        else:
            self.links = tuple((("narrow", place),) for place in range(narrow_bits))
            self.links += tuple((("wide", place),) for place in range(wide_bits))
            sums, gathers, selects = [], [], []
            length = narrow * chunk
            for (axis, place), in self.links:
                if length > SUB:
                    length //= 2
                    sums.append(Move("halve", ((axis, place),), length, (axis, place)))
                    if axis == "wide":
                        selects.append(((axis, place), length))
                        gathers.insert(0, Move("double", ((axis, place),), length))
                else:
                    sums.append(Move("add", ((axis, place),), length))
            picks = [(reversed_bits(spot, narrow_bits), 0, chunk) for spot in range(narrow)]
            self.parts = (Part(0, width, picks, sums, gathers, selects),)
        self.stages = max(len(part.moves) for part in self.parts)
        self.depth = max(part.due[-1] for part in self.parts)
        self.arrivals, self.sends, self.arrival_at, self.send_at = 0, 0, {}, {}
        for number, part in enumerate(self.parts):
            for stage in range(len(part.moves)):
                self.arrival_at[number, stage] = self.arrivals
                self.send_at[number, stage] = self.sends
                self.arrivals += part.slots(stage)
                self.sends += part.flights(stage)
        self.phases = []
        start = 0
        for rows_block, windows in (
            (ff // narrow, 1),
            (rows, ff // width),
            (rows, 1),
            (rows, 3),
        ):
            count = rows_block // chunk * windows
            self.phases.append((start, count, rows_block, windows))
            start += count
        self.chunks = start
        self.ff_tiles = ff // TILE
        self.split = self.phases[1][0] // self.ff_tiles
        assert self.split in (1, 2)
        tall = ff // narrow
        self.groups = tall // TILE if tall % TILE == 0 else 1
        self.blocks = self.ff_tiles // self.groups
        self.jobs = {}
        tick = self.split - 1
        for name, count in (
            ("ff", self.ff_tiles * self.split),
            ("norm", 1 if self.split == 1 else 4),
            ("mix", 1 if self.split == 1 else 3),
            ("item", items * self.split),
            ("pack", 1 if self.split == 1 else 3),
            ("first", 1 if self.split == 1 else 3),
            ("input", 1 if self.split == 1 else 4),
        ):
            self.jobs[name] = (tick, count)
            tick += count
        self.vector_tick = tick
        assert self.phases[2][0] >= self.jobs["item"][0]
        assert self.phases[3][0] >= self.jobs["first"][0]
        self.block = rows
        self.block_lanes = rows + -rows % 128
        self.block_order = [reversed_bits(spot, narrow_bits) for spot in range(narrow)]
        self.vector_rows = 8 + ff // width
        self.vector_rows += -self.vector_rows % SUB
        self.ticks = self.chunks + self.depth
        self.vector_lengths = [narrow * self.vector_rows]
        for flips in self.links:
            length = self.vector_lengths[-1]
            self.vector_lengths.append(length // 2 if flips[0][0] == "narrow" else length)
        self.vector_every = (self.ticks - 1 - self.vector_tick) // len(self.links)
        assert self.vector_every > 0


def layer_kernel(plan, names, *refs):
    r = types.SimpleNamespace(**dict(zip(names, refs)))
    width, chunk, narrow, slots = plan.width, plan.chunk, plan.narrow, plan.slots
    rows, padded, pairs = plan.rows, plan.padded, plan.pairs
    score_scale = HEAD_DIM ** (-0.5)
    spots = {"narrow": lax.axis_index("narrow"), "wide": lax.axis_index("wide")}
    inner = bit_of(spots["wide"], 1) != bit_of(spots["wide"], 2)
    outer = bit_of(spots["wide"], 1) == bit_of(spots["wide"], 2)

    bits = {
        (axis, place): bit_of(spots[axis], place)
        for axis, count in (("narrow", plan.narrow_bits), ("wide", plan.wide_bits))
        for place in range(count)
    }
    partners = {}
    for flips in plan.links:
        there = dict(spots)
        for axis, place in flips:
            there[axis] = there[axis] + (1 - 2 * bits[axis, place]) * 2**place
        partners[flips] = there

    loads = {}
    for number, name in enumerate(("tok", "jw", "mw", "ew", "cot", "sw")):
        loads[name] = pltpu.make_async_copy(
            getattr(r, name + "_in"), getattr(r, name), r.load_sems.at[number]
        )
    loads["tok"].start()
    loads["cot"].start()
    loads["jw"].start()

    barrier = pltpu.get_barrier_semaphore()
    for flips in plan.links:
        pl.semaphore_signal(barrier, inc=1, device_id=partners[flips], device_id_type=MESH)

    def vector(row):
        return r.vec[row : row + 1, :]

    def item_rows(item):
        return aligned(item * slots, slots, SUB)

    def row_live(item):
        return lax.broadcasted_iota(jnp.int32, (slots, 1), 0) < r.visible[item]

    lanes = lax.broadcasted_iota(jnp.int32, (slots, 2 * HEAD_DIM), 1)
    first_head = lanes < HEAD_DIM

    def both_heads(value):
        zero = jnp.zeros_like(value)
        return jnp.concatenate(
            [jnp.where(first_head, value, zero), jnp.where(first_head, zero, value)], axis=0
        ).astype(BF16)

    def one_head_each(value):
        return jnp.where(first_head, value[:slots], value[slots:])

    def normalized(values):
        center = values - jnp.mean(values, axis=-1, keepdims=True)
        spread = lax.rsqrt(jnp.mean(center * center, axis=-1, keepdims=True) + EPSILON)
        return center * spread, spread

    def norm_backward(grad, unit, spread):
        return spread * (
            grad
            - jnp.mean(grad, axis=-1, keepdims=True)
            - unit * jnp.mean(grad * unit, axis=-1, keepdims=True)
        )

    def each_item(body, unroll=1):
        lax.fori_loop(
            0, plan.items, lambda item, carry: (body(item), carry)[1], 0, unroll=unroll
        )

    def each_tile(count, body, unroll=1):
        lax.fori_loop(
            0, count, lambda tile, carry: (body(tile), carry)[1], 0, unroll=unroll
        )

    def pair_lanes(part, pair):
        start = part * width + pair * 2 * HEAD_DIM
        return slice(start, start + 2 * HEAD_DIM)

    small = (r.g1, r.s1, r.qb, r.vb, r.mb, r.g2, r.s2, r.sb)
    for row, ref in enumerate(small):
        r.vec[row : row + 1, :] = ref[...].astype(F32).reshape(1, width)
    for row in range(plan.ff // width):
        value = r.eb[row * width : (row + 1) * width].astype(F32)
        r.vec[8 + row : 9 + row, :] = value.reshape(1, width)
    r.stage[rows:, :] = jnp.zeros((padded - rows, width), F32)
    r.sums[...] = jnp.zeros_like(r.sums)
    loads["tok"].wait()

    def first_norm(item):
        unit, _ = normalized(r.tok[item].astype(F32))
        r.stage[item_rows(item), :] = unit * vector(0) + vector(1)

    each_item(first_norm, U1)
    r.first_rows[...] = r.stage[...].astype(BF16)
    for name in ("mw", "ew", "sw"):
        loads[name].start()
    loads["cot"].wait()

    def mask_cotangent(item):
        grad = r.cot[item].astype(F32)
        r.stage[item_rows(item), :] = jnp.where(row_live(item), grad, 0.0)

    each_item(mask_cotangent, U3)
    r.grad_out[...] = r.stage[...].astype(BF16)
    loads["jw"].wait()
    for part, bias in enumerate((2, None, 3)):

        cols = slice(part * width, (part + 1) * width)
        value = matmul(r.first_rows[...], r.jw[:, cols])
        if bias is not None:
            value = value + vector(bias)
        r.qkv[:, cols] = value.astype(BF16).astype(F32)
    r.qkv[rows:, :] = jnp.zeros((padded - rows, 3 * width), F32)

    def attend_item(item):
        here = item_rows(item)
        key_live = (
            lax.broadcasted_iota(jnp.int32, (2 * slots, slots), 1) < r.visible[item]
        )
        every = range(pairs)
        queries = [both_heads(r.qkv[here, pair_lanes(0, pair)]) for pair in every]
        keys = [r.qkv[here, pair_lanes(1, pair)].astype(BF16) for pair in every]
        values = [r.qkv[here, pair_lanes(2, pair)].astype(BF16) for pair in every]
        logits = [matmul(queries[pair], keys[pair], ((1,), (1,))) for pair in every]
        logits = [jnp.where(key_live, value * score_scale, -1000000000.0) for value in logits]
        tops = [jnp.max(value, axis=-1, keepdims=True) for value in logits]
        expos = [jnp.exp(logits[pair] - tops[pair]) for pair in every]
        totals = [jnp.sum(value, axis=-1, keepdims=True) for value in expos]
        attends = [expos[pair] * (1.0 / totals[pair]) for pair in every]
        mixed = [matmul(attends[pair].astype(BF16), values[pair]) for pair in every]
        for pair in every:
            r.attend[item * pairs + pair] = attends[pair]
            r.stage[here, pair_lanes(0, pair)] = one_head_each(mixed[pair])

    each_item(attend_item, U4)
    r.mixed_rows[...] = r.stage[...].astype(BF16)
    loads["mw"].wait()

    r.middle[...] = matmul(r.mixed_rows[...], r.mw[...]) + vector(4)

    def second_norm(item):
        here = item_rows(item)
        middle = r.middle[here, :] + r.tok[item].astype(F32)
        r.middle[here, :] = middle
        unit, _ = normalized(middle)
        r.stage[here, :] = unit * vector(5) + vector(6)

    each_item(second_norm, U2)
    r.second[...] = r.stage[...].astype(BF16)
    loads["ew"].wait()

    def expand_bias(tile):
        per_row = width // TILE
        return r.vec[
            pl.ds(8 + lax.div(tile, per_row), 1),
            aligned(lax.rem(tile, per_row) * TILE, TILE, TILE),
        ]

    def hidden_tile(tile):
        cols = aligned(tile * TILE, TILE, TILE)
        hidden = matmul(r.second[...], r.ew[:, cols]) + expand_bias(tile)
        return hidden, 0.5 + 0.5 * lax.erf(hidden * ROOT_HALF)

    def expand_tile(place):
        tile = place * plan.groups
        hidden, normal = hidden_tile(tile)
        r.active_t[aligned(tile * TILE, TILE, TILE), :] = (hidden * normal).astype(BF16).T

    each_tile(plan.blocks, expand_tile, U5)
    loads["sw"].wait()

    rows_full = rows // 16 * 16

    def share(name, count, turn, body):
        size = -(-count // plan.jobs[name][1])
        first = turn * size
        last = jnp.minimum(first + size, count)
        lax.fori_loop(first, last, lambda place, carry: (body(place), carry)[1], 0)

    def in_turns(turn, first_half, second_half):
        number = lax.div(turn, plan.split)
        if plan.split == 1:
            first_half(number)
            second_half(number)
        else:
            half = lax.rem(turn, plan.split)
            pl.when(half == 0)(lambda: first_half(number))
            pl.when(half == 1)(lambda: second_half(number))

    def ff_job(turn):
        def tile_job(number):
            group = lax.rem(lax.div(number, plan.blocks) + 1, plan.groups)
            tile = lax.rem(number, plan.blocks) * plan.groups + group
            cols = aligned(tile * TILE, TILE, TILE)
            hidden, normal = hidden_tile(tile)
            active = (hidden * normal).astype(BF16)
            r.active_t[cols, :] = active.T
            slope = normal + hidden * (PEAK * jnp.exp(-0.5 * hidden * hidden))
            grad = matmul(r.grad_out[...], r.sw[cols, :], ((1,), (1,)))
            grad_hidden = (grad * slope).astype(BF16)
            r.grad_hidden[:, cols] = grad_hidden
            r.expand_sums[tile] = jnp.sum(grad_hidden.astype(F32), axis=0, keepdims=True)
            r.acc_out[...] += matmul(active, r.sw[cols, :])
            r.acc_grad[...] += matmul(grad_hidden, r.ew[:, cols], ((1,), (1,)))

        in_turns(turn, tile_job, turn_rows)

    def turn_rows(turn):
        for place, (rows_ref, turned) in enumerate(
            (
                (r.second, r.second_t),
                (r.mixed_rows, r.mixed_t),
                (r.first_rows, r.first_t),
            )
        ):

            @pl.when(turn == place)
            def _():
                turned[...] = rows_ref[...].T

    def norm_job(turn):
        def one(item):
            here = item_rows(item)
            live = row_live(item)
            middle = r.middle[here, :]
            grad_out = jnp.where(live, r.cot[item].astype(F32), 0.0)
            layer_out = jnp.where(live, middle + (r.acc_out[here, :] + vector(7)), 0.0)
            r.cot[item] = layer_out.astype(BF16)
            unit, spread = normalized(middle)
            grad = r.acc_grad[here, :]
            r.sums[5:6, :] += jnp.sum(grad * unit, axis=0, keepdims=True)
            r.sums[6:7, :] += jnp.sum(grad, axis=0, keepdims=True)
            r.sums[7:8, :] += jnp.sum(grad_out, axis=0, keepdims=True)
            grad_middle = grad_out + norm_backward(grad * vector(5), unit, spread)
            r.acc_out[here, :] = grad_middle
            r.sums[4:5, :] += jnp.sum(
                grad_middle.astype(BF16).astype(F32), axis=0, keepdims=True
            )

        share("norm", plan.items, turn, one)

    def mix_job(turn):
        pl.when(turn == 0)(pack_branch)

        def one(tile):
            cols = aligned(tile * TILE, TILE, TILE)
            value = matmul(r.grad_branch[...], r.mw[cols, :], ((1,), (1,)))
            r.stage[:, cols] = value.astype(BF16).astype(F32)

        share("mix", width // TILE, turn, one)

    def pack_branch():
        r.grad_branch[:rows_full, :] = r.acc_out[:rows_full, :].astype(BF16)
        tail = jnp.concatenate(
            [r.acc_out[rows_full:rows, :], jnp.zeros((padded - rows, width), F32)], axis=0
        )
        r.grad_branch[rows_full:, :] = tail.astype(BF16)

    def item_job(turn):
        def scores(item):
            here = item_rows(item)
            for pair in range(pairs):
                values = r.qkv[here, pair_lanes(2, pair)].astype(BF16)
                grad_mixed = both_heads(r.stage[here, pair_lanes(0, pair)])
                attend = r.attend[item * pairs + pair]
                grad_attend = matmul(grad_mixed, values, ((1,), (1,)))
                inner_sum = jnp.sum(attend * grad_attend, axis=-1, keepdims=True)
                r.grad_logits[pair] = (attend * (grad_attend - inner_sum)).astype(BF16)
                r.qkv[here, pair_lanes(2, pair)] = matmul(
                    attend.astype(BF16), grad_mixed, ((0,), (0,))
                )

        def inputs(item):
            here = item_rows(item)
            for pair in range(pairs):
                query = both_heads(r.qkv[here, pair_lanes(0, pair)])
                keys = r.qkv[here, pair_lanes(1, pair)].astype(BF16)
                grad_logits = r.grad_logits[pair]
                grad_query = one_head_each(matmul(grad_logits, keys)) * score_scale
                grad_key = matmul(grad_logits, query, ((0,), (0,))) * score_scale
                r.qkv[here, pair_lanes(0, pair)] = grad_query
                r.qkv[here, pair_lanes(1, pair)] = grad_key

        in_turns(turn, scores, inputs)

    def joint_rows(part):
        return slice(part * padded, (part + 1) * padded)

    def pack_job(turn):
        for part in range(3):

            @pl.when(turn == part * (plan.jobs["pack"][1] > 1))
            def _():
                value = r.qkv[:, part * width : (part + 1) * width].astype(BF16)
                r.sw[joint_rows(part), :] = value
                if part != 1:
                    row = 2 if part == 0 else 3
                    r.sums[row : row + 1, :] = jnp.sum(value.astype(F32), axis=0, keepdims=True)

    def first_job(turn):
        def one(tile):
            cols = aligned(tile * TILE, TILE, TILE)
            total = None
            for part in range(3):
                value = matmul(
                    r.sw[joint_rows(part), :],
                    r.jw[cols, part * width : (part + 1) * width],
                    ((1,), (1,)),
                )
                total = value if total is None else total + value
            r.acc_grad[:, cols] = total

        share("first", width // TILE, turn, one)

    def input_job(turn):
        def one(item):
            here = item_rows(item)
            unit, spread = normalized(r.tok[item].astype(F32))
            grad = r.acc_grad[here, :]
            r.sums[0:1, :] += jnp.sum(grad * unit, axis=0, keepdims=True)
            r.sums[1:2, :] += jnp.sum(grad, axis=0, keepdims=True)
            total = r.acc_out[here, :] + norm_backward(grad * vector(0), unit, spread)
            r.tok[item] = total.astype(BF16)

        share("input", plan.items, turn, one)

        @pl.when(turn == 0)
        def _():
            per_row = width // TILE
            for tile in range(plan.ff_tiles):
                row, start = 8 + tile // per_row, tile % per_row * TILE
                r.sums[row : row + 1, start : start + TILE] = r.expand_sums[tile]

    def when(condition, action):
        if condition is True:
            action()
        else:
            pl.when(condition)(action)

    def roles(move):
        if move.kind == "fold":
            return outer, inner
        if move.kind == "unfold":
            return inner, outer
        return (inner, inner) if move.inner else (True, True)

    def land(number, stage, item):
        ref = getattr(r, f"land{number}_{stage}")
        return ref.at[lax.rem(item, plan.parts[number].slots(stage))]

    def source(number, stage, item):
        if stage == 0:
            return getattr(r, f"part{number}").at[lax.rem(item, 2)]
        return land(number, stage - 1, item)

    kept, given, regions = {}, {}, {}
    for number, part in enumerate(plan.parts):
        for stage, move in enumerate(part.moves):
            bit = bits[move.select] if move.select else 0
            kept[number, stage] = bit * move.length
            given[number, stage] = (1 - bit) * move.length if move.select else 0
            regions[number, stage] = sum(
                bits[select] * size for select, size in part.selects if size >= move.length
            )

    def in_whole(number, stage, item):
        part = plan.parts[number]
        return (
            item,
            aligned(regions[number, stage], part.moves[stage].length, SUB),
            pl.ds(part.column, part.columns),
        )

    def transfer(number, stage, item):
        part = plan.parts[number]
        move = part.moves[stage]
        arrival = plan.arrival_at[number, stage] + lax.rem(item, part.slots(stage))
        send = plan.send_at[number, stage] + lax.rem(item, part.flights(stage))
        if stage < len(part.sums):
            src = source(number, stage, item).at[
                aligned(given[number, stage], move.length, SUB)
            ]
            dst = land(number, stage, item)
        else:
            src = r.whole.at[in_whole(number, stage, item)]
            dst = src
        return pltpu.make_async_remote_copy(
            src_ref=src,
            dst_ref=dst,
            send_sem=r.send_sems.at[send],
            recv_sem=r.recv_sems.at[arrival],
            device_id=partners[move.flips],
            device_id_type=MESH,
        )

    def begin(number, stage, item):
        sender, _ = roles(plan.parts[number].moves[stage])
        when(sender, lambda: transfer(number, stage, item).start())

    def settle(number, stage, item):
        part = plan.parts[number]
        move = part.moves[stage]
        sender, receiver = roles(move)

        def receive():
            if stage < len(part.sums):
                land(number, stage, item)[...] += source(number, stage, item)[
                    aligned(kept[number, stage], move.length, SUB)
                ]
            if stage == len(part.sums) - 1:
                r.whole[in_whole(number, stage, item)] = land(number, stage, item)[...]

        if move.kind in ("fold", "unfold"):
            when(sender, lambda: transfer(number, stage, item).wait_send())

            def arrive():
                transfer(number, stage, item).wait_recv()
                receive()

        else:

            def arrive():
                transfer(number, stage, item).wait()
                receive()

        when(receiver, arrive)
        if stage + 1 < len(part.moves):
            begin(number, stage + 1, item)

    def rows_of(phase):
        _, count, _, windows = plan.phases[phase]
        return count // windows

    def produce(item):
        slot = lax.rem(item, 2)
        lefts = (r.active_t, r.second_t, r.mixed_t, r.first_t)
        rights = (r.grad_out, r.grad_hidden, r.grad_branch, r.sw)
        for phase, (start, count, rows_block, windows) in enumerate(plan.phases):
            left, right = lefts[phase], rights[phase]

            @pl.when((item >= start) & (item < start + count))
            def _():
                local = item - start
                tall = rows_of(phase)
                row = lax.rem(local, tall) * chunk
                window = lax.div(local, tall)
                for number, part in enumerate(plan.parts):
                    picked = [
                        left[aligned(block * rows_block + row + offset, size, size), :]
                        for block, offset, size in part.picks
                    ]
                    if phase == 3:
                        other = right[
                            aligned(window * padded, padded, 256),
                            part.column : part.column + part.columns,
                        ]
                    else:
                        other = right[
                            :, aligned(window * width + part.column, part.columns, 128)
                        ]
                    getattr(r, f"part{number}")[slot] = matmul(
                        jnp.concatenate(picked, axis=0), other
                    )

    def vector_source(stage):
        return getattr(r, f"vector{stage}")

    def vector_part(stage, own):
        before, after = plan.vector_lengths[stage : stage + 2]
        if before == after:
            return pl.ds(0, after)
        bit = bits[plan.links[stage][0]]
        return aligned((bit if own else 1 - bit) * after, after, SUB)

    def vector_exchange(stage):
        return pltpu.make_async_remote_copy(
            src_ref=vector_source(stage).at[vector_part(stage, False)],
            dst_ref=vector_source(stage + 1),
            send_sem=r.vector_sems.at[0, stage],
            recv_sem=r.vector_sems.at[1, stage],
            device_id=partners[plan.links[stage]],
            device_id_type=MESH,
        )

    def vector_pack():
        r.vector0[...] = jnp.zeros_like(r.vector0)
        block = plan.block
        for spot, owner in enumerate(plan.block_order):
            base = spot * plan.vector_rows
            own = slice(owner * block, (owner + 1) * block)
            r.vector0[base : base + 8, :block] = r.sums[:8, own]
            for piece in range(plan.ff // width):
                place = owner * (plan.ff // narrow) + piece * block
                row, start = 8 + place // width, place % width
                r.vector0[base + 8 + piece : base + 9 + piece, :block] = r.sums[
                    row : row + 1, start : start + block
                ]

    def vector_step(tick):
        count = len(plan.links)
        for stage in range(count + 1):

            @pl.when(tick == plan.vector_tick + stage * plan.vector_every)
            def _():
                if stage == 0:
                    vector_pack()
                else:
                    vector_exchange(stage - 1).wait()
                    vector_source(stage)[...] += vector_source(stage - 1)[
                        vector_part(stage - 1, True)
                    ]
                if stage < count:
                    vector_exchange(stage).start()

    pl.semaphore_wait(barrier, len(plan.links))

    def step(tick, carry):
        @pl.when(tick < plan.chunks)
        def _():
            produce(tick)
            for number in range(len(plan.parts)):
                begin(number, 0, tick)

        for stage in range(plan.stages):
            for number, part in enumerate(plan.parts):
                if stage < len(part.moves):
                    item = tick - part.due[stage]

                    @pl.when((item >= 0) & (item < plan.chunks))
                    def _():
                        settle(number, stage, item)

        vector_step(tick)
        @pl.when(tick == 0)
        def _():
            for ref in (r.acc_out, r.acc_grad):
                ref[...] = jnp.zeros_like(ref)

        run = {
            "ff": ff_job,
            "norm": norm_job,
            "mix": mix_job,
            "item": item_job,
            "pack": pack_job,
            "first": first_job,
            "input": input_job,
        }
        for name, (start, count) in plan.jobs.items():
            job = functools.partial(run[name], tick - start)
            pl.when((tick >= start) & (tick < start + count))(job)

        return carry

    lax.fori_loop(0, plan.ticks, step, 0)
    r.vector_out[...] = vector_source(len(plan.links))[...]


def write_kernel(plan, tok, cot, whole, sums, *refs):
    outs, sems = refs[:-1], refs[-1]
    copies = [(tok, outs[0]), (cot, outs[1])]
    for (start, count, _, windows), out in zip(plan.phases, outs[2:6]):
        tall = count // windows
        for window in range(windows):
            first = start + window * tall
            cols = pl.ds(window * plan.width, plan.width)
            copies.append((whole.at[first : first + tall], out.at[:, :, cols]))
    copies = [
        pltpu.make_async_copy(source, target, sems.at[number])
        for number, (source, target) in enumerate(copies)
    ]
    for copy in copies:
        copy.start()
    for row, out in enumerate(outs[6:14]):
        out[...] = sums[row : row + 1, : plan.block].reshape(plan.block)
    pieces = [
        sums[8 + piece : 9 + piece, : plan.block] for piece in range(plan.ff // plan.width)
    ]
    outs[14][...] = jnp.concatenate(pieces, axis=1).reshape(plan.ff // plan.narrow)
    for copy in copies:
        copy.wait()


def shards(
    tokens,
    visible,
    first_gain,
    first_shift,
    joint_weight,
    query_bias,
    value_bias,
    mixer_weight,
    mixer_bias,
    second_gain,
    second_shift,
    expand_weight,
    expand_bias,
    shrink_weight,
    shrink_bias,
    cotangent,
):
    items, slots, width = tokens.shape
    ff = expand_weight.shape[1]
    narrow, wide = lax.axis_size("narrow"), lax.axis_size("wide")
    plan = Plan(narrow, wide, items, slots, width, ff)
    padded, chunk = plan.padded, plan.chunk
    hbm = pl.BlockSpec(memory_space=pl.ANY)
    vmem = pl.BlockSpec(memory_space=pltpu.VMEM)
    smem = pl.BlockSpec(memory_space=pltpu.SMEM)
    inputs = {
        "visible": (visible, smem),
        "g1": (first_gain, vmem),
        "s1": (first_shift, vmem),
        "qb": (query_bias, vmem),
        "vb": (value_bias, vmem),
        "mb": (mixer_bias, vmem),
        "g2": (second_gain, vmem),
        "s2": (second_shift, vmem),
        "sb": (shrink_bias, vmem),
        "eb": (expand_bias, vmem),
        "tok_in": (tokens, hbm),
        "cot_in": (cotangent, hbm),
        "jw_in": (joint_weight, hbm),
        "mw_in": (mixer_weight, hbm),
        "ew_in": (expand_weight, hbm),
        "sw_in": (shrink_weight, hbm),
    }
    block = width // narrow
    outputs = {
        "tok": (tokens.shape, BF16),
        "cot": (tokens.shape, BF16),
        "whole": ((plan.chunks, chunk, width), F32),
        "vector_out": ((plan.vector_rows, plan.block_lanes), F32),
    }
    scratch = {
        "jw": pltpu.VMEM(joint_weight.shape, BF16),
        "mw": pltpu.VMEM(mixer_weight.shape, BF16),
        "ew": pltpu.VMEM(expand_weight.shape, BF16),
        "sw": pltpu.VMEM(shrink_weight.shape, BF16),
        "stage": pltpu.VMEM((padded, width), F32),
        "first_rows": pltpu.VMEM((padded, width), BF16),
        "mixed_rows": pltpu.VMEM((padded, width), BF16),
        "qkv": pltpu.VMEM((padded, 3 * width), F32),
        "attend": pltpu.VMEM((items * plan.pairs, 2 * slots, slots), F32),
        "first_t": pltpu.VMEM((width, padded), BF16),
        "mixed_t": pltpu.VMEM((width, padded), BF16),
        "second": pltpu.VMEM((padded, width), BF16),
        "second_t": pltpu.VMEM((width, padded), BF16),
        "middle": pltpu.VMEM((padded, width), F32),
        "grad_hidden": pltpu.VMEM((padded, ff), BF16),
        "active_t": pltpu.VMEM((ff, padded), BF16),
        "grad_out": pltpu.VMEM((padded, width), BF16),
        "acc_out": pltpu.VMEM((padded, width), F32),
        "acc_grad": pltpu.VMEM((padded, width), F32),
        "grad_branch": pltpu.VMEM((padded, width), BF16),
        "vec": pltpu.VMEM((plan.vector_rows, width), F32),
        "grad_logits": pltpu.VMEM((plan.pairs, 2 * slots, slots), BF16),
        "sums": pltpu.VMEM((plan.vector_rows, width), F32),
        "expand_sums": pltpu.VMEM((plan.ff_tiles, 1, TILE), F32),
        "load_sems": pltpu.SemaphoreType.DMA((6,)),
        "vector_sems": pltpu.SemaphoreType.DMA((2, len(plan.links))),
        "send_sems": pltpu.SemaphoreType.DMA((plan.sends,)),
        "recv_sems": pltpu.SemaphoreType.DMA((plan.arrivals,)),
    }
    for stage, length in enumerate(plan.vector_lengths):
        scratch[f"vector{stage}"] = pltpu.VMEM((length, plan.block_lanes), F32)
    for number, part in enumerate(plan.parts):
        scratch[f"part{number}"] = pltpu.VMEM((2, narrow * chunk, part.columns), F32)
        for stage, move in enumerate(part.sums):
            scratch[f"land{number}_{stage}"] = pltpu.VMEM(
                (part.slots(stage), move.length, part.columns), F32
            )
    results = pl.pallas_call(
        functools.partial(layer_kernel, plan, (*inputs, *outputs, *scratch)),
        out_shape=[pltpu.VMEM(shape, kind) for shape, kind in outputs.values()],
        in_specs=[spec for _, spec in inputs.values()],
        out_specs=[vmem] * len(outputs),
        scratch_shapes=list(scratch.values()),
        compiler_params=pltpu.CompilerParams(
            has_side_effects=True, vmem_limit_bytes=52 * 2**20, collective_id=0
        ),
        name="layer",
    )(*(value for value, _ in inputs.values()))
    row_counts = [count // windows for _, count, _, windows in plan.phases]
    shapes = [jax.ShapeDtypeStruct(tokens.shape, BF16)] * 2
    shapes += [
        jax.ShapeDtypeStruct((tall, chunk, windows * width), F32)
        for tall, (_, _, _, windows) in zip(row_counts, plan.phases)
    ]
    shapes += [jax.ShapeDtypeStruct((block,), F32)] * 8
    shapes += [jax.ShapeDtypeStruct((ff // narrow,), F32)]
    copies = 2 + sum(windows for _, _, _, windows in plan.phases)
    outs = pl.pallas_call(
        functools.partial(write_kernel, plan),
        out_shape=shapes,
        in_specs=[vmem] * len(results),
        out_specs=[hbm] * 6 + [vmem] * 9,
        scratch_shapes=[pltpu.SemaphoreType.DMA((copies,))],
        compiler_params=pltpu.CompilerParams(vmem_limit_bytes=4 * 2**20),
        name="write",
    )(*(pltpu.with_memory_space_constraint(value, pltpu.VMEM) for value in results))
    input_grad, layer_out = outs[:2]
    shrink, expand, mixer, joint = (
        out.reshape(-1, out.shape[-1]) for out in outs[2:6]
    )
    vectors = outs[6:]
    return (
        layer_out,
        input_grad,
        vectors[0],
        vectors[1],
        joint,
        vectors[2],
        vectors[3],
        mixer,
        vectors[4],
        vectors[5],
        vectors[6],
        expand,
        vectors[8],
        shrink,
        vectors[7],
    )


def solution(mesh):
    return jax.shard_map(
        shards,
        mesh=mesh,
        in_specs=(
            P(("wide", "narrow"), None, None),
            P(("wide", "narrow")),
            P(),
            P(),
            P(),
            P(),
            P(),
            P(),
            P(),
            P(),
            P(),
            P(),
            P(),
            P(),
            P(),
            P(("wide", "narrow"), None, None),
        ),
        out_specs=(
            P(("wide", "narrow"), None, None),
            P(("wide", "narrow"), None, None),
            P("narrow"),
            P("narrow"),
            P("narrow", None),
            P("narrow"),
            P("narrow"),
            P("narrow", None),
            P("narrow"),
            P("narrow"),
            P("narrow"),
            P("narrow", None),
            P("narrow"),
            P("narrow", None),
            P("narrow"),
        ),
        check_vma=False,
    )
```

```python
import functools
import types

import jax
import jax.numpy as jnp
from jax import lax
from jax.experimental import pallas as pl
from jax.experimental.pallas import tpu as pltpu
from jax.sharding import PartitionSpec as P

HEAD_DIM = 64
EPSILON = 1e-06
SUB = 8
LAGS = ([1, 2, 2, 2, 2, 2, 3] + [2] * 8, [1] + [2] * 15)
MOST = 32
TILE = 256
U1 = 7
U2 = 7
U3 = 7
U4 = 7
U5 = 4
MESH = pl.DeviceIdType.MESH
ROOT_HALF = 0.5**0.5
PEAK = 0.3989422804014327
BF16 = jnp.bfloat16
F32 = jnp.float32


def bit_of(index, place):
    return lax.rem(lax.div(index, 2**place), 2)


def reversed_bits(value, count):
    out = 0
    for place in range(count):
        out = out * 2 + (value >> place) % 2
    return out


def aligned(start, size, unit):
    return pl.ds(pl.multiple_of(start, unit), size)


def matmul(left, right, contract=((1,), (0,))):
    return lax.dot_general(left, right, (contract, ((), ())), preferred_element_type=F32)


class Move:
    def __init__(self, kind, flips, length, select=None, inner=False):
        self.kind, self.flips, self.length = kind, flips, length
        self.select, self.inner = select, inner


class Part:
    def __init__(self, column, columns, picks, sums, gathers, selects):
        self.column, self.columns, self.picks = column, columns, picks
        self.sums, self.moves = sums, sums + gathers
        self.selects = selects
        self.lags = LAGS[column > 0][: len(self.moves)]
        self.due = [sum(self.lags[: stage + 1]) for stage in range(len(self.moves))]

    def flights(self, stage):
        return self.lags[stage] + 1

    def slots(self, stage):
        after = self.lags[stage + 1] if stage + 1 < len(self.sums) else 0
        count = 2 * self.lags[stage] + after + 2
        if self.moves[stage].kind in ("fold", "unfold"):
            kinds = [move.kind for move in self.moves]
            ahead = self.due[kinds.index("unfold")] - self.due[kinds.index("fold") - 1]
            count = max(count, ahead + 2)
        return count


class Plan:
    def __init__(self, narrow, wide, items, slots, width, ff):
        self.narrow, self.wide, self.width, self.ff = narrow, wide, width, ff
        self.items, self.slots = items, slots
        self.rows = items * slots
        self.padded = self.rows + -self.rows % 256
        self.pairs = width // (2 * HEAD_DIM)
        narrow_bits = self.narrow_bits = narrow.bit_length() - 1
        wide_bits = self.wide_bits = wide.bit_length() - 1
        rows = width // narrow
        chunk = SUB
        while rows % (2 * chunk) == 0 and chunk < MOST:
            chunk *= 2
        self.chunk = chunk
        near, mirror = (("wide", 1),), (("wide", 1), ("wide", 2))
        x, y, core = (("wide", 0),), (("narrow", 1),), (("narrow", 0),)
        if (narrow, wide) == (4, 8):
            self.links = (core, y, x, near, mirror)
            half = chunk // 2
            z_bit, x_bit, y_bit, core_bit = ("wide", 2), x[0], y[0], core[0]
            one = Part(
                0,
                width // 3 * 2,
                [(spot % 2 * 2 + spot // 2, 0, chunk) for spot in range(4)],
                [
                    Move("halve", core, 2 * chunk, core_bit),
                    Move("halve", y, chunk, y_bit),
                    Move("fold", near, chunk),
                    Move("halve", mirror, half, z_bit, True),
                    Move("add", x, half, inner=True),
                ],
                [
                    Move("double", mirror, half, inner=True),
                    Move("unfold", near, chunk),
                ],
                [(z_bit, half)],
            )
            two = Part(
                width // 3 * 2,
                width // 3,
                [
                    (2 * (spot % 2) + spot // 4, spot // 2 % 2 * half, half)
                    for spot in range(8)
                ],
                [
                    Move("halve", core, 2 * chunk, core_bit),
                    Move("halve", x, chunk, x_bit),
                    Move("halve", y, half, y_bit),
                    Move("fold", near, half),
                    Move("add", mirror, half, inner=True),
                ],
                [
                    Move("unfold", near, half),
                    Move("double", x, half),
                ],
                [(x_bit, half)],
            )
            self.parts = (one, two)
        else:
            self.links = tuple((("narrow", place),) for place in range(narrow_bits))
            self.links += tuple((("wide", place),) for place in range(wide_bits))
            sums, gathers, selects = [], [], []
            length = narrow * chunk
            for (axis, place), in self.links:
                if length > SUB:
                    length //= 2
                    sums.append(Move("halve", ((axis, place),), length, (axis, place)))
                    if axis == "wide":
                        selects.append(((axis, place), length))
                        gathers.insert(0, Move("double", ((axis, place),), length))
                else:
                    sums.append(Move("add", ((axis, place),), length))
            picks = [(reversed_bits(spot, narrow_bits), 0, chunk) for spot in range(narrow)]
            self.parts = (Part(0, width, picks, sums, gathers, selects),)
        self.stages = max(len(part.moves) for part in self.parts)
        self.depth = max(part.due[-1] for part in self.parts)
        self.arrivals, self.sends, self.arrival_at, self.send_at = 0, 0, {}, {}
        for number, part in enumerate(self.parts):
            for stage in range(len(part.moves)):
                self.arrival_at[number, stage] = self.arrivals
                self.send_at[number, stage] = self.sends
                self.arrivals += part.slots(stage)
                self.sends += part.flights(stage)
        self.phases = []
        start = 0
        for rows_block, windows in (
            (ff // narrow, 1),
            (rows, ff // width),
            (rows, 1),
            (rows, 3),
        ):
            count = rows_block // chunk * windows
            self.phases.append((start, count, rows_block, windows))
            start += count
        self.chunks = start
        self.ff_tiles = ff // TILE
        self.split = self.phases[1][0] // self.ff_tiles
        assert self.split in (1, 2)
        tall = ff // narrow
        self.groups = tall // TILE if tall % TILE == 0 else 1
        self.blocks = self.ff_tiles // self.groups
        self.jobs = {}
        tick = self.split - 1
        for name, count in (
            ("ff", self.ff_tiles * self.split),
            ("norm", 1 if self.split == 1 else 4),
            ("mix", 1 if self.split == 1 else 3),
            ("item", items * self.split),
            ("pack", 1 if self.split == 1 else 3),
            ("first", 1 if self.split == 1 else 3),
            ("input", 1 if self.split == 1 else 4),
        ):
            self.jobs[name] = (tick, count)
            tick += count
        self.vector_tick = tick
        assert self.phases[2][0] >= self.jobs["item"][0]
        assert self.phases[3][0] >= self.jobs["first"][0]
        self.block = rows
        self.block_lanes = rows + -rows % 128
        self.block_order = [reversed_bits(spot, narrow_bits) for spot in range(narrow)]
        self.vector_rows = 8 + ff // width
        self.vector_rows += -self.vector_rows % SUB
        self.ticks = self.chunks + self.depth
        self.vector_lengths = [narrow * self.vector_rows]
        for flips in self.links:
            length = self.vector_lengths[-1]
            self.vector_lengths.append(length // 2 if flips[0][0] == "narrow" else length)
        self.vector_every = (self.ticks - 1 - self.vector_tick) // len(self.links)
        assert self.vector_every > 0


def layer_kernel(plan, names, *refs):
    r = types.SimpleNamespace(**dict(zip(names, refs)))
    width, chunk, narrow, slots = plan.width, plan.chunk, plan.narrow, plan.slots
    rows, padded, pairs = plan.rows, plan.padded, plan.pairs
    score_scale = HEAD_DIM ** (-0.5)
    spots = {"narrow": lax.axis_index("narrow"), "wide": lax.axis_index("wide")}
    inner = bit_of(spots["wide"], 1) != bit_of(spots["wide"], 2)
    outer = bit_of(spots["wide"], 1) == bit_of(spots["wide"], 2)

    bits = {
        (axis, place): bit_of(spots[axis], place)
        for axis, count in (("narrow", plan.narrow_bits), ("wide", plan.wide_bits))
        for place in range(count)
    }
    partners = {}
    for flips in plan.links:
        there = dict(spots)
        for axis, place in flips:
            there[axis] = there[axis] + (1 - 2 * bits[axis, place]) * 2**place
        partners[flips] = there

    loads = {}
    for number, name in enumerate(("tok", "jw", "mw", "ew", "cot", "sw")):
        loads[name] = pltpu.make_async_copy(
            getattr(r, name + "_in"), getattr(r, name), r.load_sems.at[number]
        )
    loads["tok"].start()
    loads["cot"].start()
    loads["jw"].start()

    barrier = pltpu.get_barrier_semaphore()
    for flips in plan.links:
        pl.semaphore_signal(barrier, inc=1, device_id=partners[flips], device_id_type=MESH)

    def vector(row):
        return r.vec[row : row + 1, :]

    def item_rows(item):
        return aligned(item * slots, slots, SUB)

    def row_live(item):
        return lax.broadcasted_iota(jnp.int32, (slots, 1), 0) < r.visible[item]

    lanes = lax.broadcasted_iota(jnp.int32, (slots, 2 * HEAD_DIM), 1)
    first_head = lanes < HEAD_DIM

    def both_heads(value):
        zero = jnp.zeros_like(value)
        return jnp.concatenate(
            [jnp.where(first_head, value, zero), jnp.where(first_head, zero, value)], axis=0
        ).astype(BF16)

    def one_head_each(value):
        return jnp.where(first_head, value[:slots], value[slots:])

    def normalized(values):
        center = values - jnp.mean(values, axis=-1, keepdims=True)
        spread = lax.rsqrt(jnp.mean(center * center, axis=-1, keepdims=True) + EPSILON)
        return center * spread, spread

    def norm_backward(grad, unit, spread):
        return spread * (
            grad
            - jnp.mean(grad, axis=-1, keepdims=True)
            - unit * jnp.mean(grad * unit, axis=-1, keepdims=True)
        )

    def each_item(body, unroll=1):
        lax.fori_loop(
            0, plan.items, lambda item, carry: (body(item), carry)[1], 0, unroll=unroll
        )

    def each_tile(count, body, unroll=1):
        lax.fori_loop(
            0, count, lambda tile, carry: (body(tile), carry)[1], 0, unroll=unroll
        )

    def pair_lanes(part, pair):
        start = part * width + pair * 2 * HEAD_DIM
        return slice(start, start + 2 * HEAD_DIM)

    small = (r.g1, r.s1, r.qb, r.vb, r.mb, r.g2, r.s2, r.sb)

    def place_small(first, last):
        for row in range(first, last):
            r.vec[row : row + 1, :] = small[row][...].astype(F32).reshape(1, width)

    place_small(0, 2)
    r.stage[rows:, :] = jnp.zeros((padded - rows, width), F32)
    r.sums[...] = jnp.zeros_like(r.sums)
    loads["tok"].wait()

    def first_norm(item):
        unit, _ = normalized(r.tok[item].astype(F32))
        r.stage[item_rows(item), :] = unit * vector(0) + vector(1)

    each_item(first_norm, U1)
    r.first_rows[...] = r.stage[...].astype(BF16)
    for name in ("mw", "ew", "sw"):
        loads[name].start()
    loads["cot"].wait()

    def mask_cotangent(item):
        grad = r.cot[item].astype(F32)
        r.stage[item_rows(item), :] = jnp.where(row_live(item), grad, 0.0)

    each_item(mask_cotangent, U3)
    r.grad_out[...] = r.stage[...].astype(BF16)
    place_small(2, 8)
    for row in range(plan.ff // width):
        value = r.eb[row * width : (row + 1) * width].astype(F32)
        r.vec[8 + row : 9 + row, :] = value.reshape(1, width)
    loads["jw"].wait()
    for part, bias in enumerate((2, None, 3)):

        cols = slice(part * width, (part + 1) * width)
        value = matmul(r.first_rows[...], r.jw[:, cols])
        if bias is not None:
            value = value + vector(bias)
        r.qkv[:, cols] = value.astype(BF16).astype(F32)
    r.qkv[rows:, :] = jnp.zeros((padded - rows, 3 * width), F32)

    def attend_item(item):
        here = item_rows(item)
        key_live = (
            lax.broadcasted_iota(jnp.int32, (2 * slots, slots), 1) < r.visible[item]
        )
        every = range(pairs)
        queries = [both_heads(r.qkv[here, pair_lanes(0, pair)]) for pair in every]
        keys = [r.qkv[here, pair_lanes(1, pair)].astype(BF16) for pair in every]
        values = [r.qkv[here, pair_lanes(2, pair)].astype(BF16) for pair in every]
        logits = [matmul(queries[pair], keys[pair], ((1,), (1,))) for pair in every]
        logits = [jnp.where(key_live, value * score_scale, -1000000000.0) for value in logits]
        tops = [jnp.max(value, axis=-1, keepdims=True) for value in logits]
        expos = [jnp.exp(logits[pair] - tops[pair]) for pair in every]
        totals = [jnp.sum(value, axis=-1, keepdims=True) for value in expos]
        attends = [expos[pair] * (1.0 / totals[pair]) for pair in every]
        mixed = [matmul(attends[pair].astype(BF16), values[pair]) for pair in every]
        for pair in every:
            r.attend[item * pairs + pair] = attends[pair]
            r.stage[here, pair_lanes(0, pair)] = one_head_each(mixed[pair])

    each_item(attend_item, U4)
    r.mixed_rows[...] = r.stage[...].astype(BF16)
    loads["mw"].wait()

    r.middle[...] = matmul(r.mixed_rows[...], r.mw[...]) + vector(4)

    def second_norm(item):
        here = item_rows(item)
        middle = r.middle[here, :] + r.tok[item].astype(F32)
        r.middle[here, :] = middle
        unit, _ = normalized(middle)
        r.stage[here, :] = unit * vector(5) + vector(6)

    each_item(second_norm, U2)
    r.second[...] = r.stage[...].astype(BF16)
    loads["ew"].wait()

    def expand_bias(tile):
        per_row = width // TILE
        return r.vec[
            pl.ds(8 + lax.div(tile, per_row), 1),
            aligned(lax.rem(tile, per_row) * TILE, TILE, TILE),
        ]

    def hidden_tile(tile):
        cols = aligned(tile * TILE, TILE, TILE)
        hidden = matmul(r.second[...], r.ew[:, cols]) + expand_bias(tile)
        return hidden, 0.5 + 0.5 * lax.erf(hidden * ROOT_HALF)

    def expand_tile(place):
        tile = place * plan.groups
        hidden, normal = hidden_tile(tile)
        r.active_t[aligned(tile * TILE, TILE, TILE), :] = (hidden * normal).astype(BF16).T

    each_tile(plan.blocks, expand_tile, U5)
    loads["sw"].wait()

    rows_full = rows // 16 * 16

    def share(name, count, turn, body):
        size = -(-count // plan.jobs[name][1])
        first = turn * size
        last = jnp.minimum(first + size, count)
        lax.fori_loop(first, last, lambda place, carry: (body(place), carry)[1], 0)

    def in_turns(turn, first_half, second_half):
        number = lax.div(turn, plan.split)
        if plan.split == 1:
            first_half(number)
            second_half(number)
        else:
            half = lax.rem(turn, plan.split)
            pl.when(half == 0)(lambda: first_half(number))
            pl.when(half == 1)(lambda: second_half(number))

    def ff_job(turn):
        def tile_job(number):
            group = lax.rem(lax.div(number, plan.blocks) + 1, plan.groups)
            tile = lax.rem(number, plan.blocks) * plan.groups + group
            cols = aligned(tile * TILE, TILE, TILE)
            hidden, normal = hidden_tile(tile)
            active = (hidden * normal).astype(BF16)
            r.active_t[cols, :] = active.T
            slope = normal + hidden * (PEAK * jnp.exp(-0.5 * hidden * hidden))
            grad = matmul(r.grad_out[...], r.sw[cols, :], ((1,), (1,)))
            grad_hidden = (grad * slope).astype(BF16)
            r.grad_hidden[:, cols] = grad_hidden
            r.expand_sums[tile] = jnp.sum(grad_hidden.astype(F32), axis=0, keepdims=True)
            r.acc_out[...] += matmul(active, r.sw[cols, :])
            r.acc_grad[...] += matmul(grad_hidden, r.ew[:, cols], ((1,), (1,)))

        in_turns(turn, tile_job, turn_rows)

    def turn_rows(turn):
        for place, (rows_ref, turned) in enumerate(
            (
                (r.second, r.second_t),
                (r.mixed_rows, r.mixed_t),
                (r.first_rows, r.first_t),
            )
        ):

            @pl.when(turn == place)
            def _():
                turned[...] = rows_ref[...].T

    def norm_job(turn):
        def one(item):
            here = item_rows(item)
            live = row_live(item)
            middle = r.middle[here, :]
            grad_out = jnp.where(live, r.cot[item].astype(F32), 0.0)
            layer_out = jnp.where(live, middle + (r.acc_out[here, :] + vector(7)), 0.0)
            r.cot[item] = layer_out.astype(BF16)
            unit, spread = normalized(middle)
            grad = r.acc_grad[here, :]
            r.sums[5:6, :] += jnp.sum(grad * unit, axis=0, keepdims=True)
            r.sums[6:7, :] += jnp.sum(grad, axis=0, keepdims=True)
            r.sums[7:8, :] += jnp.sum(grad_out, axis=0, keepdims=True)
            grad_middle = grad_out + norm_backward(grad * vector(5), unit, spread)
            r.acc_out[here, :] = grad_middle
            r.sums[4:5, :] += jnp.sum(
                grad_middle.astype(BF16).astype(F32), axis=0, keepdims=True
            )

        share("norm", plan.items, turn, one)

    def mix_job(turn):
        pl.when(turn == 0)(pack_branch)

        def one(tile):
            cols = aligned(tile * TILE, TILE, TILE)
            value = matmul(r.grad_branch[...], r.mw[cols, :], ((1,), (1,)))
            r.stage[:, cols] = value.astype(BF16).astype(F32)

        share("mix", width // TILE, turn, one)

    def pack_branch():
        r.grad_branch[:rows_full, :] = r.acc_out[:rows_full, :].astype(BF16)
        tail = jnp.concatenate(
            [r.acc_out[rows_full:rows, :], jnp.zeros((padded - rows, width), F32)], axis=0
        )
        r.grad_branch[rows_full:, :] = tail.astype(BF16)

    def item_job(turn):
        def scores(item):
            here = item_rows(item)
            for pair in range(pairs):
                values = r.qkv[here, pair_lanes(2, pair)].astype(BF16)
                grad_mixed = both_heads(r.stage[here, pair_lanes(0, pair)])
                attend = r.attend[item * pairs + pair]
                grad_attend = matmul(grad_mixed, values, ((1,), (1,)))
                inner_sum = jnp.sum(attend * grad_attend, axis=-1, keepdims=True)
                r.grad_logits[pair] = (attend * (grad_attend - inner_sum)).astype(BF16)
                r.qkv[here, pair_lanes(2, pair)] = matmul(
                    attend.astype(BF16), grad_mixed, ((0,), (0,))
                )

        def inputs(item):
            here = item_rows(item)
            for pair in range(pairs):
                query = both_heads(r.qkv[here, pair_lanes(0, pair)])
                keys = r.qkv[here, pair_lanes(1, pair)].astype(BF16)
                grad_logits = r.grad_logits[pair]
                grad_query = one_head_each(matmul(grad_logits, keys)) * score_scale
                grad_key = matmul(grad_logits, query, ((0,), (0,))) * score_scale
                r.qkv[here, pair_lanes(0, pair)] = grad_query
                r.qkv[here, pair_lanes(1, pair)] = grad_key

        in_turns(turn, scores, inputs)

    def joint_rows(part):
        return slice(part * padded, (part + 1) * padded)

    def pack_job(turn):
        for part in range(3):

            @pl.when(turn == part * (plan.jobs["pack"][1] > 1))
            def _():
                value = r.qkv[:, part * width : (part + 1) * width].astype(BF16)
                r.sw[joint_rows(part), :] = value
                if part != 1:
                    row = 2 if part == 0 else 3
                    r.sums[row : row + 1, :] = jnp.sum(value.astype(F32), axis=0, keepdims=True)

    def first_job(turn):
        def one(tile):
            cols = aligned(tile * TILE, TILE, TILE)
            total = None
            for part in range(3):
                value = matmul(
                    r.sw[joint_rows(part), :],
                    r.jw[cols, part * width : (part + 1) * width],
                    ((1,), (1,)),
                )
                total = value if total is None else total + value
            r.acc_grad[:, cols] = total

        share("first", width // TILE, turn, one)

    def input_job(turn):
        def one(item):
            here = item_rows(item)
            unit, spread = normalized(r.tok[item].astype(F32))
            grad = r.acc_grad[here, :]
            r.sums[0:1, :] += jnp.sum(grad * unit, axis=0, keepdims=True)
            r.sums[1:2, :] += jnp.sum(grad, axis=0, keepdims=True)
            total = r.acc_out[here, :] + norm_backward(grad * vector(0), unit, spread)
            r.tok[item] = total.astype(BF16)

        share("input", plan.items, turn, one)

        @pl.when(turn == 0)
        def _():
            per_row = width // TILE
            for tile in range(plan.ff_tiles):
                row, start = 8 + tile // per_row, tile % per_row * TILE
                r.sums[row : row + 1, start : start + TILE] = r.expand_sums[tile]

    def when(condition, action):
        if condition is True:
            action()
        else:
            pl.when(condition)(action)

    def roles(move):
        if move.kind == "fold":
            return outer, inner
        if move.kind == "unfold":
            return inner, outer
        return (inner, inner) if move.inner else (True, True)

    def land(number, stage, item):
        ref = getattr(r, f"land{number}_{stage}")
        return ref.at[lax.rem(item, plan.parts[number].slots(stage))]

    def source(number, stage, item):
        if stage == 0:
            return getattr(r, f"part{number}").at[lax.rem(item, 2)]
        return land(number, stage - 1, item)

    kept, given, regions = {}, {}, {}
    for number, part in enumerate(plan.parts):
        for stage, move in enumerate(part.moves):
            bit = bits[move.select] if move.select else 0
            kept[number, stage] = bit * move.length
            given[number, stage] = (1 - bit) * move.length if move.select else 0
            regions[number, stage] = sum(
                bits[select] * size for select, size in part.selects if size >= move.length
            )

    def in_whole(number, stage, item):
        part = plan.parts[number]
        return (
            item,
            aligned(regions[number, stage], part.moves[stage].length, SUB),
            pl.ds(part.column, part.columns),
        )

    def transfer(number, stage, item):
        part = plan.parts[number]
        move = part.moves[stage]
        arrival = plan.arrival_at[number, stage] + lax.rem(item, part.slots(stage))
        send = plan.send_at[number, stage] + lax.rem(item, part.flights(stage))
        if stage < len(part.sums):
            src = source(number, stage, item).at[
                aligned(given[number, stage], move.length, SUB)
            ]
            dst = land(number, stage, item)
        else:
            src = r.whole.at[in_whole(number, stage, item)]
            dst = src
        return pltpu.make_async_remote_copy(
            src_ref=src,
            dst_ref=dst,
            send_sem=r.send_sems.at[send],
            recv_sem=r.recv_sems.at[arrival],
            device_id=partners[move.flips],
            device_id_type=MESH,
        )

    def begin(number, stage, item):
        sender, _ = roles(plan.parts[number].moves[stage])
        when(sender, lambda: transfer(number, stage, item).start())

    def settle(number, stage, item):
        part = plan.parts[number]
        move = part.moves[stage]
        sender, receiver = roles(move)

        def receive():
            if stage < len(part.sums):
                land(number, stage, item)[...] += source(number, stage, item)[
                    aligned(kept[number, stage], move.length, SUB)
                ]
            if stage == len(part.sums) - 1:
                r.whole[in_whole(number, stage, item)] = land(number, stage, item)[...]

        if move.kind in ("fold", "unfold"):
            when(sender, lambda: transfer(number, stage, item).wait_send())

            def arrive():
                transfer(number, stage, item).wait_recv()
                receive()

        else:

            def arrive():
                transfer(number, stage, item).wait()
                receive()

        when(receiver, arrive)
        if stage + 1 < len(part.moves):
            begin(number, stage + 1, item)

    def rows_of(phase):
        _, count, _, windows = plan.phases[phase]
        return count // windows

    def produce(item):
        slot = lax.rem(item, 2)
        lefts = (r.active_t, r.second_t, r.mixed_t, r.first_t)
        rights = (r.grad_out, r.grad_hidden, r.grad_branch, r.sw)
        for phase, (start, count, rows_block, windows) in enumerate(plan.phases):
            left, right = lefts[phase], rights[phase]

            @pl.when((item >= start) & (item < start + count))
            def _():
                local = item - start
                tall = rows_of(phase)
                row = lax.rem(local, tall) * chunk
                window = lax.div(local, tall)
                for number, part in enumerate(plan.parts):
                    picked = [
                        left[aligned(block * rows_block + row + offset, size, size), :]
                        for block, offset, size in part.picks
                    ]
                    if phase == 3:
                        other = right[
                            aligned(window * padded, padded, 256),
                            part.column : part.column + part.columns,
                        ]
                    else:
                        other = right[
                            :, aligned(window * width + part.column, part.columns, 128)
                        ]
                    getattr(r, f"part{number}")[slot] = matmul(
                        jnp.concatenate(picked, axis=0), other
                    )

    def vector_source(stage):
        return getattr(r, f"vector{stage}")

    def vector_part(stage, own):
        before, after = plan.vector_lengths[stage : stage + 2]
        if before == after:
            return pl.ds(0, after)
        bit = bits[plan.links[stage][0]]
        return aligned((bit if own else 1 - bit) * after, after, SUB)

    def vector_exchange(stage):
        return pltpu.make_async_remote_copy(
            src_ref=vector_source(stage).at[vector_part(stage, False)],
            dst_ref=vector_source(stage + 1),
            send_sem=r.vector_sems.at[0, stage],
            recv_sem=r.vector_sems.at[1, stage],
            device_id=partners[plan.links[stage]],
            device_id_type=MESH,
        )

    def vector_pack():
        r.vector0[...] = jnp.zeros_like(r.vector0)
        block = plan.block
        for spot, owner in enumerate(plan.block_order):
            base = spot * plan.vector_rows
            own = slice(owner * block, (owner + 1) * block)
            r.vector0[base : base + 8, :block] = r.sums[:8, own]
            for piece in range(plan.ff // width):
                place = owner * (plan.ff // narrow) + piece * block
                row, start = 8 + place // width, place % width
                r.vector0[base + 8 + piece : base + 9 + piece, :block] = r.sums[
                    row : row + 1, start : start + block
                ]

    def vector_step(tick):
        count = len(plan.links)
        for stage in range(count + 1):

            @pl.when(tick == plan.vector_tick + stage * plan.vector_every)
            def _():
                if stage == 0:
                    vector_pack()
                else:
                    vector_exchange(stage - 1).wait()
                    vector_source(stage)[...] += vector_source(stage - 1)[
                        vector_part(stage - 1, True)
                    ]
                if stage < count:
                    vector_exchange(stage).start()

    pl.semaphore_wait(barrier, len(plan.links))

    def step(tick, carry):
        @pl.when(tick < plan.chunks)
        def _():
            produce(tick)
            for number in range(len(plan.parts)):
                begin(number, 0, tick)

        for stage in range(plan.stages):
            for number, part in enumerate(plan.parts):
                if stage < len(part.moves):
                    item = tick - part.due[stage]

                    @pl.when((item >= 0) & (item < plan.chunks))
                    def _():
                        settle(number, stage, item)

        vector_step(tick)
        @pl.when(tick == 0)
        def _():
            for ref in (r.acc_out, r.acc_grad):
                ref[...] = jnp.zeros_like(ref)

        run = {
            "ff": ff_job,
            "norm": norm_job,
            "mix": mix_job,
            "item": item_job,
            "pack": pack_job,
            "first": first_job,
            "input": input_job,
        }
        for name, (start, count) in plan.jobs.items():
            job = functools.partial(run[name], tick - start)
            pl.when((tick >= start) & (tick < start + count))(job)

        return carry

    lax.fori_loop(0, plan.ticks, step, 0)
    r.vector_out[...] = vector_source(len(plan.links))[...]


def write_kernel(plan, tok, cot, whole, sums, *refs):
    outs, held, sems = refs[:15], refs[15:-1], refs[-1]
    copies = [(tok, outs[0]), (cot, outs[1])]
    for (start, count, _, windows), out in zip(plan.phases, outs[2:6]):
        tall = count // windows
        for window in range(windows):
            first = start + window * tall
            cols = pl.ds(window * plan.width, plan.width)
            copies.append((whole.at[first : first + tall], out.at[:, :, cols]))
    copies = [
        pltpu.make_async_copy(source, target, sems.at[number])
        for number, (source, target) in enumerate(copies)
    ]
    for copy in copies:
        copy.start()
    for row, ref in enumerate(held[:8]):
        ref[...] = sums[row : row + 1, : plan.block].reshape(plan.block)
    pieces = [
        sums[8 + piece : 9 + piece, : plan.block] for piece in range(plan.ff // plan.width)
    ]
    held[8][...] = jnp.concatenate(pieces, axis=1).reshape(plan.ff // plan.narrow)
    for source, target in zip(held, outs[6:]):
        copy = pltpu.make_async_copy(source, target, sems.at[len(copies)])
        copy.start()
        copies.append(copy)
    for copy in copies:
        copy.wait()


def shards(
    tokens,
    visible,
    first_gain,
    first_shift,
    joint_weight,
    query_bias,
    value_bias,
    mixer_weight,
    mixer_bias,
    second_gain,
    second_shift,
    expand_weight,
    expand_bias,
    shrink_weight,
    shrink_bias,
    cotangent,
):
    items, slots, width = tokens.shape
    ff = expand_weight.shape[1]
    narrow, wide = lax.axis_size("narrow"), lax.axis_size("wide")
    plan = Plan(narrow, wide, items, slots, width, ff)
    padded, chunk = plan.padded, plan.chunk
    hbm = pl.BlockSpec(memory_space=pl.ANY)
    vmem = pl.BlockSpec(memory_space=pltpu.VMEM)
    smem = pl.BlockSpec(memory_space=pltpu.SMEM)
    inputs = {
        "visible": (visible, smem),
        "g1": (first_gain, vmem),
        "s1": (first_shift, vmem),
        "qb": (query_bias, vmem),
        "vb": (value_bias, vmem),
        "mb": (mixer_bias, vmem),
        "g2": (second_gain, vmem),
        "s2": (second_shift, vmem),
        "sb": (shrink_bias, vmem),
        "eb": (expand_bias, vmem),
        "tok_in": (tokens, hbm),
        "cot_in": (cotangent, hbm),
        "jw_in": (joint_weight, hbm),
        "mw_in": (mixer_weight, hbm),
        "ew_in": (expand_weight, hbm),
        "sw_in": (shrink_weight, hbm),
    }
    block = width // narrow
    outputs = {
        "tok": (tokens.shape, BF16),
        "cot": (tokens.shape, BF16),
        "whole": ((plan.chunks, chunk, width), F32),
        "vector_out": ((plan.vector_rows, plan.block_lanes), F32),
    }
    scratch = {
        "jw": pltpu.VMEM(joint_weight.shape, BF16),
        "mw": pltpu.VMEM(mixer_weight.shape, BF16),
        "ew": pltpu.VMEM(expand_weight.shape, BF16),
        "sw": pltpu.VMEM(shrink_weight.shape, BF16),
        "stage": pltpu.VMEM((padded, width), F32),
        "first_rows": pltpu.VMEM((padded, width), BF16),
        "mixed_rows": pltpu.VMEM((padded, width), BF16),
        "qkv": pltpu.VMEM((padded, 3 * width), F32),
        "attend": pltpu.VMEM((items * plan.pairs, 2 * slots, slots), F32),
        "first_t": pltpu.VMEM((width, padded), BF16),
        "mixed_t": pltpu.VMEM((width, padded), BF16),
        "second": pltpu.VMEM((padded, width), BF16),
        "second_t": pltpu.VMEM((width, padded), BF16),
        "middle": pltpu.VMEM((padded, width), F32),
        "grad_hidden": pltpu.VMEM((padded, ff), BF16),
        "active_t": pltpu.VMEM((ff, padded), BF16),
        "grad_out": pltpu.VMEM((padded, width), BF16),
        "acc_out": pltpu.VMEM((padded, width), F32),
        "acc_grad": pltpu.VMEM((padded, width), F32),
        "grad_branch": pltpu.VMEM((padded, width), BF16),
        "vec": pltpu.VMEM((plan.vector_rows, width), F32),
        "grad_logits": pltpu.VMEM((plan.pairs, 2 * slots, slots), BF16),
        "sums": pltpu.VMEM((plan.vector_rows, width), F32),
        "expand_sums": pltpu.VMEM((plan.ff_tiles, 1, TILE), F32),
        "load_sems": pltpu.SemaphoreType.DMA((6,)),
        "vector_sems": pltpu.SemaphoreType.DMA((2, len(plan.links))),
        "send_sems": pltpu.SemaphoreType.DMA((plan.sends,)),
        "recv_sems": pltpu.SemaphoreType.DMA((plan.arrivals,)),
    }
    for stage, length in enumerate(plan.vector_lengths):
        scratch[f"vector{stage}"] = pltpu.VMEM((length, plan.block_lanes), F32)
    for number, part in enumerate(plan.parts):
        scratch[f"part{number}"] = pltpu.VMEM((2, narrow * chunk, part.columns), F32)
        for stage, move in enumerate(part.sums):
            scratch[f"land{number}_{stage}"] = pltpu.VMEM(
                (part.slots(stage), move.length, part.columns), F32
            )
    results = pl.pallas_call(
        functools.partial(layer_kernel, plan, (*inputs, *outputs, *scratch)),
        out_shape=[pltpu.VMEM(shape, kind) for shape, kind in outputs.values()],
        in_specs=[spec for _, spec in inputs.values()],
        out_specs=[vmem] * len(outputs),
        scratch_shapes=list(scratch.values()),
        compiler_params=pltpu.CompilerParams(
            has_side_effects=True, vmem_limit_bytes=52 * 2**20, collective_id=0
        ),
        name="layer",
    )(*(value for value, _ in inputs.values()))
    row_counts = [count // windows for _, count, _, windows in plan.phases]
    shapes = [jax.ShapeDtypeStruct(tokens.shape, BF16)] * 2
    shapes += [
        jax.ShapeDtypeStruct((tall, chunk, windows * width), F32)
        for tall, (_, _, _, windows) in zip(row_counts, plan.phases)
    ]
    shapes += [jax.ShapeDtypeStruct((block,), F32)] * 8
    shapes += [jax.ShapeDtypeStruct((ff // narrow,), F32)]
    copies = 2 + sum(windows for _, _, _, windows in plan.phases)
    outs = pl.pallas_call(
        functools.partial(write_kernel, plan),
        out_shape=shapes,
        in_specs=[vmem] * len(results),
        out_specs=[hbm] * 15,
        scratch_shapes=[pltpu.VMEM(shape.shape, F32) for shape in shapes[6:]]
        + [pltpu.SemaphoreType.DMA((copies + 9,))],
        compiler_params=pltpu.CompilerParams(vmem_limit_bytes=4 * 2**20),
        name="write",
    )(*(pltpu.with_memory_space_constraint(value, pltpu.VMEM) for value in results))
    input_grad, layer_out = outs[:2]
    shrink, expand, mixer, joint = (
        out.reshape(-1, out.shape[-1]) for out in outs[2:6]
    )
    vectors = outs[6:]
    return (
        layer_out,
        input_grad,
        vectors[0],
        vectors[1],
        joint,
        vectors[2],
        vectors[3],
        mixer,
        vectors[4],
        vectors[5],
        vectors[6],
        expand,
        vectors[8],
        shrink,
        vectors[7],
    )


def solution(mesh):
    return jax.shard_map(
        shards,
        mesh=mesh,
        in_specs=(
            P(("wide", "narrow"), None, None),
            P(("wide", "narrow")),
            P(),
            P(),
            P(),
            P(),
            P(),
            P(),
            P(),
            P(),
            P(),
            P(),
            P(),
            P(),
            P(),
            P(("wide", "narrow"), None, None),
        ),
        out_specs=(
            P(("wide", "narrow"), None, None),
            P(("wide", "narrow"), None, None),
            P("narrow"),
            P("narrow"),
            P("narrow", None),
            P("narrow"),
            P("narrow"),
            P("narrow", None),
            P("narrow"),
            P("narrow"),
            P("narrow"),
            P("narrow", None),
            P("narrow"),
            P("narrow", None),
            P("narrow"),
        ),
        check_vma=False,
    )
```

```python
import functools
import types

import jax
import jax.numpy as jnp
from jax import lax
from jax.experimental import pallas as pl
from jax.experimental.pallas import tpu as pltpu
from jax.sharding import PartitionSpec as P

HEAD_DIM = 64
EPSILON = 1e-06
SUB = 8
LAGS = ([1, 2, 2, 2, 2, 2, 3] + [2] * 8, [1] + [2] * 15)
MOST = 32
TILE = 256
U1 = 7
U2 = 7
U3 = 7
U4 = 7
U5 = 4
MESH = pl.DeviceIdType.MESH
ROOT_HALF = 0.5**0.5
PEAK = 0.3989422804014327
BF16 = jnp.bfloat16
F32 = jnp.float32


def bit_of(index, place):
    return lax.rem(lax.div(index, 2**place), 2)


def reversed_bits(value, count):
    out = 0
    for place in range(count):
        out = out * 2 + (value >> place) % 2
    return out


def aligned(start, size, unit):
    return pl.ds(pl.multiple_of(start, unit), size)


def matmul(left, right, contract=((1,), (0,))):
    return lax.dot_general(left, right, (contract, ((), ())), preferred_element_type=F32)


class Move:
    def __init__(self, kind, flips, length, select=None, inner=False):
        self.kind, self.flips, self.length = kind, flips, length
        self.select, self.inner = select, inner


class Part:
    def __init__(self, column, columns, picks, sums, gathers, selects):
        self.column, self.columns, self.picks = column, columns, picks
        self.sums, self.moves = sums, sums + gathers
        self.selects = selects
        self.lags = LAGS[column > 0][: len(self.moves)]
        self.due = [sum(self.lags[: stage + 1]) for stage in range(len(self.moves))]

    def flights(self, stage):
        return self.lags[stage] + 1

    def slots(self, stage):
        after = self.lags[stage + 1] if stage + 1 < len(self.sums) else 0
        count = 2 * self.lags[stage] + after + 2
        if self.moves[stage].kind in ("fold", "unfold"):
            kinds = [move.kind for move in self.moves]
            ahead = self.due[kinds.index("unfold")] - self.due[kinds.index("fold") - 1]
            count = max(count, ahead + 2)
        return count


class Plan:
    def __init__(self, narrow, wide, items, slots, width, ff):
        self.narrow, self.wide, self.width, self.ff = narrow, wide, width, ff
        self.items, self.slots = items, slots
        self.rows = items * slots
        self.padded = self.rows + -self.rows % 256
        self.pairs = width // (2 * HEAD_DIM)
        narrow_bits = self.narrow_bits = narrow.bit_length() - 1
        wide_bits = self.wide_bits = wide.bit_length() - 1
        rows = width // narrow
        chunk = SUB
        while rows % (2 * chunk) == 0 and chunk < MOST:
            chunk *= 2
        self.chunk = chunk
        near, mirror = (("wide", 1),), (("wide", 1), ("wide", 2))
        x, y, core = (("wide", 0),), (("narrow", 1),), (("narrow", 0),)
        if (narrow, wide) == (4, 8):
            self.links = (core, y, x, near, mirror)
            half = chunk // 2
            z_bit, x_bit, y_bit, core_bit = ("wide", 2), x[0], y[0], core[0]
            one = Part(
                0,
                width // 3 * 2,
                [(spot % 2 * 2 + spot // 2, 0, chunk) for spot in range(4)],
                [
                    Move("halve", core, 2 * chunk, core_bit),
                    Move("halve", y, chunk, y_bit),
                    Move("fold", near, chunk),
                    Move("halve", mirror, half, z_bit, True),
                    Move("add", x, half, inner=True),
                ],
                [
                    Move("double", mirror, half, inner=True),
                    Move("unfold", near, chunk),
                ],
                [(z_bit, half)],
            )
            two = Part(
                width // 3 * 2,
                width // 3,
                [
                    (2 * (spot % 2) + spot // 4, spot // 2 % 2 * half, half)
                    for spot in range(8)
                ],
                [
                    Move("halve", core, 2 * chunk, core_bit),
                    Move("halve", x, chunk, x_bit),
                    Move("halve", y, half, y_bit),
                    Move("fold", near, half),
                    Move("add", mirror, half, inner=True),
                ],
                [
                    Move("unfold", near, half),
                    Move("double", x, half),
                ],
                [(x_bit, half)],
            )
            self.parts = (one, two)
        else:
            self.links = tuple((("narrow", place),) for place in range(narrow_bits))
            self.links += tuple((("wide", place),) for place in range(wide_bits))
            sums, gathers, selects = [], [], []
            length = narrow * chunk
            for (axis, place), in self.links:
                if length > SUB:
                    length //= 2
                    sums.append(Move("halve", ((axis, place),), length, (axis, place)))
                    if axis == "wide":
                        selects.append(((axis, place), length))
                        gathers.insert(0, Move("double", ((axis, place),), length))
                else:
                    sums.append(Move("add", ((axis, place),), length))
            picks = [(reversed_bits(spot, narrow_bits), 0, chunk) for spot in range(narrow)]
            self.parts = (Part(0, width, picks, sums, gathers, selects),)
        self.stages = max(len(part.moves) for part in self.parts)
        self.depth = max(part.due[-1] for part in self.parts)
        self.arrivals, self.sends, self.arrival_at, self.send_at = 0, 0, {}, {}
        for number, part in enumerate(self.parts):
            for stage in range(len(part.moves)):
                self.arrival_at[number, stage] = self.arrivals
                self.send_at[number, stage] = self.sends
                self.arrivals += part.slots(stage)
                self.sends += part.flights(stage)
        self.phases = []
        start = 0
        for rows_block, windows in (
            (ff // narrow, 1),
            (rows, ff // width),
            (rows, 1),
            (rows, 3),
        ):
            count = rows_block // chunk * windows
            self.phases.append((start, count, rows_block, windows))
            start += count
        self.chunks = start
        self.ff_tiles = ff // TILE
        self.split = self.phases[1][0] // self.ff_tiles
        assert self.split in (1, 2)
        tall = ff // narrow
        self.groups = tall // TILE if tall % TILE == 0 else 1
        self.blocks = self.ff_tiles // self.groups
        self.jobs = {}
        tick = self.split - 1
        for name, count in (
            ("ff", self.ff_tiles * self.split),
            ("norm", 1 if self.split == 1 else 4),
            ("mix", 1 if self.split == 1 else 3),
            ("item", items * self.split),
            ("pack", 1 if self.split == 1 else 3),
            ("first", 1 if self.split == 1 else 3),
            ("input", 1 if self.split == 1 else 4),
        ):
            self.jobs[name] = (tick, count)
            tick += count
        self.vector_tick = tick
        assert self.phases[2][0] >= self.jobs["item"][0]
        assert self.phases[3][0] >= self.jobs["first"][0]
        self.block = rows
        self.block_lanes = rows + -rows % 128
        self.block_order = [reversed_bits(spot, narrow_bits) for spot in range(narrow)]
        self.vector_rows = 8 + ff // width
        self.vector_rows += -self.vector_rows % SUB
        self.ticks = self.chunks + self.depth
        self.vector_lengths = [narrow * self.vector_rows]
        for flips in self.links:
            length = self.vector_lengths[-1]
            self.vector_lengths.append(length // 2 if flips[0][0] == "narrow" else length)
        self.vector_every = (self.ticks - 1 - self.vector_tick) // len(self.links)
        assert self.vector_every > 0


def layer_kernel(plan, names, *refs):
    r = types.SimpleNamespace(**dict(zip(names, refs)))
    width, chunk, narrow, slots = plan.width, plan.chunk, plan.narrow, plan.slots
    rows, padded, pairs = plan.rows, plan.padded, plan.pairs
    score_scale = HEAD_DIM ** (-0.5)
    spots = {"narrow": lax.axis_index("narrow"), "wide": lax.axis_index("wide")}
    inner = bit_of(spots["wide"], 1) != bit_of(spots["wide"], 2)
    outer = bit_of(spots["wide"], 1) == bit_of(spots["wide"], 2)

    bits = {
        (axis, place): bit_of(spots[axis], place)
        for axis, count in (("narrow", plan.narrow_bits), ("wide", plan.wide_bits))
        for place in range(count)
    }
    partners = {}
    for flips in plan.links:
        there = dict(spots)
        for axis, place in flips:
            there[axis] = there[axis] + (1 - 2 * bits[axis, place]) * 2**place
        partners[flips] = there

    loads = {}
    for number, name in enumerate(("tok", "jw", "mw", "ew", "cot", "sw")):
        loads[name] = pltpu.make_async_copy(
            getattr(r, name + "_in"), getattr(r, name), r.load_sems.at[number]
        )
    loads["tok"].start()
    loads["cot"].start()
    loads["jw"].start()

    barrier = pltpu.get_barrier_semaphore()
    for flips in plan.links:
        pl.semaphore_signal(barrier, inc=1, device_id=partners[flips], device_id_type=MESH)

    def vector(row):
        return r.vec[row : row + 1, :]

    def item_rows(item):
        return aligned(item * slots, slots, SUB)

    def row_live(item):
        return lax.broadcasted_iota(jnp.int32, (slots, 1), 0) < r.visible[item]

    lanes = lax.broadcasted_iota(jnp.int32, (slots, 2 * HEAD_DIM), 1)
    first_head = lanes < HEAD_DIM

    def both_heads(value):
        zero = jnp.zeros_like(value)
        return jnp.concatenate(
            [jnp.where(first_head, value, zero), jnp.where(first_head, zero, value)], axis=0
        ).astype(BF16)

    def one_head_each(value):
        return jnp.where(first_head, value[:slots], value[slots:])

    def normalized(values):
        center = values - jnp.mean(values, axis=-1, keepdims=True)
        spread = lax.rsqrt(jnp.mean(center * center, axis=-1, keepdims=True) + EPSILON)
        return center * spread, spread

    def norm_backward(grad, unit, spread):
        return spread * (
            grad
            - jnp.mean(grad, axis=-1, keepdims=True)
            - unit * jnp.mean(grad * unit, axis=-1, keepdims=True)
        )

    def each_item(body, unroll=1):
        lax.fori_loop(
            0, plan.items, lambda item, carry: (body(item), carry)[1], 0, unroll=unroll
        )

    def each_tile(count, body, unroll=1):
        lax.fori_loop(
            0, count, lambda tile, carry: (body(tile), carry)[1], 0, unroll=unroll
        )

    def pair_lanes(part, pair):
        start = part * width + pair * 2 * HEAD_DIM
        return slice(start, start + 2 * HEAD_DIM)

    small = (r.g1, r.s1, r.qb, r.vb, r.mb, r.g2, r.s2, r.sb)

    def place_small(first, last):
        for row in range(first, last):
            r.vec[row : row + 1, :] = small[row][...].astype(F32).reshape(1, width)

    place_small(0, 2)
    r.stage[rows:, :] = jnp.zeros((padded - rows, width), F32)
    r.sums[...] = jnp.zeros_like(r.sums)
    loads["tok"].wait()

    def first_norm(item):
        unit, _ = normalized(r.tok[item].astype(F32))
        r.stage[item_rows(item), :] = unit * vector(0) + vector(1)

    each_item(first_norm, U1)
    r.first_rows[...] = r.stage[...].astype(BF16)
    for name in ("mw", "ew", "sw"):
        loads[name].start()
    loads["cot"].wait()

    def mask_cotangent(item):
        grad = r.cot[item].astype(F32)
        r.stage[item_rows(item), :] = jnp.where(row_live(item), grad, 0.0)

    each_item(mask_cotangent, U3)
    r.grad_out[...] = r.stage[...].astype(BF16)
    place_small(2, 8)
    for row in range(plan.ff // width):
        value = r.eb[row * width : (row + 1) * width].astype(F32)
        r.vec[8 + row : 9 + row, :] = value.reshape(1, width)
    loads["jw"].wait()
    for part, bias in enumerate((2, None, 3)):

        cols = slice(part * width, (part + 1) * width)
        value = matmul(r.first_rows[...], r.jw[:, cols])
        if bias is not None:
            value = value + vector(bias)
        r.qkv[:, cols] = value.astype(BF16).astype(F32)
    r.qkv[rows:, :] = jnp.zeros((padded - rows, 3 * width), F32)

    def attend_item(item):
        here = item_rows(item)
        key_live = (
            lax.broadcasted_iota(jnp.int32, (2 * slots, slots), 1) < r.visible[item]
        )
        every = range(pairs)
        queries = [both_heads(r.qkv[here, pair_lanes(0, pair)]) for pair in every]
        keys = [r.qkv[here, pair_lanes(1, pair)].astype(BF16) for pair in every]
        values = [r.qkv[here, pair_lanes(2, pair)].astype(BF16) for pair in every]
        logits = [matmul(queries[pair], keys[pair], ((1,), (1,))) for pair in every]
        logits = [jnp.where(key_live, value * score_scale, -1000000000.0) for value in logits]
        tops = [jnp.max(value, axis=-1, keepdims=True) for value in logits]
        expos = [jnp.exp(logits[pair] - tops[pair]) for pair in every]
        totals = [jnp.sum(value, axis=-1, keepdims=True) for value in expos]
        attends = [expos[pair] * (1.0 / totals[pair]) for pair in every]
        mixed = [matmul(attends[pair].astype(BF16), values[pair]) for pair in every]
        for pair in every:
            r.attend[item * pairs + pair] = attends[pair]
            r.stage[here, pair_lanes(0, pair)] = one_head_each(mixed[pair])

    each_item(attend_item, U4)
    r.mixed_rows[...] = r.stage[...].astype(BF16)
    loads["mw"].wait()

    r.middle[...] = matmul(r.mixed_rows[...], r.mw[...]) + vector(4)

    def second_norm(item):
        here = item_rows(item)
        middle = r.middle[here, :] + r.tok[item].astype(F32)
        r.middle[here, :] = middle
        unit, _ = normalized(middle)
        r.stage[here, :] = unit * vector(5) + vector(6)

    each_item(second_norm, U2)
    r.second[...] = r.stage[...].astype(BF16)
    loads["ew"].wait()

    def expand_bias(tile):
        per_row = width // TILE
        return r.vec[
            pl.ds(8 + lax.div(tile, per_row), 1),
            aligned(lax.rem(tile, per_row) * TILE, TILE, TILE),
        ]

    def hidden_tile(tile):
        cols = aligned(tile * TILE, TILE, TILE)
        hidden = matmul(r.second[...], r.ew[:, cols]) + expand_bias(tile)
        return hidden, 0.5 + 0.5 * lax.erf(hidden * ROOT_HALF)

    def expand_tile(place):
        tile = place * plan.groups
        hidden, normal = hidden_tile(tile)
        r.active_t[aligned(tile * TILE, TILE, TILE), :] = (hidden * normal).astype(BF16).T

    each_tile(plan.blocks, expand_tile, U5)
    loads["sw"].wait()

    rows_full = rows // 16 * 16

    def share(name, count, turn, body):
        size = -(-count // plan.jobs[name][1])
        first = turn * size
        last = jnp.minimum(first + size, count)
        lax.fori_loop(first, last, lambda place, carry: (body(place), carry)[1], 0)

    def in_turns(turn, first_half, second_half):
        number = lax.div(turn, plan.split)
        if plan.split == 1:
            first_half(number)
            second_half(number)
        else:
            half = lax.rem(turn, plan.split)
            pl.when(half == 0)(lambda: first_half(number))
            pl.when(half == 1)(lambda: second_half(number))

    def ff_job(turn):
        def tile_job(number):
            group = lax.rem(lax.div(number, plan.blocks) + 1, plan.groups)
            tile = lax.rem(number, plan.blocks) * plan.groups + group
            cols = aligned(tile * TILE, TILE, TILE)
            hidden, normal = hidden_tile(tile)
            active = (hidden * normal).astype(BF16)
            r.active_t[cols, :] = active.T
            slope = normal + hidden * (PEAK * jnp.exp(-0.5 * hidden * hidden))
            grad = matmul(r.grad_out[...], r.sw[cols, :], ((1,), (1,)))
            grad_hidden = (grad * slope).astype(BF16)
            r.grad_hidden[:, cols] = grad_hidden
            r.expand_sums[tile] = jnp.sum(grad_hidden.astype(F32), axis=0, keepdims=True)
            r.acc_out[...] += matmul(active, r.sw[cols, :])
            r.acc_grad[...] += matmul(grad_hidden, r.ew[:, cols], ((1,), (1,)))

        in_turns(turn, tile_job, turn_rows)

    def turn_rows(turn):
        for place, (rows_ref, turned) in enumerate(
            (
                (r.second, r.second_t),
                (r.mixed_rows, r.mixed_t),
                (r.first_rows, r.first_t),
            )
        ):

            @pl.when(turn == place)
            def _():
                turned[...] = rows_ref[...].T

    def norm_job(turn):
        def one(item):
            here = item_rows(item)
            live = row_live(item)
            middle = r.middle[here, :]
            grad_out = jnp.where(live, r.cot[item].astype(F32), 0.0)
            layer_out = jnp.where(live, middle + (r.acc_out[here, :] + vector(7)), 0.0)
            r.cot[item] = layer_out.astype(BF16)
            unit, spread = normalized(middle)
            grad = r.acc_grad[here, :]
            r.sums[5:6, :] += jnp.sum(grad * unit, axis=0, keepdims=True)
            r.sums[6:7, :] += jnp.sum(grad, axis=0, keepdims=True)
            r.sums[7:8, :] += jnp.sum(grad_out, axis=0, keepdims=True)
            grad_middle = grad_out + norm_backward(grad * vector(5), unit, spread)
            r.acc_out[here, :] = grad_middle
            r.sums[4:5, :] += jnp.sum(
                grad_middle.astype(BF16).astype(F32), axis=0, keepdims=True
            )

        share("norm", plan.items, turn, one)

    def mix_job(turn):
        pl.when(turn == 0)(pack_branch)

        def one(tile):
            cols = aligned(tile * TILE, TILE, TILE)
            value = matmul(r.grad_branch[...], r.mw[cols, :], ((1,), (1,)))
            r.stage[:, cols] = value.astype(BF16).astype(F32)

        share("mix", width // TILE, turn, one)

    def pack_branch():
        r.grad_branch[:rows_full, :] = r.acc_out[:rows_full, :].astype(BF16)
        tail = jnp.concatenate(
            [r.acc_out[rows_full:rows, :], jnp.zeros((padded - rows, width), F32)], axis=0
        )
        r.grad_branch[rows_full:, :] = tail.astype(BF16)

    def item_job(turn):
        def scores(item):
            here = item_rows(item)
            for pair in range(pairs):
                values = r.qkv[here, pair_lanes(2, pair)].astype(BF16)
                grad_mixed = both_heads(r.stage[here, pair_lanes(0, pair)])
                attend = r.attend[item * pairs + pair]
                grad_attend = matmul(grad_mixed, values, ((1,), (1,)))
                inner_sum = jnp.sum(attend * grad_attend, axis=-1, keepdims=True)
                r.grad_logits[pair] = (attend * (grad_attend - inner_sum)).astype(BF16)
                r.qkv[here, pair_lanes(2, pair)] = matmul(
                    attend.astype(BF16), grad_mixed, ((0,), (0,))
                )

        def inputs(item):
            here = item_rows(item)
            for pair in range(pairs):
                query = both_heads(r.qkv[here, pair_lanes(0, pair)])
                keys = r.qkv[here, pair_lanes(1, pair)].astype(BF16)
                grad_logits = r.grad_logits[pair]
                grad_query = one_head_each(matmul(grad_logits, keys)) * score_scale
                grad_key = matmul(grad_logits, query, ((0,), (0,))) * score_scale
                r.qkv[here, pair_lanes(0, pair)] = grad_query
                r.qkv[here, pair_lanes(1, pair)] = grad_key

        in_turns(turn, scores, inputs)

    def joint_rows(part):
        return slice(part * padded, (part + 1) * padded)

    def pack_job(turn):
        for part in range(3):

            @pl.when(turn == part * (plan.jobs["pack"][1] > 1))
            def _():
                value = r.qkv[:, part * width : (part + 1) * width].astype(BF16)
                r.sw[joint_rows(part), :] = value
                if part != 1:
                    row = 2 if part == 0 else 3
                    r.sums[row : row + 1, :] = jnp.sum(value.astype(F32), axis=0, keepdims=True)

    def first_job(turn):
        def one(tile):
            cols = aligned(tile * TILE, TILE, TILE)
            total = None
            for part in range(3):
                value = matmul(
                    r.sw[joint_rows(part), :],
                    r.jw[cols, part * width : (part + 1) * width],
                    ((1,), (1,)),
                )
                total = value if total is None else total + value
            r.acc_grad[:, cols] = total

        share("first", width // TILE, turn, one)

    def input_job(turn):
        def one(item):
            here = item_rows(item)
            unit, spread = normalized(r.tok[item].astype(F32))
            grad = r.acc_grad[here, :]
            r.sums[0:1, :] += jnp.sum(grad * unit, axis=0, keepdims=True)
            r.sums[1:2, :] += jnp.sum(grad, axis=0, keepdims=True)
            total = r.acc_out[here, :] + norm_backward(grad * vector(0), unit, spread)
            r.tok[item] = total.astype(BF16)

        share("input", plan.items, turn, one)

        @pl.when(turn == 0)
        def _():
            per_row = width // TILE
            for tile in range(plan.ff_tiles):
                row, start = 8 + tile // per_row, tile % per_row * TILE
                r.sums[row : row + 1, start : start + TILE] = r.expand_sums[tile]

    def when(condition, action):
        if condition is True:
            action()
        else:
            pl.when(condition)(action)

    def roles(move):
        if move.kind == "fold":
            return outer, inner
        if move.kind == "unfold":
            return inner, outer
        return (inner, inner) if move.inner else (True, True)

    def land(number, stage, item):
        ref = getattr(r, f"land{number}_{stage}")
        return ref.at[lax.rem(item, plan.parts[number].slots(stage))]

    def source(number, stage, item):
        if stage == 0:
            return getattr(r, f"part{number}").at[lax.rem(item, 2)]
        return land(number, stage - 1, item)

    kept, given, regions = {}, {}, {}
    for number, part in enumerate(plan.parts):
        for stage, move in enumerate(part.moves):
            bit = bits[move.select] if move.select else 0
            kept[number, stage] = bit * move.length
            given[number, stage] = (1 - bit) * move.length if move.select else 0
            regions[number, stage] = sum(
                bits[select] * size for select, size in part.selects if size >= move.length
            )

    def in_whole(number, stage, item):
        part = plan.parts[number]
        return (
            item,
            aligned(regions[number, stage], part.moves[stage].length, SUB),
            pl.ds(part.column, part.columns),
        )

    def transfer(number, stage, item):
        part = plan.parts[number]
        move = part.moves[stage]
        arrival = plan.arrival_at[number, stage] + lax.rem(item, part.slots(stage))
        send = plan.send_at[number, stage] + lax.rem(item, part.flights(stage))
        if stage < len(part.sums):
            src = source(number, stage, item).at[
                aligned(given[number, stage], move.length, SUB)
            ]
            dst = land(number, stage, item)
        else:
            src = r.whole.at[in_whole(number, stage, item)]
            dst = src
        return pltpu.make_async_remote_copy(
            src_ref=src,
            dst_ref=dst,
            send_sem=r.send_sems.at[send],
            recv_sem=r.recv_sems.at[arrival],
            device_id=partners[move.flips],
            device_id_type=MESH,
        )

    def begin(number, stage, item):
        sender, _ = roles(plan.parts[number].moves[stage])
        when(sender, lambda: transfer(number, stage, item).start())

    def settle(number, stage, item):
        part = plan.parts[number]
        move = part.moves[stage]
        sender, receiver = roles(move)

        def receive():
            if stage < len(part.sums):
                land(number, stage, item)[...] += source(number, stage, item)[
                    aligned(kept[number, stage], move.length, SUB)
                ]
            if stage == len(part.sums) - 1:
                r.whole[in_whole(number, stage, item)] = land(number, stage, item)[...]

        if move.kind in ("fold", "unfold"):
            when(sender, lambda: transfer(number, stage, item).wait_send())

            def arrive():
                transfer(number, stage, item).wait_recv()
                receive()

        else:

            def arrive():
                transfer(number, stage, item).wait()
                receive()

        when(receiver, arrive)
        if stage + 1 < len(part.moves):
            begin(number, stage + 1, item)

    def rows_of(phase):
        _, count, _, windows = plan.phases[phase]
        return count // windows

    def produce(item):
        slot = lax.rem(item, 2)
        lefts = (r.active_t, r.second_t, r.mixed_t, r.first_t)
        rights = (r.grad_out, r.grad_hidden, r.grad_branch, r.sw)
        for phase, (start, count, rows_block, windows) in enumerate(plan.phases):
            left, right = lefts[phase], rights[phase]

            @pl.when((item >= start) & (item < start + count))
            def _():
                local = item - start
                tall = rows_of(phase)
                row = lax.rem(local, tall) * chunk
                window = lax.div(local, tall)
                for number, part in enumerate(plan.parts):
                    picked = [
                        left[aligned(block * rows_block + row + offset, size, size), :]
                        for block, offset, size in part.picks
                    ]
                    if phase == 3:
                        other = right[
                            aligned(window * padded, padded, 256),
                            part.column : part.column + part.columns,
                        ]
                    else:
                        other = right[
                            :, aligned(window * width + part.column, part.columns, 128)
                        ]
                    getattr(r, f"part{number}")[slot] = matmul(
                        jnp.concatenate(picked, axis=0), other
                    )

    def vector_source(stage):
        return getattr(r, f"vector{stage}")

    def vector_part(stage, own):
        before, after = plan.vector_lengths[stage : stage + 2]
        if before == after:
            return pl.ds(0, after)
        bit = bits[plan.links[stage][0]]
        return aligned((bit if own else 1 - bit) * after, after, SUB)

    def vector_exchange(stage):
        return pltpu.make_async_remote_copy(
            src_ref=vector_source(stage).at[vector_part(stage, False)],
            dst_ref=vector_source(stage + 1),
            send_sem=r.vector_sems.at[0, stage],
            recv_sem=r.vector_sems.at[1, stage],
            device_id=partners[plan.links[stage]],
            device_id_type=MESH,
        )

    def vector_pack():
        r.vector0[...] = jnp.zeros_like(r.vector0)
        block = plan.block
        for spot, owner in enumerate(plan.block_order):
            base = spot * plan.vector_rows
            own = slice(owner * block, (owner + 1) * block)
            r.vector0[base : base + 8, :block] = r.sums[:8, own]
            for piece in range(plan.ff // width):
                place = owner * (plan.ff // narrow) + piece * block
                row, start = 8 + place // width, place % width
                r.vector0[base + 8 + piece : base + 9 + piece, :block] = r.sums[
                    row : row + 1, start : start + block
                ]

    def vector_step(tick):
        count = len(plan.links)
        for stage in range(count + 1):

            @pl.when(tick == plan.vector_tick + stage * plan.vector_every)
            def _():
                if stage == 0:
                    vector_pack()
                else:
                    vector_exchange(stage - 1).wait()
                    vector_source(stage)[...] += vector_source(stage - 1)[
                        vector_part(stage - 1, True)
                    ]
                if stage < count:
                    vector_exchange(stage).start()

    pl.semaphore_wait(barrier, len(plan.links))

    def open_chunk(item):
        produce(item)
        for number in range(len(plan.parts)):
            begin(number, 0, item)

    def step(tick, carry):
        for stage in range(plan.stages):
            if stage == 1:
                pl.when(tick < plan.chunks)(functools.partial(open_chunk, tick))
            for number, part in enumerate(plan.parts):
                if stage < len(part.moves):
                    item = tick - part.due[stage]

                    @pl.when((item >= 0) & (item < plan.chunks))
                    def _():
                        settle(number, stage, item)

        vector_step(tick)
        @pl.when(tick == 0)
        def _():
            for ref in (r.acc_out, r.acc_grad):
                ref[...] = jnp.zeros_like(ref)

        run = {
            "ff": ff_job,
            "norm": norm_job,
            "mix": mix_job,
            "item": item_job,
            "pack": pack_job,
            "first": first_job,
            "input": input_job,
        }
        for name, (start, count) in plan.jobs.items():
            job = functools.partial(run[name], tick - start)
            pl.when((tick >= start) & (tick < start + count))(job)

        return carry

    lax.fori_loop(0, plan.ticks, step, 0)
    r.vector_out[...] = vector_source(len(plan.links))[...]


def write_kernel(plan, tok, cot, whole, sums, *refs):
    outs, held, sems = refs[:15], refs[15:-1], refs[-1]
    copies = [(tok, outs[0]), (cot, outs[1])]
    for (start, count, _, windows), out in zip(plan.phases, outs[2:6]):
        tall = count // windows
        for window in range(windows):
            first = start + window * tall
            cols = pl.ds(window * plan.width, plan.width)
            copies.append((whole.at[first : first + tall], out.at[:, :, cols]))
    copies = [
        pltpu.make_async_copy(source, target, sems.at[number])
        for number, (source, target) in enumerate(copies)
    ]
    for copy in copies:
        copy.start()
    for row, ref in enumerate(held[:8]):
        ref[...] = sums[row : row + 1, : plan.block].reshape(plan.block)
    pieces = [
        sums[8 + piece : 9 + piece, : plan.block] for piece in range(plan.ff // plan.width)
    ]
    held[8][...] = jnp.concatenate(pieces, axis=1).reshape(plan.ff // plan.narrow)
    for source, target in zip(held, outs[6:]):
        copy = pltpu.make_async_copy(source, target, sems.at[len(copies)])
        copy.start()
        copies.append(copy)
    for copy in copies:
        copy.wait()


def shards(
    tokens,
    visible,
    first_gain,
    first_shift,
    joint_weight,
    query_bias,
    value_bias,
    mixer_weight,
    mixer_bias,
    second_gain,
    second_shift,
    expand_weight,
    expand_bias,
    shrink_weight,
    shrink_bias,
    cotangent,
):
    items, slots, width = tokens.shape
    ff = expand_weight.shape[1]
    narrow, wide = lax.axis_size("narrow"), lax.axis_size("wide")
    plan = Plan(narrow, wide, items, slots, width, ff)
    padded, chunk = plan.padded, plan.chunk
    hbm = pl.BlockSpec(memory_space=pl.ANY)
    vmem = pl.BlockSpec(memory_space=pltpu.VMEM)
    smem = pl.BlockSpec(memory_space=pltpu.SMEM)
    inputs = {
        "visible": (visible, smem),
        "g1": (first_gain, vmem),
        "s1": (first_shift, vmem),
        "qb": (query_bias, vmem),
        "vb": (value_bias, vmem),
        "mb": (mixer_bias, vmem),
        "g2": (second_gain, vmem),
        "s2": (second_shift, vmem),
        "sb": (shrink_bias, vmem),
        "eb": (expand_bias, vmem),
        "tok_in": (tokens, hbm),
        "cot_in": (cotangent, hbm),
        "jw_in": (joint_weight, hbm),
        "mw_in": (mixer_weight, hbm),
        "ew_in": (expand_weight, hbm),
        "sw_in": (shrink_weight, hbm),
    }
    block = width // narrow
    outputs = {
        "tok": (tokens.shape, BF16),
        "cot": (tokens.shape, BF16),
        "whole": ((plan.chunks, chunk, width), F32),
        "vector_out": ((plan.vector_rows, plan.block_lanes), F32),
    }
    scratch = {
        "jw": pltpu.VMEM(joint_weight.shape, BF16),
        "mw": pltpu.VMEM(mixer_weight.shape, BF16),
        "ew": pltpu.VMEM(expand_weight.shape, BF16),
        "sw": pltpu.VMEM(shrink_weight.shape, BF16),
        "stage": pltpu.VMEM((padded, width), F32),
        "first_rows": pltpu.VMEM((padded, width), BF16),
        "mixed_rows": pltpu.VMEM((padded, width), BF16),
        "qkv": pltpu.VMEM((padded, 3 * width), F32),
        "attend": pltpu.VMEM((items * plan.pairs, 2 * slots, slots), F32),
        "first_t": pltpu.VMEM((width, padded), BF16),
        "mixed_t": pltpu.VMEM((width, padded), BF16),
        "second": pltpu.VMEM((padded, width), BF16),
        "second_t": pltpu.VMEM((width, padded), BF16),
        "middle": pltpu.VMEM((padded, width), F32),
        "grad_hidden": pltpu.VMEM((padded, ff), BF16),
        "active_t": pltpu.VMEM((ff, padded), BF16),
        "grad_out": pltpu.VMEM((padded, width), BF16),
        "acc_out": pltpu.VMEM((padded, width), F32),
        "acc_grad": pltpu.VMEM((padded, width), F32),
        "grad_branch": pltpu.VMEM((padded, width), BF16),
        "vec": pltpu.VMEM((plan.vector_rows, width), F32),
        "grad_logits": pltpu.VMEM((plan.pairs, 2 * slots, slots), BF16),
        "sums": pltpu.VMEM((plan.vector_rows, width), F32),
        "expand_sums": pltpu.VMEM((plan.ff_tiles, 1, TILE), F32),
        "load_sems": pltpu.SemaphoreType.DMA((6,)),
        "vector_sems": pltpu.SemaphoreType.DMA((2, len(plan.links))),
        "send_sems": pltpu.SemaphoreType.DMA((plan.sends,)),
        "recv_sems": pltpu.SemaphoreType.DMA((plan.arrivals,)),
    }
    for stage, length in enumerate(plan.vector_lengths):
        scratch[f"vector{stage}"] = pltpu.VMEM((length, plan.block_lanes), F32)
    for number, part in enumerate(plan.parts):
        scratch[f"part{number}"] = pltpu.VMEM((2, narrow * chunk, part.columns), F32)
        for stage, move in enumerate(part.sums):
            scratch[f"land{number}_{stage}"] = pltpu.VMEM(
                (part.slots(stage), move.length, part.columns), F32
            )
    results = pl.pallas_call(
        functools.partial(layer_kernel, plan, (*inputs, *outputs, *scratch)),
        out_shape=[pltpu.VMEM(shape, kind) for shape, kind in outputs.values()],
        in_specs=[spec for _, spec in inputs.values()],
        out_specs=[vmem] * len(outputs),
        scratch_shapes=list(scratch.values()),
        compiler_params=pltpu.CompilerParams(
            has_side_effects=True, vmem_limit_bytes=52 * 2**20, collective_id=0
        ),
        name="layer",
    )(*(value for value, _ in inputs.values()))
    row_counts = [count // windows for _, count, _, windows in plan.phases]
    shapes = [jax.ShapeDtypeStruct(tokens.shape, BF16)] * 2
    shapes += [
        jax.ShapeDtypeStruct((tall, chunk, windows * width), F32)
        for tall, (_, _, _, windows) in zip(row_counts, plan.phases)
    ]
    shapes += [jax.ShapeDtypeStruct((block,), F32)] * 8
    shapes += [jax.ShapeDtypeStruct((ff // narrow,), F32)]
    copies = 2 + sum(windows for _, _, _, windows in plan.phases)
    outs = pl.pallas_call(
        functools.partial(write_kernel, plan),
        out_shape=shapes,
        in_specs=[vmem] * len(results),
        out_specs=[hbm] * 15,
        scratch_shapes=[pltpu.VMEM(shape.shape, F32) for shape in shapes[6:]]
        + [pltpu.SemaphoreType.DMA((copies + 9,))],
        compiler_params=pltpu.CompilerParams(vmem_limit_bytes=4 * 2**20),
        name="write",
    )(*(pltpu.with_memory_space_constraint(value, pltpu.VMEM) for value in results))
    input_grad, layer_out = outs[:2]
    shrink, expand, mixer, joint = (
        out.reshape(-1, out.shape[-1]) for out in outs[2:6]
    )
    vectors = outs[6:]
    return (
        layer_out,
        input_grad,
        vectors[0],
        vectors[1],
        joint,
        vectors[2],
        vectors[3],
        mixer,
        vectors[4],
        vectors[5],
        vectors[6],
        expand,
        vectors[8],
        shrink,
        vectors[7],
    )


def solution(mesh):
    return jax.shard_map(
        shards,
        mesh=mesh,
        in_specs=(
            P(("wide", "narrow"), None, None),
            P(("wide", "narrow")),
            P(),
            P(),
            P(),
            P(),
            P(),
            P(),
            P(),
            P(),
            P(),
            P(),
            P(),
            P(),
            P(),
            P(("wide", "narrow"), None, None),
        ),
        out_specs=(
            P(("wide", "narrow"), None, None),
            P(("wide", "narrow"), None, None),
            P("narrow"),
            P("narrow"),
            P("narrow", None),
            P("narrow"),
            P("narrow"),
            P("narrow", None),
            P("narrow"),
            P("narrow"),
            P("narrow"),
            P("narrow", None),
            P("narrow"),
            P("narrow", None),
            P("narrow"),
        ),
        check_vma=False,
    )
```

```python
import functools
import types

import jax
import jax.numpy as jnp
from jax import lax
from jax.experimental import pallas as pl
from jax.experimental.pallas import tpu as pltpu
from jax.sharding import PartitionSpec as P

HEAD_DIM = 64
EPSILON = 1e-06
SUB = 8
LAGS = ([1, 2, 2, 2, 2, 2, 4] + [2] * 8, [1, 2, 2, 2, 2, 2, 3] + [2] * 8)
MOST = 32
TILE = 256
U1 = 7
U2 = 7
U3 = 7
U4 = 7
U5 = 4
MESH = pl.DeviceIdType.MESH
ROOT_HALF = 0.5**0.5
PEAK = 0.3989422804014327
BF16 = jnp.bfloat16
F32 = jnp.float32


def bit_of(index, place):
    return lax.rem(lax.div(index, 2**place), 2)


def reversed_bits(value, count):
    out = 0
    for place in range(count):
        out = out * 2 + (value >> place) % 2
    return out


def aligned(start, size, unit):
    return pl.ds(pl.multiple_of(start, unit), size)


def matmul(left, right, contract=((1,), (0,))):
    return lax.dot_general(left, right, (contract, ((), ())), preferred_element_type=F32)


class Move:
    def __init__(self, kind, flips, length, select=None, inner=False):
        self.kind, self.flips, self.length = kind, flips, length
        self.select, self.inner = select, inner


class Part:
    def __init__(self, column, columns, picks, sums, gathers, selects):
        self.column, self.columns, self.picks = column, columns, picks
        self.sums, self.moves = sums, sums + gathers
        self.selects = selects
        self.lags = LAGS[column > 0][: len(self.moves)]
        self.due = [sum(self.lags[: stage + 1]) for stage in range(len(self.moves))]

    def flights(self, stage):
        return self.lags[stage] + 1

    def slots(self, stage):
        after = self.lags[stage + 1] if stage + 1 < len(self.sums) else 0
        count = 2 * self.lags[stage] + after + 2
        if self.moves[stage].kind in ("fold", "unfold"):
            kinds = [move.kind for move in self.moves]
            ahead = self.due[kinds.index("unfold")] - self.due[kinds.index("fold") - 1]
            count = max(count, ahead + 2)
        return count


class Plan:
    def __init__(self, narrow, wide, items, slots, width, ff):
        self.narrow, self.wide, self.width, self.ff = narrow, wide, width, ff
        self.items, self.slots = items, slots
        self.rows = items * slots
        self.padded = self.rows + -self.rows % 256
        self.pairs = width // (2 * HEAD_DIM)
        narrow_bits = self.narrow_bits = narrow.bit_length() - 1
        wide_bits = self.wide_bits = wide.bit_length() - 1
        rows = width // narrow
        chunk = SUB
        while rows % (2 * chunk) == 0 and chunk < MOST:
            chunk *= 2
        self.chunk = chunk
        near, mirror = (("wide", 1),), (("wide", 1), ("wide", 2))
        x, y, core = (("wide", 0),), (("narrow", 1),), (("narrow", 0),)
        if (narrow, wide) == (4, 8):
            self.links = (core, y, x, near, mirror)
            half = chunk // 2
            z_bit, x_bit, y_bit, core_bit = ("wide", 2), x[0], y[0], core[0]
            one = Part(
                0,
                width // 3 * 2,
                [(spot % 2 * 2 + spot // 2, 0, chunk) for spot in range(4)],
                [
                    Move("halve", core, 2 * chunk, core_bit),
                    Move("halve", y, chunk, y_bit),
                    Move("fold", near, chunk),
                    Move("halve", mirror, half, z_bit, True),
                    Move("add", x, half, inner=True),
                ],
                [
                    Move("double", mirror, half, inner=True),
                    Move("unfold", near, chunk),
                ],
                [(z_bit, half)],
            )
            two = Part(
                width // 3 * 2,
                width // 3,
                [
                    (2 * (spot % 2) + spot // 4, spot // 2 % 2 * half, half)
                    for spot in range(8)
                ],
                [
                    Move("halve", core, 2 * chunk, core_bit),
                    Move("halve", x, chunk, x_bit),
                    Move("halve", y, half, y_bit),
                    Move("fold", near, half),
                    Move("add", mirror, half, inner=True),
                ],
                [
                    Move("unfold", near, half),
                    Move("double", x, half),
                ],
                [(x_bit, half)],
            )
            self.parts = (one, two)
        else:
            self.links = tuple((("narrow", place),) for place in range(narrow_bits))
            self.links += tuple((("wide", place),) for place in range(wide_bits))
            sums, gathers, selects = [], [], []
            length = narrow * chunk
            for (axis, place), in self.links:
                if length > SUB:
                    length //= 2
                    sums.append(Move("halve", ((axis, place),), length, (axis, place)))
                    if axis == "wide":
                        selects.append(((axis, place), length))
                        gathers.insert(0, Move("double", ((axis, place),), length))
                else:
                    sums.append(Move("add", ((axis, place),), length))
            picks = [(reversed_bits(spot, narrow_bits), 0, chunk) for spot in range(narrow)]
            self.parts = (Part(0, width, picks, sums, gathers, selects),)
        self.stages = max(len(part.moves) for part in self.parts)
        self.depth = max(part.due[-1] for part in self.parts)
        self.arrivals, self.sends, self.arrival_at, self.send_at = 0, 0, {}, {}
        for number, part in enumerate(self.parts):
            for stage in range(len(part.moves)):
                self.arrival_at[number, stage] = self.arrivals
                self.send_at[number, stage] = self.sends
                self.arrivals += part.slots(stage)
                self.sends += part.flights(stage)
        self.phases = []
        start = 0
        for rows_block, windows in (
            (ff // narrow, 1),
            (rows, ff // width),
            (rows, 1),
            (rows, 3),
        ):
            count = rows_block // chunk * windows
            self.phases.append((start, count, rows_block, windows))
            start += count
        self.chunks = start
        self.ff_tiles = ff // TILE
        self.split = self.phases[1][0] // self.ff_tiles
        assert self.split in (1, 2)
        tall = ff // narrow
        self.groups = tall // TILE if tall % TILE == 0 else 1
        self.blocks = self.ff_tiles // self.groups
        self.jobs = {}
        tick = self.split - 1
        for name, count in (
            ("ff", self.ff_tiles * self.split),
            ("norm", 1 if self.split == 1 else 4),
            ("mix", 1 if self.split == 1 else 3),
            ("item", items * self.split),
            ("pack", 1 if self.split == 1 else 3),
            ("first", 1 if self.split == 1 else 3),
            ("input", 1 if self.split == 1 else 4),
        ):
            self.jobs[name] = (tick, count)
            tick += count
        self.vector_tick = tick
        assert self.phases[2][0] >= self.jobs["item"][0]
        assert self.phases[3][0] >= self.jobs["first"][0]
        self.block = rows
        self.block_lanes = rows + -rows % 128
        self.block_order = [reversed_bits(spot, narrow_bits) for spot in range(narrow)]
        self.vector_rows = 8 + ff // width
        self.vector_rows += -self.vector_rows % SUB
        self.ticks = self.chunks + self.depth
        self.vector_lengths = [narrow * self.vector_rows]
        for flips in self.links:
            length = self.vector_lengths[-1]
            self.vector_lengths.append(length // 2 if flips[0][0] == "narrow" else length)
        self.vector_every = (self.ticks - 1 - self.vector_tick) // len(self.links)
        assert self.vector_every > 0


def layer_kernel(plan, names, *refs):
    r = types.SimpleNamespace(**dict(zip(names, refs)))
    width, chunk, narrow, slots = plan.width, plan.chunk, plan.narrow, plan.slots
    rows, padded, pairs = plan.rows, plan.padded, plan.pairs
    score_scale = HEAD_DIM ** (-0.5)
    spots = {"narrow": lax.axis_index("narrow"), "wide": lax.axis_index("wide")}
    inner = bit_of(spots["wide"], 1) != bit_of(spots["wide"], 2)
    outer = bit_of(spots["wide"], 1) == bit_of(spots["wide"], 2)

    bits = {
        (axis, place): bit_of(spots[axis], place)
        for axis, count in (("narrow", plan.narrow_bits), ("wide", plan.wide_bits))
        for place in range(count)
    }
    partners = {}
    for flips in plan.links:
        there = dict(spots)
        for axis, place in flips:
            there[axis] = there[axis] + (1 - 2 * bits[axis, place]) * 2**place
        partners[flips] = there

    loads = {}
    for number, name in enumerate(("tok", "jw", "mw", "ew", "cot", "sw")):
        loads[name] = pltpu.make_async_copy(
            getattr(r, name + "_in"), getattr(r, name), r.load_sems.at[number]
        )
    loads["tok"].start()
    loads["cot"].start()
    loads["jw"].start()

    barrier = pltpu.get_barrier_semaphore()
    for flips in plan.links:
        pl.semaphore_signal(barrier, inc=1, device_id=partners[flips], device_id_type=MESH)

    def vector(row):
        return r.vec[row : row + 1, :]

    def item_rows(item):
        return aligned(item * slots, slots, SUB)

    def row_live(item):
        return lax.broadcasted_iota(jnp.int32, (slots, 1), 0) < r.visible[item]

    lanes = lax.broadcasted_iota(jnp.int32, (slots, 2 * HEAD_DIM), 1)
    first_head = lanes < HEAD_DIM

    def both_heads(value):
        zero = jnp.zeros_like(value)
        return jnp.concatenate(
            [jnp.where(first_head, value, zero), jnp.where(first_head, zero, value)], axis=0
        ).astype(BF16)

    def one_head_each(value):
        return jnp.where(first_head, value[:slots], value[slots:])

    def normalized(values):
        center = values - jnp.mean(values, axis=-1, keepdims=True)
        spread = lax.rsqrt(jnp.mean(center * center, axis=-1, keepdims=True) + EPSILON)
        return center * spread, spread

    def norm_backward(grad, unit, spread):
        return spread * (
            grad
            - jnp.mean(grad, axis=-1, keepdims=True)
            - unit * jnp.mean(grad * unit, axis=-1, keepdims=True)
        )

    def each_item(body, unroll=1):
        lax.fori_loop(
            0, plan.items, lambda item, carry: (body(item), carry)[1], 0, unroll=unroll
        )

    def each_tile(count, body, unroll=1):
        lax.fori_loop(
            0, count, lambda tile, carry: (body(tile), carry)[1], 0, unroll=unroll
        )

    def pair_lanes(part, pair):
        start = part * width + pair * 2 * HEAD_DIM
        return slice(start, start + 2 * HEAD_DIM)

    small = (r.g1, r.s1, r.qb, r.vb, r.mb, r.g2, r.s2, r.sb)

    def place_small(first, last):
        for row in range(first, last):
            r.vec[row : row + 1, :] = small[row][...].astype(F32).reshape(1, width)

    place_small(0, 2)
    r.stage[rows:, :] = jnp.zeros((padded - rows, width), F32)
    r.sums[...] = jnp.zeros_like(r.sums)
    loads["tok"].wait()

    def first_norm(item):
        unit, _ = normalized(r.tok[item].astype(F32))
        r.stage[item_rows(item), :] = unit * vector(0) + vector(1)

    each_item(first_norm, U1)
    r.first_rows[...] = r.stage[...].astype(BF16)
    for name in ("mw", "ew", "sw"):
        loads[name].start()
    loads["cot"].wait()

    def mask_cotangent(item):
        grad = r.cot[item].astype(F32)
        r.stage[item_rows(item), :] = jnp.where(row_live(item), grad, 0.0)

    each_item(mask_cotangent, U3)
    r.grad_out[...] = r.stage[...].astype(BF16)
    place_small(2, 8)
    for row in range(plan.ff // width):
        value = r.eb[row * width : (row + 1) * width].astype(F32)
        r.vec[8 + row : 9 + row, :] = value.reshape(1, width)
    loads["jw"].wait()
    for part, bias in enumerate((2, None, 3)):

        cols = slice(part * width, (part + 1) * width)
        value = matmul(r.first_rows[...], r.jw[:, cols])
        if bias is not None:
            value = value + vector(bias)
        r.qkv[:, cols] = value.astype(BF16).astype(F32)
    r.qkv[rows:, :] = jnp.zeros((padded - rows, 3 * width), F32)

    def attend_item(item):
        here = item_rows(item)
        key_live = (
            lax.broadcasted_iota(jnp.int32, (2 * slots, slots), 1) < r.visible[item]
        )
        every = range(pairs)
        queries = [both_heads(r.qkv[here, pair_lanes(0, pair)]) for pair in every]
        keys = [r.qkv[here, pair_lanes(1, pair)].astype(BF16) for pair in every]
        values = [r.qkv[here, pair_lanes(2, pair)].astype(BF16) for pair in every]
        logits = [matmul(queries[pair], keys[pair], ((1,), (1,))) for pair in every]
        logits = [jnp.where(key_live, value * score_scale, -1000000000.0) for value in logits]
        tops = [jnp.max(value, axis=-1, keepdims=True) for value in logits]
        expos = [jnp.exp(logits[pair] - tops[pair]) for pair in every]
        totals = [jnp.sum(value, axis=-1, keepdims=True) for value in expos]
        attends = [expos[pair] * (1.0 / totals[pair]) for pair in every]
        mixed = [matmul(attends[pair].astype(BF16), values[pair]) for pair in every]
        for pair in every:
            r.attend[item * pairs + pair] = attends[pair]
            r.stage[here, pair_lanes(0, pair)] = one_head_each(mixed[pair])

    each_item(attend_item, U4)
    r.mixed_rows[...] = r.stage[...].astype(BF16)
    loads["mw"].wait()

    r.middle[...] = matmul(r.mixed_rows[...], r.mw[...]) + vector(4)

    def second_norm(item):
        here = item_rows(item)
        middle = r.middle[here, :] + r.tok[item].astype(F32)
        r.middle[here, :] = middle
        unit, _ = normalized(middle)
        r.stage[here, :] = unit * vector(5) + vector(6)

    each_item(second_norm, U2)
    r.second[...] = r.stage[...].astype(BF16)
    loads["ew"].wait()

    def expand_bias(tile):
        per_row = width // TILE
        return r.vec[
            pl.ds(8 + lax.div(tile, per_row), 1),
            aligned(lax.rem(tile, per_row) * TILE, TILE, TILE),
        ]

    def hidden_tile(tile):
        cols = aligned(tile * TILE, TILE, TILE)
        hidden = matmul(r.second[...], r.ew[:, cols]) + expand_bias(tile)
        return hidden, 0.5 + 0.5 * lax.erf(hidden * ROOT_HALF)

    def expand_tile(place):
        tile = place * plan.groups
        hidden, normal = hidden_tile(tile)
        r.active_t[aligned(tile * TILE, TILE, TILE), :] = (hidden * normal).astype(BF16).T

    each_tile(plan.blocks, expand_tile, U5)
    loads["sw"].wait()

    rows_full = rows // 16 * 16

    def share(name, count, turn, body):
        size = -(-count // plan.jobs[name][1])
        first = turn * size
        last = jnp.minimum(first + size, count)
        lax.fori_loop(first, last, lambda place, carry: (body(place), carry)[1], 0)

    def in_turns(turn, first_half, second_half):
        number = lax.div(turn, plan.split)
        if plan.split == 1:
            first_half(number)
            second_half(number)
        else:
            half = lax.rem(turn, plan.split)
            pl.when(half == 0)(lambda: first_half(number))
            pl.when(half == 1)(lambda: second_half(number))

    def ff_job(turn):
        def tile_job(number):
            group = lax.rem(lax.div(number, plan.blocks) + 1, plan.groups)
            tile = lax.rem(number, plan.blocks) * plan.groups + group
            cols = aligned(tile * TILE, TILE, TILE)
            hidden, normal = hidden_tile(tile)
            active = (hidden * normal).astype(BF16)
            r.active_t[cols, :] = active.T
            slope = normal + hidden * (PEAK * jnp.exp(-0.5 * hidden * hidden))
            grad = matmul(r.grad_out[...], r.sw[cols, :], ((1,), (1,)))
            grad_hidden = (grad * slope).astype(BF16)
            r.grad_hidden[:, cols] = grad_hidden
            r.expand_sums[tile] = jnp.sum(grad_hidden.astype(F32), axis=0, keepdims=True)
            r.acc_out[...] += matmul(active, r.sw[cols, :])
            r.acc_grad[...] += matmul(grad_hidden, r.ew[:, cols], ((1,), (1,)))

        in_turns(turn, tile_job, turn_rows)

    def turn_rows(turn):
        for place, (rows_ref, turned) in enumerate(
            (
                (r.second, r.second_t),
                (r.mixed_rows, r.mixed_t),
                (r.first_rows, r.first_t),
            )
        ):

            @pl.when(turn == place)
            def _():
                turned[...] = rows_ref[...].T

    def norm_job(turn):
        def one(item):
            here = item_rows(item)
            live = row_live(item)
            middle = r.middle[here, :]
            grad_out = jnp.where(live, r.cot[item].astype(F32), 0.0)
            layer_out = jnp.where(live, middle + (r.acc_out[here, :] + vector(7)), 0.0)
            r.cot[item] = layer_out.astype(BF16)
            unit, spread = normalized(middle)
            grad = r.acc_grad[here, :]
            r.sums[5:6, :] += jnp.sum(grad * unit, axis=0, keepdims=True)
            r.sums[6:7, :] += jnp.sum(grad, axis=0, keepdims=True)
            r.sums[7:8, :] += jnp.sum(grad_out, axis=0, keepdims=True)
            grad_middle = grad_out + norm_backward(grad * vector(5), unit, spread)
            r.acc_out[here, :] = grad_middle
            r.sums[4:5, :] += jnp.sum(
                grad_middle.astype(BF16).astype(F32), axis=0, keepdims=True
            )

        share("norm", plan.items, turn, one)

    def mix_job(turn):
        pl.when(turn == 0)(pack_branch)

        def one(tile):
            cols = aligned(tile * TILE, TILE, TILE)
            value = matmul(r.grad_branch[...], r.mw[cols, :], ((1,), (1,)))
            r.stage[:, cols] = value.astype(BF16).astype(F32)

        share("mix", width // TILE, turn, one)

    def pack_branch():
        r.grad_branch[:rows_full, :] = r.acc_out[:rows_full, :].astype(BF16)
        tail = jnp.concatenate(
            [r.acc_out[rows_full:rows, :], jnp.zeros((padded - rows, width), F32)], axis=0
        )
        r.grad_branch[rows_full:, :] = tail.astype(BF16)

    def item_job(turn):
        def scores(item):
            here = item_rows(item)
            for pair in range(pairs):
                values = r.qkv[here, pair_lanes(2, pair)].astype(BF16)
                grad_mixed = both_heads(r.stage[here, pair_lanes(0, pair)])
                attend = r.attend[item * pairs + pair]
                grad_attend = matmul(grad_mixed, values, ((1,), (1,)))
                inner_sum = jnp.sum(attend * grad_attend, axis=-1, keepdims=True)
                r.grad_logits[pair] = (attend * (grad_attend - inner_sum)).astype(BF16)
                r.qkv[here, pair_lanes(2, pair)] = matmul(
                    attend.astype(BF16), grad_mixed, ((0,), (0,))
                )

        def inputs(item):
            here = item_rows(item)
            for pair in range(pairs):
                query = both_heads(r.qkv[here, pair_lanes(0, pair)])
                keys = r.qkv[here, pair_lanes(1, pair)].astype(BF16)
                grad_logits = r.grad_logits[pair]
                grad_query = one_head_each(matmul(grad_logits, keys)) * score_scale
                grad_key = matmul(grad_logits, query, ((0,), (0,))) * score_scale
                r.qkv[here, pair_lanes(0, pair)] = grad_query
                r.qkv[here, pair_lanes(1, pair)] = grad_key

        in_turns(turn, scores, inputs)

    def joint_rows(part):
        return slice(part * padded, (part + 1) * padded)

    def pack_job(turn):
        for part in range(3):

            @pl.when(turn == part * (plan.jobs["pack"][1] > 1))
            def _():
                value = r.qkv[:, part * width : (part + 1) * width].astype(BF16)
                r.sw[joint_rows(part), :] = value
                if part != 1:
                    row = 2 if part == 0 else 3
                    r.sums[row : row + 1, :] = jnp.sum(value.astype(F32), axis=0, keepdims=True)

    def first_job(turn):
        def one(tile):
            cols = aligned(tile * TILE, TILE, TILE)
            total = None
            for part in range(3):
                value = matmul(
                    r.sw[joint_rows(part), :],
                    r.jw[cols, part * width : (part + 1) * width],
                    ((1,), (1,)),
                )
                total = value if total is None else total + value
            r.acc_grad[:, cols] = total

        share("first", width // TILE, turn, one)

    def input_job(turn):
        def one(item):
            here = item_rows(item)
            unit, spread = normalized(r.tok[item].astype(F32))
            grad = r.acc_grad[here, :]
            r.sums[0:1, :] += jnp.sum(grad * unit, axis=0, keepdims=True)
            r.sums[1:2, :] += jnp.sum(grad, axis=0, keepdims=True)
            total = r.acc_out[here, :] + norm_backward(grad * vector(0), unit, spread)
            r.tok[item] = total.astype(BF16)

        share("input", plan.items, turn, one)

        @pl.when(turn == 0)
        def _():
            per_row = width // TILE
            for tile in range(plan.ff_tiles):
                row, start = 8 + tile // per_row, tile % per_row * TILE
                r.sums[row : row + 1, start : start + TILE] = r.expand_sums[tile]

    def when(condition, action):
        if condition is True:
            action()
        else:
            pl.when(condition)(action)

    def roles(move):
        if move.kind == "fold":
            return outer, inner
        if move.kind == "unfold":
            return inner, outer
        return (inner, inner) if move.inner else (True, True)

    def land(number, stage, item):
        ref = getattr(r, f"land{number}_{stage}")
        return ref.at[lax.rem(item, plan.parts[number].slots(stage))]

    def source(number, stage, item):
        if stage == 0:
            return getattr(r, f"part{number}").at[lax.rem(item, 2)]
        return land(number, stage - 1, item)

    kept, given, regions = {}, {}, {}
    for number, part in enumerate(plan.parts):
        for stage, move in enumerate(part.moves):
            bit = bits[move.select] if move.select else 0
            kept[number, stage] = bit * move.length
            given[number, stage] = (1 - bit) * move.length if move.select else 0
            regions[number, stage] = sum(
                bits[select] * size for select, size in part.selects if size >= move.length
            )

    def in_whole(number, stage, item):
        part = plan.parts[number]
        return (
            item,
            aligned(regions[number, stage], part.moves[stage].length, SUB),
            pl.ds(part.column, part.columns),
        )

    def transfer(number, stage, item):
        part = plan.parts[number]
        move = part.moves[stage]
        arrival = plan.arrival_at[number, stage] + lax.rem(item, part.slots(stage))
        send = plan.send_at[number, stage] + lax.rem(item, part.flights(stage))
        if stage < len(part.sums):
            src = source(number, stage, item).at[
                aligned(given[number, stage], move.length, SUB)
            ]
            dst = land(number, stage, item)
        else:
            src = r.whole.at[in_whole(number, stage, item)]
            dst = src
        return pltpu.make_async_remote_copy(
            src_ref=src,
            dst_ref=dst,
            send_sem=r.send_sems.at[send],
            recv_sem=r.recv_sems.at[arrival],
            device_id=partners[move.flips],
            device_id_type=MESH,
        )

    def begin(number, stage, item):
        sender, _ = roles(plan.parts[number].moves[stage])
        when(sender, lambda: transfer(number, stage, item).start())

    def settle(number, stage, item):
        part = plan.parts[number]
        move = part.moves[stage]
        sender, receiver = roles(move)

        def receive():
            if stage < len(part.sums):
                land(number, stage, item)[...] += source(number, stage, item)[
                    aligned(kept[number, stage], move.length, SUB)
                ]
            if stage == len(part.sums) - 1:
                r.whole[in_whole(number, stage, item)] = land(number, stage, item)[...]

        if move.kind in ("fold", "unfold"):
            when(sender, lambda: transfer(number, stage, item).wait_send())

            def arrive():
                transfer(number, stage, item).wait_recv()
                receive()

        else:

            def arrive():
                transfer(number, stage, item).wait()
                receive()

        when(receiver, arrive)
        if stage + 1 < len(part.moves):
            begin(number, stage + 1, item)

    def rows_of(phase):
        _, count, _, windows = plan.phases[phase]
        return count // windows

    def produce(item):
        slot = lax.rem(item, 2)
        lefts = (r.active_t, r.second_t, r.mixed_t, r.first_t)
        rights = (r.grad_out, r.grad_hidden, r.grad_branch, r.sw)
        for phase, (start, count, rows_block, windows) in enumerate(plan.phases):
            left, right = lefts[phase], rights[phase]

            @pl.when((item >= start) & (item < start + count))
            def _():
                local = item - start
                tall = rows_of(phase)
                row = lax.rem(local, tall) * chunk
                window = lax.div(local, tall)
                for number, part in enumerate(plan.parts):
                    picked = [
                        left[aligned(block * rows_block + row + offset, size, size), :]
                        for block, offset, size in part.picks
                    ]
                    if phase == 3:
                        other = right[
                            aligned(window * padded, padded, 256),
                            part.column : part.column + part.columns,
                        ]
                    else:
                        other = right[
                            :, aligned(window * width + part.column, part.columns, 128)
                        ]
                    getattr(r, f"part{number}")[slot] = matmul(
                        jnp.concatenate(picked, axis=0), other
                    )

    def vector_source(stage):
        return getattr(r, f"vector{stage}")

    def vector_part(stage, own):
        before, after = plan.vector_lengths[stage : stage + 2]
        if before == after:
            return pl.ds(0, after)
        bit = bits[plan.links[stage][0]]
        return aligned((bit if own else 1 - bit) * after, after, SUB)

    def vector_exchange(stage):
        return pltpu.make_async_remote_copy(
            src_ref=vector_source(stage).at[vector_part(stage, False)],
            dst_ref=vector_source(stage + 1),
            send_sem=r.vector_sems.at[0, stage],
            recv_sem=r.vector_sems.at[1, stage],
            device_id=partners[plan.links[stage]],
            device_id_type=MESH,
        )

    def vector_pack():
        r.vector0[...] = jnp.zeros_like(r.vector0)
        block = plan.block
        for spot, owner in enumerate(plan.block_order):
            base = spot * plan.vector_rows
            own = slice(owner * block, (owner + 1) * block)
            r.vector0[base : base + 8, :block] = r.sums[:8, own]
            for piece in range(plan.ff // width):
                place = owner * (plan.ff // narrow) + piece * block
                row, start = 8 + place // width, place % width
                r.vector0[base + 8 + piece : base + 9 + piece, :block] = r.sums[
                    row : row + 1, start : start + block
                ]

    def vector_step(tick):
        count = len(plan.links)
        for stage in range(count + 1):

            @pl.when(tick == plan.vector_tick + stage * plan.vector_every)
            def _():
                if stage == 0:
                    vector_pack()
                else:
                    vector_exchange(stage - 1).wait()
                    vector_source(stage)[...] += vector_source(stage - 1)[
                        vector_part(stage - 1, True)
                    ]
                if stage < count:
                    vector_exchange(stage).start()

    pl.semaphore_wait(barrier, len(plan.links))

    def open_chunk(item):
        produce(item)
        for number in range(len(plan.parts)):
            begin(number, 0, item)

    def step(tick, carry):
        for stage in range(plan.stages):
            if stage == 1:
                pl.when(tick < plan.chunks)(functools.partial(open_chunk, tick))
            for number, part in enumerate(plan.parts):
                if stage < len(part.moves):
                    item = tick - part.due[stage]

                    @pl.when((item >= 0) & (item < plan.chunks))
                    def _():
                        settle(number, stage, item)

        vector_step(tick)
        @pl.when(tick == 0)
        def _():
            for ref in (r.acc_out, r.acc_grad):
                ref[...] = jnp.zeros_like(ref)

        run = {
            "ff": ff_job,
            "norm": norm_job,
            "mix": mix_job,
            "item": item_job,
            "pack": pack_job,
            "first": first_job,
            "input": input_job,
        }
        for name, (start, count) in plan.jobs.items():
            job = functools.partial(run[name], tick - start)
            pl.when((tick >= start) & (tick < start + count))(job)

        return carry

    lax.fori_loop(0, plan.ticks, step, 0)
    r.vector_out[...] = vector_source(len(plan.links))[...]


def write_kernel(plan, tok, cot, whole, sums, *refs):
    outs, held, sems = refs[:15], refs[15:-1], refs[-1]
    copies = [(tok, outs[0]), (cot, outs[1])]
    for (start, count, _, windows), out in zip(plan.phases, outs[2:6]):
        tall = count // windows
        for window in range(windows):
            first = start + window * tall
            cols = pl.ds(window * plan.width, plan.width)
            copies.append((whole.at[first : first + tall], out.at[:, :, cols]))
    copies = [
        pltpu.make_async_copy(source, target, sems.at[number])
        for number, (source, target) in enumerate(copies)
    ]
    for copy in copies:
        copy.start()
    for row, ref in enumerate(held[:8]):
        ref[...] = sums[row : row + 1, : plan.block].reshape(plan.block)
    pieces = [
        sums[8 + piece : 9 + piece, : plan.block] for piece in range(plan.ff // plan.width)
    ]
    held[8][...] = jnp.concatenate(pieces, axis=1).reshape(plan.ff // plan.narrow)
    for source, target in zip(held, outs[6:]):
        copy = pltpu.make_async_copy(source, target, sems.at[len(copies)])
        copy.start()
        copies.append(copy)
    for copy in copies:
        copy.wait()


def shards(
    tokens,
    visible,
    first_gain,
    first_shift,
    joint_weight,
    query_bias,
    value_bias,
    mixer_weight,
    mixer_bias,
    second_gain,
    second_shift,
    expand_weight,
    expand_bias,
    shrink_weight,
    shrink_bias,
    cotangent,
):
    items, slots, width = tokens.shape
    ff = expand_weight.shape[1]
    narrow, wide = lax.axis_size("narrow"), lax.axis_size("wide")
    plan = Plan(narrow, wide, items, slots, width, ff)
    padded, chunk = plan.padded, plan.chunk
    hbm = pl.BlockSpec(memory_space=pl.ANY)
    vmem = pl.BlockSpec(memory_space=pltpu.VMEM)
    smem = pl.BlockSpec(memory_space=pltpu.SMEM)
    inputs = {
        "visible": (visible, smem),
        "g1": (first_gain, vmem),
        "s1": (first_shift, vmem),
        "qb": (query_bias, vmem),
        "vb": (value_bias, vmem),
        "mb": (mixer_bias, vmem),
        "g2": (second_gain, vmem),
        "s2": (second_shift, vmem),
        "sb": (shrink_bias, vmem),
        "eb": (expand_bias, vmem),
        "tok_in": (tokens, hbm),
        "cot_in": (cotangent, hbm),
        "jw_in": (joint_weight, hbm),
        "mw_in": (mixer_weight, hbm),
        "ew_in": (expand_weight, hbm),
        "sw_in": (shrink_weight, hbm),
    }
    block = width // narrow
    outputs = {
        "tok": (tokens.shape, BF16),
        "cot": (tokens.shape, BF16),
        "whole": ((plan.chunks, chunk, width), F32),
        "vector_out": ((plan.vector_rows, plan.block_lanes), F32),
    }
    scratch = {
        "jw": pltpu.VMEM(joint_weight.shape, BF16),
        "mw": pltpu.VMEM(mixer_weight.shape, BF16),
        "ew": pltpu.VMEM(expand_weight.shape, BF16),
        "sw": pltpu.VMEM(shrink_weight.shape, BF16),
        "stage": pltpu.VMEM((padded, width), F32),
        "first_rows": pltpu.VMEM((padded, width), BF16),
        "mixed_rows": pltpu.VMEM((padded, width), BF16),
        "qkv": pltpu.VMEM((padded, 3 * width), F32),
        "attend": pltpu.VMEM((items * plan.pairs, 2 * slots, slots), F32),
        "first_t": pltpu.VMEM((width, padded), BF16),
        "mixed_t": pltpu.VMEM((width, padded), BF16),
        "second": pltpu.VMEM((padded, width), BF16),
        "second_t": pltpu.VMEM((width, padded), BF16),
        "middle": pltpu.VMEM((padded, width), F32),
        "grad_hidden": pltpu.VMEM((padded, ff), BF16),
        "active_t": pltpu.VMEM((ff, padded), BF16),
        "grad_out": pltpu.VMEM((padded, width), BF16),
        "acc_out": pltpu.VMEM((padded, width), F32),
        "acc_grad": pltpu.VMEM((padded, width), F32),
        "grad_branch": pltpu.VMEM((padded, width), BF16),
        "vec": pltpu.VMEM((plan.vector_rows, width), F32),
        "grad_logits": pltpu.VMEM((plan.pairs, 2 * slots, slots), BF16),
        "sums": pltpu.VMEM((plan.vector_rows, width), F32),
        "expand_sums": pltpu.VMEM((plan.ff_tiles, 1, TILE), F32),
        "load_sems": pltpu.SemaphoreType.DMA((6,)),
        "vector_sems": pltpu.SemaphoreType.DMA((2, len(plan.links))),
        "send_sems": pltpu.SemaphoreType.DMA((plan.sends,)),
        "recv_sems": pltpu.SemaphoreType.DMA((plan.arrivals,)),
    }
    for stage, length in enumerate(plan.vector_lengths):
        scratch[f"vector{stage}"] = pltpu.VMEM((length, plan.block_lanes), F32)
    for number, part in enumerate(plan.parts):
        scratch[f"part{number}"] = pltpu.VMEM((2, narrow * chunk, part.columns), F32)
        for stage, move in enumerate(part.sums):
            scratch[f"land{number}_{stage}"] = pltpu.VMEM(
                (part.slots(stage), move.length, part.columns), F32
            )
    results = pl.pallas_call(
        functools.partial(layer_kernel, plan, (*inputs, *outputs, *scratch)),
        out_shape=[pltpu.VMEM(shape, kind) for shape, kind in outputs.values()],
        in_specs=[spec for _, spec in inputs.values()],
        out_specs=[vmem] * len(outputs),
        scratch_shapes=list(scratch.values()),
        compiler_params=pltpu.CompilerParams(
            has_side_effects=True, vmem_limit_bytes=52 * 2**20, collective_id=0
        ),
        name="layer",
    )(*(value for value, _ in inputs.values()))
    row_counts = [count // windows for _, count, _, windows in plan.phases]
    shapes = [jax.ShapeDtypeStruct(tokens.shape, BF16)] * 2
    shapes += [
        jax.ShapeDtypeStruct((tall, chunk, windows * width), F32)
        for tall, (_, _, _, windows) in zip(row_counts, plan.phases)
    ]
    shapes += [jax.ShapeDtypeStruct((block,), F32)] * 8
    shapes += [jax.ShapeDtypeStruct((ff // narrow,), F32)]
    copies = 2 + sum(windows for _, _, _, windows in plan.phases)
    outs = pl.pallas_call(
        functools.partial(write_kernel, plan),
        out_shape=shapes,
        in_specs=[vmem] * len(results),
        out_specs=[hbm] * 15,
        scratch_shapes=[pltpu.VMEM(shape.shape, F32) for shape in shapes[6:]]
        + [pltpu.SemaphoreType.DMA((copies + 9,))],
        compiler_params=pltpu.CompilerParams(vmem_limit_bytes=4 * 2**20),
        name="write",
    )(*(pltpu.with_memory_space_constraint(value, pltpu.VMEM) for value in results))
    input_grad, layer_out = outs[:2]
    shrink, expand, mixer, joint = (
        out.reshape(-1, out.shape[-1]) for out in outs[2:6]
    )
    vectors = outs[6:]
    return (
        layer_out,
        input_grad,
        vectors[0],
        vectors[1],
        joint,
        vectors[2],
        vectors[3],
        mixer,
        vectors[4],
        vectors[5],
        vectors[6],
        expand,
        vectors[8],
        shrink,
        vectors[7],
    )


def solution(mesh):
    return jax.shard_map(
        shards,
        mesh=mesh,
        in_specs=(
            P(("wide", "narrow"), None, None),
            P(("wide", "narrow")),
            P(),
            P(),
            P(),
            P(),
            P(),
            P(),
            P(),
            P(),
            P(),
            P(),
            P(),
            P(),
            P(),
            P(("wide", "narrow"), None, None),
        ),
        out_specs=(
            P(("wide", "narrow"), None, None),
            P(("wide", "narrow"), None, None),
            P("narrow"),
            P("narrow"),
            P("narrow", None),
            P("narrow"),
            P("narrow"),
            P("narrow", None),
            P("narrow"),
            P("narrow"),
            P("narrow"),
            P("narrow", None),
            P("narrow"),
            P("narrow", None),
            P("narrow"),
        ),
        check_vma=False,
    )
```
